128 devices in a mesh: pool: 2 (over z_hi), blk: 8 (over x, core), batch: 8 (over y, z_lo).
Axes of the slice: x: 4, y: 4, z: 4 (z_hi: 2, z_lo: 2; z = z_hi * 2 + z_lo), core: 2. Of those that a mesh axis runs over, the one named last changes fastest.
Arguments:
- prompt: bfloat16 [16, 1024, 4096], P(('pool', 'batch'), 'blk'), may hold values from -40 to 40
- prompt_len: int32 [2, 8], P('pool', 'batch'), may hold values from 256 to 1024
- dec_tokens: bfloat16 [4, 64, 4096], P(None, ('pool', 'batch')), may hold values from -40 to 40
- cache_k: bfloat16 [64, 4096, 1024], P(('pool', 'batch'), None, 'blk'), may hold values from -72 to 72
- cache_v: bfloat16 [64, 4096, 1024], P(('pool', 'batch'), None, 'blk'), may hold values from -6 to 6
- cache_len: int32 [64], P(('pool', 'batch')), may hold values from 1 to 4092
- assign: int32 [2, 8], P('pool', 'batch'), may hold values from 0 to 7, each once within a row
- slot: int32 [2, 8], P('pool', 'batch'), may hold values from 0 to 3
- gain: float32 [4096], replicated, may hold values from 0.5 to 1.5
- w_qkv: bfloat16 [4096, 6144], P(None, 'blk'), may hold values from -4 to 4
- w_out: bfloat16 [4096, 4096], P('blk'), may hold values from -0.09375 to 0.09375
Outputs:
- prefill_out: bfloat16 [16, 1024, 4096], P(('pool', 'batch'), 'blk')
- dec_out: bfloat16 [4, 64, 4096], P(None, ('pool', 'batch'))
The draws below stay inside these ranges and needn't reach their ends.
Inputs may be any that keep to these rules, and one draw needn't show every extreme that they name: For each pool p, assign[p] is a permutation of the 8 stretch indices of the other pool.
All inputs are finite; a program needn't handle non-finite values.
Results may differ from the reference program's by a relative error of at most 0.011.
Values may be sent and summed in bfloat16 or wider, within the bound.
A program may use at most 128 MiB of HBM per device.

```python
import jax
import jax.numpy as jnp
from jax import lax

D = 4096
HEADS = 32
KV_HEADS = 8
HEAD_DIM = 128
GROUP = 4
STRETCH = 1024
R_DEV = 4
CACHE = 4096
STEPS = 4
GROUPS = 16
ROWS = 64
N_POOL = 2
N_BLK = 8
N_BATCH = 8


def draw_prompt(key, part):
    shape = (GROUPS, STRETCH, D)
    drawn = jax.random.truncated_normal(jax.random.fold_in(key, 4100), -6.0, 6.0, shape, jnp.float32)
    return drawn.astype(jnp.bfloat16)


def draw_dec_tokens(key, part):
    shape = (STEPS, ROWS, D)
    drawn = jax.random.truncated_normal(jax.random.fold_in(key, 4200), -6.0, 6.0, shape, jnp.float32)
    return drawn.astype(jnp.bfloat16)


def draw_cache_k(key, part):
    shape = (ROWS, CACHE, KV_HEADS, HEAD_DIM)
    drawn = jax.random.truncated_normal(jax.random.fold_in(key, 4300), -6.0, 6.0, shape, jnp.float32)
    return drawn.reshape(ROWS, CACHE, KV_HEADS * HEAD_DIM).astype(jnp.bfloat16)


def draw_w_qkv(key, part):
    width = KV_HEADS * (GROUP + 2) * HEAD_DIM
    drawn = jax.random.truncated_normal(jax.random.fold_in(key, 4400), -6.0, 6.0, (D, width), jnp.float32) * D ** (-0.5)
    return drawn.astype(jnp.bfloat16)


def place_ends(entries, own_key, least, high):
    place = [jax.random.randint(jax.random.fold_in(own_key, axis), (), 0, length) for axis, length in enumerate(entries.shape)]
    main_axis = entries.shape.index(max(entries.shape))
    next_to = place[:main_axis] + [(place[main_axis] + 1) % entries.shape[main_axis]] + place[main_axis + 1:]
    return entries.at[tuple(place)].set(least).at[tuple(next_to)].set(high)


def block_levels(rng, shape, cuts, low, high):
    level = 1.0
    for axis_at, blocks in cuts:
        draws = jax.random.uniform(jax.random.fold_in(jax.random.fold_in(rng, 6), axis_at), (blocks,), jnp.float32, low / len(cuts), high / len(cuts))
        level = level * jnp.repeat(jnp.exp(draws), shape[axis_at] // blocks).reshape((-1,) + (1,) * (len(shape) - 1 - axis_at))
    return level


def centred(own_key, shape, scale, bound, pieces=(), held_as=jnp.bfloat16):
    level = block_levels(own_key, shape, pieces, -0.22, 0.18) if pieces else 1.0
    result = jax.random.normal(own_key, shape, jnp.float32) * scale * level
    return jnp.minimum(jnp.maximum(result, -bound), bound).astype(held_as)


def setup_inputs(seed: int = 0) -> dict:
    arg_keys = jax.random.split(jax.random.key(seed), 12)
    prompt = draw_prompt(jax.random.fold_in(arg_keys[11], 71), 0)
    prompt_len = place_ends(jax.random.randint(arg_keys[1], (N_POOL, N_BATCH), STRETCH // 4, STRETCH + 1), jax.random.fold_in(arg_keys[1], 1), STRETCH // 4, STRETCH).astype(jnp.int32)
    dec_tokens = draw_dec_tokens(jax.random.fold_in(arg_keys[11], 71), 0)
    cache_k = draw_cache_k(jax.random.fold_in(arg_keys[11], 71), 0)
    cache_v = centred(arg_keys[4], (ROWS, CACHE, KV_HEADS * HEAD_DIM), 1.0, 6.0, ((0, 16), (2, 8)))
    cache_len = place_ends(jax.random.randint(arg_keys[5], (ROWS,), 1, CACHE - STEPS + 1), jax.random.fold_in(arg_keys[5], 1), 1, CACHE - STEPS).astype(jnp.int32)
    assign = jax.vmap(lambda own: jax.random.permutation(own, N_BATCH))(jax.random.split(arg_keys[6], N_POOL)).reshape((N_POOL, N_BATCH)).astype(jnp.int32)
    slot = place_ends(jax.random.randint(arg_keys[7], (N_POOL, N_BATCH), 0, R_DEV), jax.random.fold_in(arg_keys[7], 1), 0, R_DEV - 1).astype(jnp.int32)
    gain = jnp.clip(1.0 + 0.1 * jax.random.normal(arg_keys[8], (D,), jnp.float32), 0.5, 1.5)
    w_qkv = draw_w_qkv(jax.random.fold_in(arg_keys[11], 71), 0)
    w_out = centred(arg_keys[10], (HEADS * HEAD_DIM, D), (HEADS * HEAD_DIM) ** -0.5, 0.09375, ((0, 8),))
    return dict(prompt=prompt, prompt_len=prompt_len, dec_tokens=dec_tokens, cache_k=cache_k, cache_v=cache_v, cache_len=cache_len, assign=assign, slot=slot, gain=gain, w_qkv=w_qkv, w_out=w_out)


EPSILON = 1e-05
THETA = 500000.0

def rms_norm(values, gain):
    wide = values.astype(jnp.float32)
    factor = lax.rsqrt(lax.optimization_barrier(jnp.mean(wide * wide, axis=-1, keepdims=True)) + EPSILON)
    return (wide * factor * gain.astype(jnp.float32)).astype(jnp.bfloat16)

def rotate(vector, places):
    half = vector.shape[-1] // 2
    freqs = THETA ** (-jnp.arange(half, dtype=jnp.float32) / half)
    angles = places.astype(jnp.float32)[..., None] * freqs
    cosine = jnp.cos(angles)
    sine = jnp.sin(angles)
    first = vector[..., :half]
    second = vector[..., half:]
    return jnp.concatenate([first * cosine - second * sine, second * cosine + first * sine], axis=-1)

def softmax_weights(scores):
    top = lax.optimization_barrier(jnp.max(scores, axis=-1, keepdims=True))
    expo = jnp.exp(scores - top)
    return (expo / lax.optimization_barrier(jnp.sum(expo, axis=-1, keepdims=True))).astype(jnp.bfloat16)

def head_blocks(mixed, w_out):
    width = HEADS * HEAD_DIM // N_BLK
    total = jnp.zeros((mixed.shape[0], D), jnp.float32)
    for index in range(N_BLK):
        piece_term = jnp.dot(mixed[:, index * width:(index + 1) * width], w_out[index * width:(index + 1) * width], preferred_element_type=jnp.float32).astype(jnp.bfloat16)
        total = total + lax.optimization_barrier(piece_term).astype(jnp.float32)
    return total

def prefill_group(hidden, plen, gain, w_qkv, w_out):
    f32 = jnp.float32
    normed = rms_norm(hidden, gain)
    joined = jnp.dot(normed, w_qkv, preferred_element_type=f32)
    joined = joined.reshape(STRETCH, KV_HEADS, GROUP + 2, HEAD_DIM)
    places = jnp.arange(STRETCH, dtype=jnp.int32)
    query = rotate(joined[:, :, :GROUP], places[:, None, None]).astype(jnp.bfloat16)
    key = rotate(joined[:, :, GROUP], places[:, None]).astype(jnp.bfloat16)
    value = joined[:, :, GROUP + 1].astype(jnp.bfloat16)
    scale = HEAD_DIM ** (-0.5)
    scores = jnp.einsum('qhgd,khd->hgqk', query.astype(f32), key.astype(f32)) * scale
    allowed = (places[None, :] <= places[:, None]) & (places[None, :] < plen)
    scores = jnp.where(allowed, scores, -jnp.inf)
    probs = softmax_weights(scores)
    mixed = jnp.einsum('hgqk,khd->qhgd', probs.astype(f32), value.astype(f32)).astype(jnp.bfloat16)
    mixed = mixed.reshape(STRETCH, HEADS * HEAD_DIM)
    term = head_blocks(mixed, w_out)
    return ((hidden.astype(f32) + term).astype(jnp.bfloat16), key, value)

def decode_group(tokens, cache_key, cache_value, lengths, new_key, new_value, new_len, row_slot, gain, w_qkv, w_out):
    f32 = jnp.float32
    normed = rms_norm(tokens, gain)
    joined = jnp.dot(normed.reshape(STEPS * R_DEV, D), w_qkv, preferred_element_type=f32)
    joined = joined.reshape(STEPS, R_DEV, KV_HEADS, GROUP + 2, HEAD_DIM)
    fresh = jnp.arange(R_DEV, dtype=jnp.int32) == row_slot
    begin = jnp.where(fresh, new_len, lengths)
    places = begin[None, :] + jnp.arange(STEPS, dtype=jnp.int32)[:, None]
    query = rotate(joined[:, :, :, :GROUP], places[:, :, None, None]).astype(jnp.bfloat16)
    key = rotate(joined[:, :, :, GROUP], places[:, :, None]).astype(jnp.bfloat16)
    value = joined[:, :, :, GROUP + 1].astype(jnp.bfloat16)
    cache_key = cache_key.reshape(R_DEV, CACHE, KV_HEADS, HEAD_DIM).astype(f32)
    cache_value = cache_value.reshape(R_DEV, CACHE, KV_HEADS, HEAD_DIM).astype(f32)
    scale = HEAD_DIM ** (-0.5)
    wq = query.astype(f32)
    old = jnp.einsum('srhgd,rchd->srhgc', wq, cache_key) * scale
    span = jnp.arange(CACHE, dtype=jnp.int32)
    old_ok = (span[None, :] < lengths[:, None]) & jnp.logical_not(fresh)[:, None]
    old = jnp.where(old_ok[None, :, None, None, :], old, -jnp.inf)
    new = jnp.einsum('srhgd,chd->srhgc', wq, new_key.astype(f32)) * scale
    reach = jnp.arange(STRETCH, dtype=jnp.int32)
    new_ok = (reach[None, :] < new_len) & fresh[:, None]
    new = jnp.where(new_ok[None, :, None, None, :], new, -jnp.inf)
    own = jnp.einsum('srhgd,trhd->srhgt', wq, key.astype(f32)) * scale
    steps_ok = jnp.arange(STEPS)[None, :] <= jnp.arange(STEPS)[:, None]
    own = jnp.where(steps_ok[:, None, None, None, :], own, -jnp.inf)
    probs = softmax_weights(jnp.concatenate([old, new, own], axis=-1)).astype(f32)
    mixed = jnp.einsum('srhgc,rchd->srhgd', probs[..., :CACHE], cache_value)
    mixed = mixed + jnp.einsum('srhgc,chd->srhgd', probs[..., CACHE:CACHE + STRETCH], new_value.astype(f32))
    mixed = mixed + jnp.einsum('srhgt,trhd->srhgd', probs[..., CACHE + STRETCH:], value.astype(f32))
    mixed = mixed.astype(jnp.bfloat16).reshape(STEPS * R_DEV, HEADS * HEAD_DIM)
    term = jnp.dot(mixed, w_out, preferred_element_type=f32).reshape(STEPS, R_DEV, D)
    return (tokens.astype(f32) + term).astype(jnp.bfloat16)

def reference(prompt, prompt_len, dec_tokens, cache_k, cache_v, cache_len, assign, slot, gain, w_qkv, w_out):

    def one_prefill(item):
        return prefill_group(item[0], item[1], gain, w_qkv, w_out)
    prefill_out, new_keys, new_values = lax.map(one_prefill, (prompt, prompt_len.reshape(GROUPS)))
    groups = jnp.arange(GROUPS, dtype=jnp.int32)
    source = ((1 - groups // N_BATCH) * N_BATCH + assign.reshape(GROUPS)).astype(jnp.int32)
    taken_keys = jnp.take(new_keys, source, axis=0)
    taken_values = jnp.take(new_values, source, axis=0)
    taken_lens = jnp.take(prompt_len.reshape(GROUPS), source, axis=0)
    tokens = dec_tokens.reshape(STEPS, GROUPS, R_DEV, D).transpose(1, 0, 2, 3)
    cache_key = cache_k.reshape(GROUPS, R_DEV, CACHE, KV_HEADS * HEAD_DIM)
    cache_value = cache_v.reshape(GROUPS, R_DEV, CACHE, KV_HEADS * HEAD_DIM)
    lengths = cache_len.reshape(GROUPS, R_DEV)

    def one_decode(item):
        return decode_group(item[0], item[1], item[2], item[3], item[4], item[5], item[6], item[7], gain, w_qkv, w_out)
    decoded = lax.map(one_decode, (tokens, cache_key, cache_value, lengths, taken_keys, taken_values, taken_lens, slot.reshape(GROUPS)))
    dec_out = decoded.transpose(1, 0, 2, 3).reshape(STEPS, ROWS, D)
    return (prefill_out, dec_out)
```

```python
import functools

import jax
import jax.numpy as jnp
import numpy as np
from jax import lax
from jax.experimental import pallas as pl
from jax.experimental.pallas import tpu as pltpu
from jax.sharding import PartitionSpec as P

MESH = pl.DeviceIdType.MESH
HEAD = 128
GROUP = 4
D = 4096
TOK = 128
STRETCH = 1024
CACHE = 4096
STEPS = 4
ROWS = 4
QKV = (GROUP + 2) * HEAD
PIECE = 1024
EPSILON = 1e-05
THETA = 500000.0
NEG = -1e30
SCALE2 = float(HEAD ** (-0.5) * np.log2(np.e))

f32 = jnp.float32
bf16 = jnp.bfloat16


def tables():
    half = HEAD // 2
    freqs = (THETA ** (-np.arange(half, dtype=np.float64) / half)).astype(np.float32)
    angles = np.arange(STRETCH, dtype=np.float32)[:, None] * freqs
    cosine = np.cos(angles.astype(np.float64)).astype(np.float32)
    sine = np.sin(angles.astype(np.float64)).astype(np.float32)
    ct = np.concatenate([cosine, cosine], axis=1)
    st = np.concatenate([-sine, sine], axis=1)
    fr = np.broadcast_to(np.concatenate([freqs, freqs])[None, :], (8, HEAD))
    return ct, st, np.ascontiguousarray(fr)


def dot(a, b):
    return jnp.dot(a, b, preferred_element_type=f32)


def dot_t(a, b):
    return lax.dot_general(a, b, (((1,), (1,)), ((), ())), preferred_element_type=f32)


def kernel(
    plen_ref, assign_ref, slot_ref, clen_ref, gain_ref, freq_ref,
    prompt_ref, dec_ref, ck_ref, cv_ref, wqkv_ref, wout_ref, ct_ref, st_ref,
    out_ref, dout_ref,
    xp, xs, wq, wo, ck, cv, acc, qs, kv, at, pb, fr, nr, ct, st, ob, bias,
    dmv, x16, xd, qd, kd, vd, qr, ms, ls, os_, plt, pls, qnew, qn, pks, pk, od, dsb, drb, dfb, o32,
    lsem, outS, agS, agR, wS, wR, plS, plR, qnS, qnR, pkS, pkR, kvS, kvR, fS, fR, nS, nR, dS, dR, eS, eR,
):
    me = lax.axis_index("blk")
    pool = lax.axis_index("pool")
    batch = lax.axis_index("batch")
    x = me // 2
    c = lax.rem(me, 2)

    def near(dx, dc):
        return {"blk": lax.rem(x + dx + 4, 4) * 2 + lax.rem(c + dc, 2)}

    def other(j):
        return {"pool": 1 - pool, "batch": j}

    def peer(j):
        return {"blk": lax.rem(me + j, 8)}

    def remote(src, dst, ss, rs, dev):
        return pltpu.make_async_remote_copy(
            src_ref=src, dst_ref=dst, send_sem=ss, recv_sem=rs, device_id=dev, device_id_type=MESH
        )

    local = [
        pltpu.make_async_copy(prompt_ref.at[0], xp, lsem.at[0]),
        pltpu.make_async_copy(dec_ref, dmv, lsem.at[1]),
    ]
    for q in range(4):
        rows = pl.ds(q * PIECE, PIECE)
        local.append(pltpu.make_async_copy(wqkv_ref.at[rows], wq.at[0, rows], lsem.at[2 + q]))
    local.append(pltpu.make_async_copy(ct_ref, ct, lsem.at[6]))
    local.append(pltpu.make_async_copy(st_ref, st, lsem.at[7]))
    local.append(pltpu.make_async_copy(ck_ref, ck, lsem.at[8]))
    local.append(pltpu.make_async_copy(cv_ref, cv, lsem.at[9]))
    local.append(pltpu.make_async_copy(wout_ref, wo.at[0], lsem.at[10]))
    for cp in local:
        cp.start()

    barrier = pltpu.get_barrier_semaphore()
    for j in range(1, 8):
        pl.semaphore_signal(barrier, inc=1, device_id=peer(j), device_id_type=MESH)
    for j in range(8):
        pl.semaphore_signal(barrier, inc=1, device_id=other(j), device_id_type=MESH)

    plt[...] = jnp.full((8, 128), plen_ref[0, 0], jnp.int32)
    col = lax.broadcasted_iota(jnp.int32, (8, STRETCH), 1)
    bias[...] = jnp.where(col < jnp.full((8, STRETCH), plen_ref[0, 0], jnp.int32), 0.0, NEG)

    local[0].wait()

    def norm_band(i, _):
        rows = pl.ds(pl.multiple_of(i * 16, 16), 16)
        wide = xp[rows, :].astype(f32)
        factor = lax.rsqrt(jnp.mean(wide * wide, axis=-1, keepdims=True) + EPSILON)
        normed = (wide * factor * gain_ref[...]).astype(bf16)
        for q in range(4):
            xs[0, q, rows, :] = normed[:, q * PIECE:(q + 1) * PIECE]
        return 0

    lax.fori_loop(0, TOK // 16, norm_band, 0)
    pl.semaphore_wait(barrier, 15)

    def gather(direction, k):
        if direction == 0:
            if k < 4:
                return remote(xs.at[0, k], xs.at[1, k], agS.at[0, k], agR.at[0, k], near(1, 0))
            return remote(xs.at[1, k - 4], xs.at[3, k - 4], agS.at[0, k], agR.at[2, k - 4], near(1, 0))
        if k < 4:
            q = (k + 2) % 4
            return remote(xs.at[0, q], xs.at[2, q], agS.at[1, k], agR.at[1, q], near(-1, 0))
        return remote(xs.at[2, k - 2], xs.at[3, k - 2], agS.at[1, k], agR.at[2, k - 2], near(-1, 0))

    for k in range(4):
        gather(0, k).start()
        gather(1, k).start()

    def weight(k):
        if k < 4:
            rows = pl.ds(k * PIECE, PIECE)
            return remote(wqkv_ref.at[rows], wq.at[1, rows], wS.at[k], wR.at[k], near(0, 1))
        return remote(wout_ref, wo.at[1], wS.at[4], wR.at[4], near(0, 1))

    for k in range(5):
        weight(k).start()

    def length(j):
        return remote(plt, pls.at[batch], plS.at[j], plR.at[batch], other(j))

    for j in range(8):
        length(j).start()

    local[1].wait()
    for s in range(STEPS):
        x16[pl.ds(s * ROWS, ROWS), :] = dmv[s].astype(f32)
    wide = x16[...]
    factor = lax.rsqrt(jnp.mean(wide * wide, axis=-1, keepdims=True) + EPSILON)
    xd[...] = (wide * factor * gain_ref[...]).astype(bf16)
    joined = jnp.zeros((16, QKV), f32)
    for q in range(4):
        local[2 + q].wait()
        joined = joined + dot(xd[:, q * PIECE:(q + 1) * PIECE], wq[0, pl.ds(q * PIECE, PIECE), :])

    wanted = jnp.full((8, 128), assign_ref[0, 0], jnp.int32)
    newlen = jnp.zeros((8, 128), jnp.int32)
    for j in range(8):
        remote(plt, pls.at[j], plS.at[j], plR.at[j], other(j)).wait_recv()
    for j in range(8):
        newlen = newlen + jnp.where(wanted == j, pls[j], 0)
    row = lax.broadcasted_iota(jnp.int32, (16, 128), 0)
    row_r = lax.rem(row, ROWS)
    place = jnp.zeros((16, 128), jnp.int32)
    for r in range(ROWS):
        place = jnp.where(row_r == r, jnp.full((16, 128), clen_ref[r], jnp.int32), place)
    fresh = row_r == jnp.full((16, 128), slot_ref[0, 0], jnp.int32)
    place = jnp.where(fresh, jnp.broadcast_to(newlen[0:1, :], (16, 128)), place) + row // ROWS
    angle = place.astype(f32) * freq_ref[0:1, :]
    lane = lax.broadcasted_iota(jnp.int32, (16, 128), 1)
    dcos = jnp.cos(angle)
    dsin = jnp.sin(angle)
    dsin = jnp.where(lane < HEAD // 2, -dsin, dsin)

    def turn(u, cosine, sine):
        return u * cosine + pltpu.roll(u, HEAD // 2, 1) * sine

    for h in range(GROUP):
        qd[pl.ds(h * 16, 16), :] = turn(joined[:, h * HEAD:(h + 1) * HEAD], dcos, dsin)
    kd[...] = turn(joined[:, GROUP * HEAD:(GROUP + 1) * HEAD], dcos, dsin).astype(bf16)
    vd[...] = joined[:, (GROUP + 1) * HEAD:].astype(bf16)
    slots = jnp.full((16, 128), slot_ref[0, 0], jnp.int32)
    picked = jnp.zeros((16, 128), f32)
    for r in range(ROWS):
        part = qd[pl.ds(r, 16, stride=ROWS), :]
        qr[r] = part.astype(bf16)
        picked = picked + jnp.where(slots == r, part, 0.0)
    qnew[...] = picked.astype(bf16)

    def project(slot, q, a):
        tokens = xs[slot, q]
        rows = pl.ds(pl.multiple_of(q * PIECE, PIECE), PIECE)
        for h in range(2):
            acc[a, h] += dot(tokens, wq[h, rows, :])

    def origin(slot):
        return lax.rem(x + (0, 3, 1, 2)[slot], 4)

    def exchange(slot, h):
        rows = pl.ds(pl.multiple_of((origin(slot) * 2 + c) * TOK, TOK), TOK)
        return remote(kv.at[h, :, rows], kv.at[1 - h, :, rows], kvS.at[slot, h], kvR.at[slot, 1 - h], near(0, 1))

    def exchanged(slot, h):
        rows = pl.ds(pl.multiple_of((origin(slot) * 2 + 1 - c) * TOK, TOK), TOK)
        return remote(kv.at[h, :, rows], kv.at[h, :, rows], kvS.at[slot, h], kvR.at[slot, h], near(0, 1))

    def finish(slot, a):
        rows = pl.ds(pl.multiple_of((origin(slot) * 2 + c) * TOK, TOK), TOK)
        cosine = ct[rows, :]
        sine = st[rows, :]
        for h in range(2):
            kv[h, 0, rows, :] = turn(acc[a, h, :, GROUP * HEAD:(GROUP + 1) * HEAD], cosine, sine).astype(bf16)
            kv[h, 1, rows, :] = acc[a, h, :, (GROUP + 1) * HEAD:].astype(bf16)
        for h in range(2):
            for g in range(GROUP):
                qs[slot, h * GROUP + g] = turn(acc[a, h, :, g * HEAD:(g + 1) * HEAD], cosine, sine).astype(bf16)
        for h in range(2):
            exchange(slot, h).start()

    for k in range(4):
        weight(k).wait_recv()
    local[6].wait()
    local[7].wait()
    acc[0] = jnp.zeros((2, TOK, QKV), f32)
    lax.fori_loop(0, 4, lambda q, _: (project(0, q, 0), 0)[1], 0)

    def query(j):
        return remote(qnew, qn.at[batch], qnS.at[j], qnR.at[batch], other(j))

    for j in range(8):
        query(j).start()
    finish(0, 0)

    local[8].wait()
    local[9].wait()

    def old_row(r):
        q16 = qr[r]
        edge = jnp.full((16, CACHE), clen_ref[r], jnp.int32)
        edge = jnp.where(jnp.full((16, CACHE), slot_ref[0, 0], jnp.int32) == r, 0, edge)
        span = lax.broadcasted_iota(jnp.int32, (16, CACHE), 1)
        old = jnp.where(span < edge, dot_t(q16, ck[r]) * SCALE2, NEG)
        own = dot_t(q16, kd[...]) * SCALE2
        i16 = lax.broadcasted_iota(jnp.int32, (16, 16), 0)
        j16 = lax.broadcasted_iota(jnp.int32, (16, 16), 1)
        keep = (lax.rem(j16, ROWS) == r) & (j16 // ROWS <= lax.rem(i16, STEPS))
        own = jnp.where(keep, own, NEG)
        top = jnp.maximum(jnp.max(old, axis=-1, keepdims=True), jnp.max(own, axis=-1, keepdims=True))
        pold = jnp.exp2(old - top)
        pown = jnp.exp2(own - top)
        total = jnp.sum(pold, axis=-1, keepdims=True) + jnp.sum(pown, axis=-1, keepdims=True)
        mixed = dot(pold.astype(bf16), cv[r]) + dot(pown.astype(bf16), vd[...])
        ms[r] = jnp.broadcast_to(top, (16, 128))
        ls[r] = jnp.broadcast_to(total, (16, 128))
        os_[r] = mixed

    acc[0] = jnp.zeros((2, TOK, QKV), f32)
    acc[1] = jnp.zeros((2, TOK, QKV), f32)

    def near_step(t, _):
        q1 = t
        q2 = lax.rem(t + 2, 4)
        remote(xs.at[1, q1], xs.at[1, q1], agS.at[0, q1], agR.at[0, q1], near(1, 0)).wait_recv()
        remote(xs.at[2, q2], xs.at[2, q2], agS.at[1, q2], agR.at[1, q2], near(1, 0)).wait_recv()

        @pl.when(t < 2)
        def _():
            remote(xs.at[1, q1], xs.at[3, q1], agS.at[0, 4 + t], agR.at[2, q1], near(1, 0)).start()
            remote(xs.at[2, q2], xs.at[3, q2], agS.at[1, 4 + t], agR.at[2, q2], near(-1, 0)).start()

        project(1, q1, 0)
        project(2, q2, 1)
        old_row(t)
        return 0

    lax.fori_loop(0, 4, near_step, 0)
    finish(1, 0)
    finish(2, 1)

    acc[0] = jnp.zeros((2, TOK, QKV), f32)

    def far_step(t, _):
        for q in (t, t + 2):
            remote(xs.at[3, q], xs.at[3, q], agS.at[0, q], agR.at[2, q], near(1, 0)).wait_recv()
            project(3, q, 0)
        return 0

    lax.fori_loop(0, 2, far_step, 0)
    finish(3, 0)
    local[10].wait()
    weight(4).wait_recv()
    for slot in range(4):
        for h in range(2):
            exchanged(slot, h).wait_recv()

    def attend(d, X):
        for n in range(4):
            @pl.when(X == n)
            def _(n=n):
                size = 256 * (n + 1)

                def pair(hp, _):
                    q2 = qs[d, pl.ds(hp * 2, 2)].reshape(2 * TOK, HEAD)
                    h = hp // 2
                    s = dot_t(q2, kv[h, 0, pl.ds(0, size), :]) * SCALE2 + bias[0:1, :size]
                    last = s[:, size - 256:]
                    qi = lax.rem(lax.broadcasted_iota(jnp.int32, (2 * TOK, 256), 0), TOK) + c * TOK
                    ki = lax.broadcasted_iota(jnp.int32, (2 * TOK, 256), 1)
                    last = jnp.where(ki <= qi, last, NEG)
                    s = jnp.concatenate([s[:, :size - 256], last], axis=1) if n else last
                    top = jnp.max(s, axis=-1, keepdims=True)
                    p = jnp.exp2(s - top)
                    total = jnp.sum(p, axis=-1, keepdims=True)
                    o = dot(p.astype(bf16), kv[h, 1, pl.ds(0, size), :]) / total
                    o = o.astype(bf16)
                    at[:, pl.ds(pl.multiple_of(hp * 256, 256), HEAD)] = o[:TOK]
                    at[:, pl.ds(pl.multiple_of(hp * 256 + HEAD, HEAD), HEAD)] = o[TOK:]
                    return 0

                lax.fori_loop(0, 4, pair, 0)

    def out_piece(d, q):
        cols = pl.ds(pl.multiple_of(q * PIECE, PIECE), PIECE)
        part = dot(at[:, :512], wo[0, :, cols]) + dot(at[:, 512:], wo[1, :, cols])
        pb[d, q] = part.astype(bf16)

    def far_send(q):
        if q < 2:
            return remote(pb.at[3, q], fr.at[0, q], fS.at[0, q], fR.at[0, q], near(1, 0))
        return remote(pb.at[3, q], fr.at[1, q - 2], fS.at[1, q - 2], fR.at[1, q - 2], near(-1, 0))

    def near_send(direction, q):
        return remote(
            pb.at[2 - direction, q], nr.at[direction, q], nS.at[direction, q], nR.at[direction, q],
            near(1 - 2 * direction, 0),
        )

    def answer():
        for j in range(8):
            remote(qnew, qn.at[j], qnS.at[j], qnR.at[j], other(j)).wait_recv()
        q = qn[...].reshape(8 * 16, HEAD)
        s = dot_t(q, kv[0, 0]) * SCALE2 + bias[0:1, :]
        top = jnp.max(s, axis=-1, keepdims=True)
        p = jnp.exp2(s - top)
        total = jnp.sum(p, axis=-1, keepdims=True)
        o = dot(p.astype(bf16), kv[0, 1])
        pks[:, 0] = o.reshape(8, 16, HEAD)
        pks[:, 1] = jnp.broadcast_to(top, (128, HEAD)).reshape(8, 16, HEAD)
        pks[:, 2] = jnp.broadcast_to(total, (128, HEAD)).reshape(8, 16, HEAD)

    def reply(j):
        return remote(pks.at[j], pk.at[batch], pkS.at[j], pkR.at[batch], other(j))

    def block(t, _):
        d = 3 - t
        X = lax.rem(x + jnp.where(d == 3, 2, jnp.where(d == 2, 1, jnp.where(d == 1, 3, 0))), 4)
        attend(d, X)

        def piece(k, _):
            out_piece(d, lax.rem(k, 2) * 2 + k // 2)
            return 0

        lax.fori_loop(0, 4, piece, 0)

        @pl.when(t == 0)
        def _():
            for q in (0, 2, 1, 3):
                far_send(q).start()
            answer()

        @pl.when(t == 1)
        def _():
            for j in range(8):
                reply(j).start()
            for q in (2, 3):
                near_send(0, q).start()

        @pl.when(t == 2)
        def _():
            for q in (0, 1):
                near_send(1, q).start()

        return 0

    lax.fori_loop(0, 4, block, 0)

    for j in range(8):
        remote(pks.at[j], pk.at[j], pkS.at[j], pkR.at[j], other(j)).wait_recv()
    want = jnp.full((16, 128), assign_ref[0, 0], jnp.int32)
    no = jnp.zeros((16, 128), f32)
    nm = jnp.zeros((16, 128), f32)
    nl = jnp.zeros((16, 128), f32)
    for j in range(8):
        hit = want == j
        no = no + jnp.where(hit, pk[j, 0], 0.0)
        nm = nm + jnp.where(hit, pk[j, 1], 0.0)
        nl = nl + jnp.where(hit, pk[j, 2], 0.0)
    for r in range(ROWS):
        mine = slots == r
        m2 = jnp.where(mine, nm, NEG)
        top = jnp.maximum(ms[r], m2)
        a = jnp.exp2(ms[r] - top)
        b = jnp.exp2(m2 - top)
        o = (os_[r] * a + no * b) / (ls[r] * a + nl * b)
        od[pl.ds(r, 16, stride=ROWS), :] = o
    part = jnp.zeros((16, D), f32)
    for h in range(GROUP):
        part = part + dot(od[pl.ds(h * 16, 16), :].astype(bf16), wo[0, pl.ds(h * HEAD, HEAD), :])
    for k in range(8):
        dsb[k] = part[:, k * 512:(k + 1) * 512].astype(bf16)

    def scatter(j):
        return remote(dsb.at[lax.rem(me + j, 8)], drb.at[j - 1], dS.at[j - 1], dR.at[j - 1], peer(j))

    for j in range(1, 8):
        scatter(j).start()

    for q in (0, 1):
        far_send(q).wait_recv()
        pb[2, q] = (pb[2, q].astype(f32) + fr[0, q].astype(f32)).astype(bf16)
        far_send(q + 2).wait_recv()
        pb[1, q + 2] = (pb[1, q + 2].astype(f32) + fr[1, q].astype(f32)).astype(bf16)
        near_send(0, q).start()
        near_send(1, q + 2).start()

    for j in range(1, 8):
        scatter(j).wait_recv()
    mycols = pl.ds(pl.multiple_of(me * 512, 512), 512)
    total = dsb[me].astype(f32)
    for j in range(7):
        total = total + drb[j].astype(f32)
    done = (x16[:, mycols] + total).astype(bf16)
    dfb[0] = done
    o32[:, mycols] = done.astype(f32)

    def spread(j):
        return remote(dfb.at[0], dfb.at[j], eS.at[j - 1], eR.at[j - 1], peer(j))

    for j in range(1, 8):
        spread(j).start()

    outs = []
    for i, q in enumerate((0, 2, 1, 3)):
        near_send(0, q).wait_recv()
        near_send(1, q).wait_recv()
        cols = slice(q * PIECE, (q + 1) * PIECE)
        total = pb[0, q].astype(f32) + nr[0, q].astype(f32) + nr[1, q].astype(f32)
        ob[:, cols] = (xp[:, cols].astype(f32) + total).astype(bf16)
        cp = pltpu.make_async_copy(ob.at[:, cols], out_ref.at[0, :, cols], outS.at[q])
        cp.start()
        outs.append(cp)

    for j in range(1, 8):
        spread(j).wait_recv()
    for j in range(1, 8):
        cols = pl.ds(pl.multiple_of(lax.rem(me - j + 8, 8) * 512, 512), 512)
        o32[:, cols] = dfb[j].astype(f32)
    for s in range(STEPS):
        dout_ref[s] = o32[pl.ds(s * ROWS, ROWS), :].astype(bf16)

    for k in range(6):
        gather(0, k).wait_send()
        gather(1, k).wait_send()
    for k in range(5):
        weight(k).wait_send()
    for j in range(8):
        length(j).wait_send()
        query(j).wait_send()
        reply(j).wait_send()
    for slot in range(4):
        for h in range(2):
            exchange(slot, h).wait_send()
    for q in range(4):
        far_send(q).wait_send()
        near_send(0, q).wait_send()
        near_send(1, q).wait_send()
    for j in range(1, 8):
        scatter(j).wait_send()
        spread(j).wait_send()
    for cp in outs:
        cp.wait()


def body(
    prompt, prompt_len, dec_tokens, cache_k, cache_v, cache_len, assign, slot, gain, w_qkv, w_out
):
    ct, st, fr = tables()
    any_ = pl.BlockSpec(memory_space=pl.ANY)
    smem = pl.BlockSpec(memory_space=pltpu.SMEM)
    vmem = pl.BlockSpec(memory_space=pltpu.VMEM)
    V = pltpu.VMEM
    dma = pltpu.SemaphoreType.DMA
    return pl.pallas_call(
        kernel,
        out_shape=(
            jax.ShapeDtypeStruct((1, TOK, D), bf16),
            jax.ShapeDtypeStruct((STEPS, ROWS, D), bf16),
        ),
        in_specs=[smem] * 4 + [vmem] * 2 + [any_] * 8,
        out_specs=(any_, vmem),
        scratch_shapes=[
            V((TOK, D), bf16),
            V((4, 4, TOK, PIECE), bf16),
            V((2, D, QKV), bf16),
            V((2, 512, D), bf16),
            V((ROWS, CACHE, HEAD), bf16),
            V((ROWS, CACHE, HEAD), bf16),
            V((2, 2, TOK, QKV), f32),
            V((4, 8, TOK, HEAD), bf16),
            V((2, 2, STRETCH, HEAD), bf16),
            V((TOK, 1024), bf16),
            V((4, 4, TOK, PIECE), bf16),
            V((2, 2, TOK, PIECE), bf16),
            V((2, 4, TOK, PIECE), bf16),
            V((STRETCH, HEAD), f32),
            V((STRETCH, HEAD), f32),
            V((TOK, D), bf16),
            V((8, STRETCH), f32),
            V((STEPS, ROWS, D), bf16),
            V((16, D), f32),
            V((16, D), bf16),
            V((64, HEAD), f32),
            V((16, HEAD), bf16),
            V((16, HEAD), bf16),
            V((ROWS, 16, HEAD), bf16),
            V((ROWS, 16, HEAD), f32),
            V((ROWS, 16, HEAD), f32),
            V((ROWS, 16, HEAD), f32),
            V((8, 128), jnp.int32),
            V((8, 8, 128), jnp.int32),
            V((16, HEAD), bf16),
            V((8, 16, HEAD), bf16),
            V((8, 3, 16, HEAD), f32),
            V((8, 3, 16, HEAD), f32),
            V((64, HEAD), f32),
            V((8, 16, 512), bf16),
            V((7, 16, 512), bf16),
            V((8, 16, 512), bf16),
            V((16, D), f32),
            dma((11,)), dma((4,)),
            dma((2, 6)), dma((3, 4)),
            dma((5,)), dma((5,)),
            dma((8,)), dma((8,)),
            dma((8,)), dma((8,)),
            dma((8,)), dma((8,)),
            dma((4, 2)), dma((4, 2)),
            dma((2, 2)), dma((2, 2)),
            dma((2, 4)), dma((2, 4)),
            dma((7,)), dma((7,)),
            dma((7,)), dma((7,)),
        ],
        compiler_params=pltpu.CompilerParams(
            collective_id=0, has_side_effects=True, vmem_limit_bytes=61 * 2**20
        ),
        name="layer",
    )(
        prompt_len, assign, slot, cache_len, gain.reshape(1, D), jnp.asarray(fr),
        prompt, dec_tokens, cache_k, cache_v, w_qkv, w_out, jnp.asarray(ct), jnp.asarray(st),
    )


def solution(mesh):
    return jax.shard_map(
        body,
        mesh=mesh,
        in_specs=(
            P(("pool", "batch"), "blk", None),
            P("pool", "batch"),
            P(None, ("pool", "batch"), None),
            P(("pool", "batch"), None, "blk"),
            P(("pool", "batch"), None, "blk"),
            P(("pool", "batch")),
            P("pool", "batch"),
            P("pool", "batch"),
            P(),
            P(None, "blk"),
            P("blk", None),
        ),
        out_specs=(P(("pool", "batch"), "blk", None), P(None, ("pool", "batch"), None)),
        check_vma=False,
    )
```

```python
import functools

import jax
import jax.numpy as jnp
import numpy as np
from jax import lax
from jax.experimental import pallas as pl
from jax.experimental.pallas import tpu as pltpu
from jax.sharding import PartitionSpec as P

MESH = pl.DeviceIdType.MESH
HEAD = 128
GROUP = 4
D = 4096
TOK = 128
STRETCH = 1024
CACHE = 4096
STEPS = 4
ROWS = 4
QKV = (GROUP + 2) * HEAD
PIECE = 1024
EPSILON = 1e-05
THETA = 500000.0
NEG = -1e30
SCALE2 = float(HEAD ** (-0.5) * np.log2(np.e))

f32 = jnp.float32
bf16 = jnp.bfloat16


def tables():
    half = HEAD // 2
    freqs = (THETA ** (-np.arange(half, dtype=np.float64) / half)).astype(np.float32)
    angles = np.arange(STRETCH, dtype=np.float32)[:, None] * freqs
    cosine = np.cos(angles.astype(np.float64)).astype(np.float32)
    sine = np.sin(angles.astype(np.float64)).astype(np.float32)
    ct = np.concatenate([cosine, cosine], axis=1)
    st = np.concatenate([-sine, sine], axis=1)
    fr = np.broadcast_to(np.concatenate([freqs, freqs])[None, :], (8, HEAD))
    return ct, st, np.ascontiguousarray(fr)


def dot(a, b):
    return jnp.dot(a, b, preferred_element_type=f32)


def dot_t(a, b):
    return lax.dot_general(a, b, (((1,), (1,)), ((), ())), preferred_element_type=f32)


def kernel(
    plen_ref, assign_ref, slot_ref, clen_ref, gain_ref, freq_ref,
    prompt_ref, dec_ref, ck_ref, cv_ref, wqkv_ref, wout_ref, ct_ref, st_ref,
    out_ref, dout_ref,
    xs, wq, wo, ck, cv, acc, ssq, qs, kv, so, sm, sl, at, pb, fr, nr, ct, st, bias,
    xn, dmv, x16, xd, qd, kd, vd, qr, ms, ls, os_, plt, pls, qnew, qn, pks, pk, od, dsb, drb, dfb, o32,
    lsem, agS, agR, wS, wR, plS, plR, qnS, qnR, pkS, pkR, kvS, kvR, fS, fR, nS, nR, dS, dR, eS, eR,
):
    me = lax.axis_index("blk")
    pool = lax.axis_index("pool")
    batch = lax.axis_index("batch")
    x = me // 2
    c = lax.rem(me, 2)

    def near(dx, dc):
        return {"blk": lax.rem(x + dx + 4, 4) * 2 + lax.rem(c + dc, 2)}

    def other(j):
        return {"pool": 1 - pool, "batch": j}

    def peer(j):
        return {"blk": lax.rem(me + j, 8)}

    def remote(src, dst, ss, rs, dev):
        return pltpu.make_async_remote_copy(
            src_ref=src, dst_ref=dst, send_sem=ss, recv_sem=rs, device_id=dev, device_id_type=MESH
        )

    local = [pltpu.make_async_copy(dec_ref, dmv, lsem.at[1])]
    for q in range(4):
        rows = pl.ds(q * PIECE, PIECE)
        local.append(pltpu.make_async_copy(wqkv_ref.at[rows], wq.at[0, rows], lsem.at[2 + q]))
    local.append(pltpu.make_async_copy(ct_ref, ct, lsem.at[6]))
    local.append(pltpu.make_async_copy(st_ref, st, lsem.at[7]))
    local.append(pltpu.make_async_copy(ck_ref, ck, lsem.at[8]))
    local.append(pltpu.make_async_copy(cv_ref, cv, lsem.at[9]))
    local.append(pltpu.make_async_copy(wout_ref, wo.at[0], lsem.at[10]))
    for q in range(4):
        local.insert(2 + 2 * q, pltpu.make_async_copy(prompt_ref.at[0, :, pl.ds(q * PIECE, PIECE)], xs.at[0, q], lsem.at[(0, 11, 12, 13)[q]]))
    ldec, w0, t0, w1, t1, w2, t2, w3, t3, lct, lst, lck, lcv, lwo = local
    lweights = (w0, w1, w2, w3)
    ltokens = (t0, t1, t2, t3)
    for cp in local:
        cp.start()

    barrier = pltpu.get_barrier_semaphore()
    for j in range(1, 8):
        pl.semaphore_signal(barrier, inc=1, device_id=peer(j), device_id_type=MESH)
    for j in range(8):
        pl.semaphore_signal(barrier, inc=1, device_id=other(j), device_id_type=MESH)

    plt[...] = jnp.full((8, 128), plen_ref[0, 0], jnp.int32)
    col = lax.broadcasted_iota(jnp.int32, (8, STRETCH), 1)
    bias[...] = jnp.where(col < jnp.full((8, STRETCH), plen_ref[0, 0], jnp.int32), 0.0, NEG)

    pl.semaphore_wait(barrier, 15)

    def gather(direction, k):
        if direction == 0:
            if k < 4:
                return remote(prompt_ref.at[0, :, pl.ds(k * PIECE, PIECE)], xs.at[1, k], agS.at[0, k], agR.at[0, k], near(1, 0))
            return remote(xs.at[1, k - 4], xs.at[3, k - 4], agS.at[0, k], agR.at[2, k - 4], near(1, 0))
        if k < 4:
            q = (k + 2) % 4
            return remote(prompt_ref.at[0, :, pl.ds(q * PIECE, PIECE)], xs.at[2, q], agS.at[1, k], agR.at[1, q], near(-1, 0))
        return remote(xs.at[2, k - 2], xs.at[3, k - 2], agS.at[1, k], agR.at[2, k - 2], near(-1, 0))

    for k in range(4):
        gather(0, k).start()
        gather(1, k).start()

    def weight(k):
        if k < 4:
            rows = pl.ds(k * PIECE, PIECE)
            return remote(wqkv_ref.at[rows], wq.at[1, rows], wS.at[k], wR.at[k], near(0, 1))
        return remote(wout_ref, wo.at[1], wS.at[4], wR.at[4], near(0, 1))

    for k in range(5):
        weight(k).start()

    def length(j):
        return remote(plt, pls.at[batch], plS.at[j], plR.at[batch], other(j))

    for j in range(8):
        length(j).start()

    ldec.wait()
    for s in range(STEPS):
        x16[pl.ds(s * ROWS, ROWS), :] = dmv[s].astype(f32)
    wide = x16[...]
    factor = lax.rsqrt(jnp.mean(wide * wide, axis=-1, keepdims=True) + EPSILON)
    xd[...] = (wide * factor * gain_ref[...]).astype(bf16)
    joined = jnp.zeros((16, QKV), f32)
    for q in range(4):
        lweights[q].wait()
        joined = joined + dot(xd[:, q * PIECE:(q + 1) * PIECE], wq[0, pl.ds(q * PIECE, PIECE), :])

    def scaled(slot, q, a):
        wide = xs[slot, q].astype(f32)
        square = wide * wide
        part = square[:, :HEAD]
        for i in range(1, PIECE // HEAD):
            part = part + square[:, i * HEAD:(i + 1) * HEAD]
        ssq[a] += part
        return (wide * gain_ref[:, pl.ds(pl.multiple_of(q * PIECE, PIECE), PIECE)]).astype(bf16)

    def project(slot, q, a):
        tokens = scaled(slot, q, a)
        rows = pl.ds(pl.multiple_of(q * PIECE, PIECE), PIECE)
        for h in range(2):
            acc[a, h] += dot(tokens, wq[h, rows, :])

    def clear(a):
        acc[a] = jnp.zeros((2, TOK, QKV), f32)
        ssq[a] = jnp.zeros((TOK, HEAD), f32)

    clear(0)
    for q in range(4):
        ltokens[q].wait()

    def own_first(q, _):
        tokens = scaled(0, q, 0)
        xn[q] = tokens
        acc[0, 0] += dot(tokens, wq[0, pl.ds(pl.multiple_of(q * PIECE, PIECE), PIECE), :])
        return 0

    lax.fori_loop(0, 4, own_first, 0)

    wanted = jnp.full((8, 128), assign_ref[0, 0], jnp.int32)
    newlen = jnp.zeros((8, 128), jnp.int32)
    for j in range(8):
        remote(plt, pls.at[j], plS.at[j], plR.at[j], other(j)).wait_recv()
    for j in range(8):
        newlen = newlen + jnp.where(wanted == j, pls[j], 0)
    row = lax.broadcasted_iota(jnp.int32, (16, 128), 0)
    row_r = lax.rem(row, ROWS)
    place = jnp.zeros((16, 128), jnp.int32)
    for r in range(ROWS):
        place = jnp.where(row_r == r, jnp.full((16, 128), clen_ref[r], jnp.int32), place)
    fresh = row_r == jnp.full((16, 128), slot_ref[0, 0], jnp.int32)
    place = jnp.where(fresh, jnp.broadcast_to(newlen[0:1, :], (16, 128)), place) + row // ROWS
    angle = place.astype(f32) * freq_ref[0:1, :]
    lane = lax.broadcasted_iota(jnp.int32, (16, 128), 1)
    dcos = jnp.cos(angle)
    dsin = jnp.sin(angle)
    dsin = jnp.where(lane < HEAD // 2, -dsin, dsin)

    def turn(u, cosine, sine):
        return u * cosine + pltpu.roll(u, HEAD // 2, 1) * sine

    for h in range(GROUP):
        qd[pl.ds(h * 16, 16), :] = turn(joined[:, h * HEAD:(h + 1) * HEAD], dcos, dsin)
    kd[...] = turn(joined[:, GROUP * HEAD:(GROUP + 1) * HEAD], dcos, dsin).astype(bf16)
    vd[...] = joined[:, (GROUP + 1) * HEAD:].astype(bf16)
    slots = jnp.full((16, 128), slot_ref[0, 0], jnp.int32)
    picked = jnp.zeros((16, 128), f32)
    for r in range(ROWS):
        part = qd[pl.ds(r, 16, stride=ROWS), :]
        qr[r] = part.astype(bf16)
        picked = picked + jnp.where(slots == r, part, 0.0)
    qnew[...] = picked.astype(bf16)

    def origin(slot):
        if isinstance(slot, int):
            return lax.rem(x + (0, 3, 1, 2)[slot], 4)
        return lax.rem(x + jnp.where(slot == 1, 3, jnp.where(slot == 2, 1, jnp.where(slot == 3, 2, 0))), 4)

    def exchange(slot, h):
        rows = pl.ds(pl.multiple_of((origin(slot) * 2 + c) * TOK, TOK), TOK)
        return remote(kv.at[h, :, rows], kv.at[1 - h, :, rows], kvS.at[slot, h], kvR.at[slot, 1 - h], near(0, 1))

    def exchanged(slot, h):
        rows = pl.ds(pl.multiple_of((origin(slot) * 2 + 1 - c) * TOK, TOK), TOK)
        return remote(kv.at[h, :, rows], kv.at[h, :, rows], kvS.at[slot, h], kvR.at[slot, h], near(0, 1))

    def finish(slot, a):
        rows = pl.ds(pl.multiple_of((origin(slot) * 2 + c) * TOK, TOK), TOK)
        factor = lax.rsqrt(jnp.sum(ssq[a], axis=-1, keepdims=True) * (1.0 / D) + EPSILON)
        cosine = ct[rows, :] * factor
        sine = st[rows, :] * factor
        for h in range(2):
            kv[h, 0, rows, :] = turn(acc[a, h, :, GROUP * HEAD:(GROUP + 1) * HEAD], cosine, sine).astype(bf16)
            kv[h, 1, rows, :] = (acc[a, h, :, (GROUP + 1) * HEAD:] * factor).astype(bf16)
        for h in range(2):
            for g in range(GROUP):
                qs[slot, h * GROUP + g] = turn(acc[a, h, :, g * HEAD:(g + 1) * HEAD], cosine, sine).astype(bf16)
        for h in range(2):
            exchange(slot, h).start()

    def old_row(r):
        q16 = qr[r]
        edge = jnp.full((16, CACHE), clen_ref[r], jnp.int32)
        edge = jnp.where(jnp.full((16, CACHE), slot_ref[0, 0], jnp.int32) == r, 0, edge)
        span = lax.broadcasted_iota(jnp.int32, (16, CACHE), 1)
        old = jnp.where(span < edge, dot_t(q16, ck[r]) * SCALE2, NEG)
        own = dot_t(q16, kd[...]) * SCALE2
        i16 = lax.broadcasted_iota(jnp.int32, (16, 16), 0)
        j16 = lax.broadcasted_iota(jnp.int32, (16, 16), 1)
        keep = (lax.rem(j16, ROWS) == r) & (j16 // ROWS <= lax.rem(i16, STEPS))
        own = jnp.where(keep, own, NEG)
        top = jnp.maximum(jnp.max(old, axis=-1, keepdims=True), jnp.max(own, axis=-1, keepdims=True))
        pold = jnp.exp2(old - top)
        pown = jnp.exp2(own - top)
        total = jnp.sum(pold, axis=-1, keepdims=True) + jnp.sum(pown, axis=-1, keepdims=True)
        mixed = dot(pold.astype(bf16), cv[r]) + dot(pown.astype(bf16), vd[...])
        ms[r] = jnp.broadcast_to(top, (16, 128))
        ls[r] = jnp.broadcast_to(total, (16, 128))
        os_[r] = mixed

    def query(j):
        return remote(qnew, qn.at[batch], qnS.at[j], qnR.at[batch], other(j))

    lck.wait()
    lcv.wait()

    def early_row(r, _):
        old_row(r)
        return 0

    lax.fori_loop(0, 2, early_row, 0)
    for j in range(8):
        query(j).start()
    for k in range(4):
        weight(k).wait_recv()
    lct.wait()
    lst.wait()

    def own_second(q, _):
        acc[0, 1] += dot(xn[q], wq[1, pl.ds(pl.multiple_of(q * PIECE, PIECE), PIECE), :])
        return 0

    lax.fori_loop(0, 4, own_second, 0)
    finish(0, 0)

    clear(0)
    clear(1)

    def near_step(t, _):
        q1 = t
        q2 = lax.rem(t + 2, 4)
        remote(xs.at[1, q1], xs.at[1, q1], agS.at[0, q1], agR.at[0, q1], near(1, 0)).wait_recv()
        remote(xs.at[2, q2], xs.at[2, q2], agS.at[1, q2], agR.at[1, q2], near(1, 0)).wait_recv()

        @pl.when(t < 2)
        def _():
            remote(xs.at[1, q1], xs.at[3, q1], agS.at[0, 4 + t], agR.at[2, q1], near(1, 0)).start()
            remote(xs.at[2, q2], xs.at[3, q2], agS.at[1, 4 + t], agR.at[2, q2], near(-1, 0)).start()

        project(1, q1, 0)
        project(2, q2, 1)

        @pl.when(t < 2)
        def _():
            old_row(t + 2)

        return 0

    lax.fori_loop(0, 4, near_step, 0)
    finish(1, 0)
    finish(2, 1)

    def attend_own(d):
        krows = pl.ds(pl.multiple_of(origin(d) * 256, 256), 256)

        def pair(hp, _):
            q2 = qs[d, pl.ds(hp * 2, 2)].reshape(2 * TOK, HEAD)
            h = hp // 2
            s = dot_t(q2, kv[h, 0, krows, :]) * SCALE2 + bias[0:1, krows]
            qi = lax.rem(lax.broadcasted_iota(jnp.int32, (2 * TOK, 256), 0), TOK) + c * TOK
            ki = lax.broadcasted_iota(jnp.int32, (2 * TOK, 256), 1)
            s = jnp.where(ki <= qi, s, NEG)
            top = jnp.max(s, axis=-1, keepdims=True)
            p = jnp.exp2(s - top)
            sm[d, hp] = jnp.broadcast_to(top, (2 * TOK, HEAD))
            sl[d, hp] = jnp.broadcast_to(jnp.sum(p, axis=-1, keepdims=True), (2 * TOK, HEAD))
            so[d, hp] = dot(p.astype(bf16), kv[h, 1, krows, :])
            return 0

        lax.fori_loop(0, 4, pair, 0)

    def attend_more(d, k):
        krows = pl.ds(pl.multiple_of(origin(k) * 256, 256), 256)

        def pair(hp, _):
            q2 = qs[d, pl.ds(hp * 2, 2)].reshape(2 * TOK, HEAD)
            h = hp // 2
            s = dot_t(q2, kv[h, 0, krows, :]) * SCALE2 + bias[0:1, krows]
            before = sm[d, hp]
            top = jnp.maximum(before, jnp.broadcast_to(jnp.max(s, axis=-1, keepdims=True), (2 * TOK, HEAD)))
            p = jnp.exp2(s - jnp.concatenate([top, top], axis=1))
            fade = jnp.exp2(before - top)
            sm[d, hp] = top
            sl[d, hp] = sl[d, hp] * fade + jnp.broadcast_to(jnp.sum(p, axis=-1, keepdims=True), (2 * TOK, HEAD))
            so[d, hp] = so[d, hp] * fade + dot(p.astype(bf16), kv[h, 1, krows, :])
            return 0

        @pl.when(origin(k) < origin(d))
        def _():
            lax.fori_loop(0, 4, pair, 0)

    def attend_near(d):
        attend_own(d)
        for i in (1, 2) if not isinstance(d, int) else ():
            attend_more(d, lax.rem(d + i, 3))

    def settle(d):
        for hp in range(4):
            o = (so[d, hp] / sl[d, hp]).astype(bf16)
            at[d, :, hp * 256:hp * 256 + HEAD] = o[:TOK]
            at[d, :, hp * 256 + HEAD:(hp + 1) * 256] = o[TOK:]

    for slot in range(3):
        for h in range(2):
            exchanged(slot, h).wait_recv()

    def before_far(i, _):
        attend_near(lax.rem(i + 1, 3))
        return 0

    lax.fori_loop(0, 3, before_far, 0)

    clear(0)

    def far_step(t, _):
        for q in (t, t + 2):
            remote(xs.at[3, q], xs.at[3, q], agS.at[0, q], agR.at[2, q], near(1, 0)).wait_recv()
            project(3, q, 0)
        return 0

    lax.fori_loop(0, 2, far_step, 0)
    finish(3, 0)
    lwo.wait()
    weight(4).wait_recv()
    for h in range(2):
        exchanged(3, h).wait_recv()

    def out_piece(d, q):
        cols = pl.ds(pl.multiple_of(q * PIECE, PIECE), PIECE)
        part = dot(at[d, :, :512], wo[0, :, cols]) + dot(at[d, :, 512:], wo[1, :, cols])
        pb[d, q] = part.astype(bf16)

    def far_send(q):
        if q < 2:
            return remote(pb.at[3, q], fr.at[0, q], fS.at[0, q], fR.at[0, q], near(1, 0))
        return remote(pb.at[3, q], fr.at[1, q - 2], fS.at[1, q - 2], fR.at[1, q - 2], near(-1, 0))

    def near_send(direction, q):
        return remote(
            pb.at[2 - direction, q], nr.at[direction, q], nS.at[direction, q], nR.at[direction, q],
            near(1 - 2 * direction, 0),
        )

    def answer():
        for j in range(8):
            remote(qnew, qn.at[j], qnS.at[j], qnR.at[j], other(j)).wait_recv()
        q = qn[...].reshape(8 * 16, HEAD)
        s = dot_t(q, kv[0, 0]) * SCALE2 + bias[0:1, :]
        top = jnp.max(s, axis=-1, keepdims=True)
        p = jnp.exp2(s - top)
        total = jnp.sum(p, axis=-1, keepdims=True)
        o = dot(p.astype(bf16), kv[0, 1])
        pks[:, 0] = o.reshape(8, 16, HEAD)
        pks[:, 1] = jnp.broadcast_to(top, (128, HEAD)).reshape(8, 16, HEAD)
        pks[:, 2] = jnp.broadcast_to(total, (128, HEAD)).reshape(8, 16, HEAD)

    def reply(j):
        return remote(pks.at[j], pk.at[batch], pkS.at[j], pkR.at[batch], other(j))

    def pieces(d, first, second):
        def piece(k, _):
            out_piece(d, jnp.where(k == 0, first, second))
            return 0

        lax.fori_loop(0, 2, piece, 0)

    attend_more(2, 3)
    settle(2)
    pieces(2, 2, 3)
    near_send(0, 2).start()
    near_send(0, 3).start()
    attend_more(1, 3)
    settle(1)
    pieces(1, 0, 1)
    near_send(1, 0).start()
    near_send(1, 1).start()
    answer()

    attend_own(3)

    def far_keys(k, _):
        attend_more(3, k)
        return 0

    lax.fori_loop(0, 3, far_keys, 0)
    for j in range(8):
        reply(j).start()
    settle(3)
    pieces(3, 0, 2)
    far_send(0).start()
    far_send(2).start()
    pieces(3, 1, 3)
    far_send(1).start()
    far_send(3).start()

    for j in range(8):
        remote(pks.at[j], pk.at[j], pkS.at[j], pkR.at[j], other(j)).wait_recv()
    want = jnp.full((16, 128), assign_ref[0, 0], jnp.int32)
    no = jnp.zeros((16, 128), f32)
    nm = jnp.zeros((16, 128), f32)
    nl = jnp.zeros((16, 128), f32)
    for j in range(8):
        hit = want == j
        no = no + jnp.where(hit, pk[j, 0], 0.0)
        nm = nm + jnp.where(hit, pk[j, 1], 0.0)
        nl = nl + jnp.where(hit, pk[j, 2], 0.0)
    for r in range(ROWS):
        mine = slots == r
        m2 = jnp.where(mine, nm, NEG)
        top = jnp.maximum(ms[r], m2)
        a = jnp.exp2(ms[r] - top)
        b = jnp.exp2(m2 - top)
        o = (os_[r] * a + no * b) / (ls[r] * a + nl * b)
        od[pl.ds(r, 16, stride=ROWS), :] = o
    part = jnp.zeros((16, D), f32)
    for h in range(GROUP):
        part = part + dot(od[pl.ds(h * 16, 16), :].astype(bf16), wo[0, pl.ds(h * HEAD, HEAD), :])
    for k in range(8):
        dsb[k] = part[:, k * 512:(k + 1) * 512].astype(bf16)

    def scatter(j):
        return remote(dsb.at[lax.rem(me + j, 8)], drb.at[j - 1], dS.at[j - 1], dR.at[j - 1], peer(j))

    for j in range(1, 8):
        scatter(j).start()

    pieces(2, 0, 1)
    pieces(1, 2, 3)
    attend_more(0, 3)
    settle(0)
    pieces(0, 0, 2)
    pieces(0, 1, 3)

    for j in range(1, 8):
        scatter(j).wait_recv()
    mycols = pl.ds(pl.multiple_of(me * 512, 512), 512)
    total = dsb[me].astype(f32)
    for j in range(7):
        total = total + drb[j].astype(f32)
    done = (x16[:, mycols] + total).astype(bf16)
    dfb[0] = done
    o32[:, mycols] = done.astype(f32)

    def spread(j):
        return remote(dfb.at[0], dfb.at[j], eS.at[j - 1], eR.at[j - 1], peer(j))

    for j in range(1, 8):
        spread(j).start()

    def relay(q):
        far_send(q).wait_recv()
        pb[2, q] = (pb[2, q].astype(f32) + fr[0, q].astype(f32)).astype(bf16)
        far_send(q + 2).wait_recv()
        pb[1, q + 2] = (pb[1, q + 2].astype(f32) + fr[1, q].astype(f32)).astype(bf16)
        near_send(0, q).start()
        near_send(1, q + 2).start()

    relay(0)
    for j in range(1, 8):
        spread(j).wait_recv()
    for j in range(1, 8):
        cols = pl.ds(pl.multiple_of(lax.rem(me - j + 8, 8) * 512, 512), 512)
        o32[:, cols] = dfb[j].astype(f32)
    dout_ref[...] = o32[...].astype(bf16)
    relay(1)

    for i, q in enumerate((0, 2, 1, 3)):
        near_send(0, q).wait_recv()
        near_send(1, q).wait_recv()
        cols = slice(q * PIECE, (q + 1) * PIECE)
        total = pb[0, q].astype(f32) + nr[0, q].astype(f32) + nr[1, q].astype(f32)
        out_ref[:, cols] = (xs[0, q].astype(f32) + total).astype(bf16)

    for k in range(6):
        gather(0, k).wait_send()
        gather(1, k).wait_send()
    for k in range(5):
        weight(k).wait_send()
    for j in range(8):
        length(j).wait_send()
        query(j).wait_send()
        reply(j).wait_send()
    for slot in range(4):
        for h in range(2):
            exchange(slot, h).wait_send()
    for q in range(4):
        far_send(q).wait_send()
        near_send(0, q).wait_send()
        near_send(1, q).wait_send()
    for j in range(1, 8):
        scatter(j).wait_send()
        spread(j).wait_send()


def body(
    prompt, prompt_len, dec_tokens, cache_k, cache_v, cache_len, assign, slot, gain, w_qkv, w_out
):
    ct, st, fr = tables()
    any_ = pl.BlockSpec(memory_space=pl.ANY)
    smem = pl.BlockSpec(memory_space=pltpu.SMEM)
    vmem = pl.BlockSpec(memory_space=pltpu.VMEM)
    V = pltpu.VMEM
    dma = pltpu.SemaphoreType.DMA
    OUT = pltpu.VMEM
    out, dout = pl.pallas_call(
        kernel,
        out_shape=(
            OUT((TOK, D), bf16),
            OUT((16, D), bf16),
        ),
        in_specs=[smem] * 4 + [vmem] * 2 + [any_] * 8,
        out_specs=(vmem, vmem),
        scratch_shapes=[
            V((4, 4, TOK, PIECE), bf16),
            V((2, D, QKV), bf16),
            V((2, 512, D), bf16),
            V((ROWS, CACHE, HEAD), bf16),
            V((ROWS, CACHE, HEAD), bf16),
            V((2, 2, TOK, QKV), f32),
            V((2, TOK, HEAD), f32),
            V((4, 8, TOK, HEAD), bf16),
            V((2, 2, STRETCH, HEAD), bf16),
            V((4, 4, 2 * TOK, HEAD), f32),
            V((4, 4, 2 * TOK, HEAD), f32),
            V((4, 4, 2 * TOK, HEAD), f32),
            V((4, TOK, 1024), bf16),
            V((4, 4, TOK, PIECE), bf16),
            V((2, 2, TOK, PIECE), bf16),
            V((2, 4, TOK, PIECE), bf16),
            V((STRETCH, HEAD), f32),
            V((STRETCH, HEAD), f32),
            V((8, STRETCH), f32),
            V((4, TOK, PIECE), bf16),
            V((STEPS, ROWS, D), bf16),
            V((16, D), f32),
            V((16, D), bf16),
            V((64, HEAD), f32),
            V((16, HEAD), bf16),
            V((16, HEAD), bf16),
            V((ROWS, 16, HEAD), bf16),
            V((ROWS, 16, HEAD), f32),
            V((ROWS, 16, HEAD), f32),
            V((ROWS, 16, HEAD), f32),
            V((8, 128), jnp.int32),
            V((8, 8, 128), jnp.int32),
            V((16, HEAD), bf16),
            V((8, 16, HEAD), bf16),
            V((8, 3, 16, HEAD), f32),
            V((8, 3, 16, HEAD), f32),
            V((64, HEAD), f32),
            V((8, 16, 512), bf16),
            V((7, 16, 512), bf16),
            V((8, 16, 512), bf16),
            V((16, D), f32),
            dma((14,)),
            dma((2, 6)), dma((3, 4)),
            dma((5,)), dma((5,)),
            dma((8,)), dma((8,)),
            dma((8,)), dma((8,)),
            dma((8,)), dma((8,)),
            dma((4, 2)), dma((4, 2)),
            dma((2, 2)), dma((2, 2)),
            dma((2, 4)), dma((2, 4)),
            dma((7,)), dma((7,)),
            dma((7,)), dma((7,)),
        ],
        compiler_params=pltpu.CompilerParams(
            collective_id=0, has_side_effects=True, vmem_limit_bytes=59 * 2**20
        ),
        name="layer",
    )(
        prompt_len, assign, slot, cache_len, gain.reshape(1, D), jnp.asarray(fr),
        prompt, dec_tokens, cache_k, cache_v, w_qkv, w_out, jnp.asarray(ct), jnp.asarray(st),
    )
    return pl.pallas_call(
        writer,
        out_shape=(
            jax.ShapeDtypeStruct((1, TOK, D), bf16),
            jax.ShapeDtypeStruct((STEPS, ROWS, D), bf16),
        ),
        in_specs=[vmem, vmem],
        out_specs=(any_, any_),
        scratch_shapes=[V((STEPS, ROWS, D), bf16), dma((2,))],
        compiler_params=pltpu.CompilerParams(vmem_limit_bytes=8 * 2**20),
        name="write",
    )(out, dout)


def writer(out_ref, dout_ref, full_ref, dec_ref, stage, sem):
    copies = [pltpu.make_async_copy(out_ref, full_ref.at[0], sem.at[0])]
    copies[0].start()
    for s in range(STEPS):
        stage[s] = dout_ref[pl.ds(s * ROWS, ROWS), :]
    copies.append(pltpu.make_async_copy(stage, dec_ref, sem.at[1]))
    copies[1].start()
    for cp in copies:
        cp.wait()


def solution(mesh):
    return jax.shard_map(
        body,
        mesh=mesh,
        in_specs=(
            P(("pool", "batch"), "blk", None),
            P("pool", "batch"),
            P(None, ("pool", "batch"), None),
            P(("pool", "batch"), None, "blk"),
            P(("pool", "batch"), None, "blk"),
            P(("pool", "batch")),
            P("pool", "batch"),
            P("pool", "batch"),
            P(),
            P(None, "blk"),
            P("blk", None),
        ),
        out_specs=(P(("pool", "batch"), "blk", None), P(None, ("pool", "batch"), None)),
        check_vma=False,
    )
```

```python
import functools

import jax
import jax.numpy as jnp
import numpy as np
from jax import lax
from jax.experimental import pallas as pl
from jax.experimental.pallas import tpu as pltpu
from jax.sharding import PartitionSpec as P

MESH = pl.DeviceIdType.MESH
HEAD = 128
GROUP = 4
D = 4096
TOK = 128
STRETCH = 1024
CACHE = 4096
STEPS = 4
ROWS = 4
QKV = (GROUP + 2) * HEAD
PIECE = 1024
EPSILON = 1e-05
THETA = 500000.0
NEG = -1e30
SCALE2 = float(HEAD ** (-0.5) * np.log2(np.e))

f32 = jnp.float32
bf16 = jnp.bfloat16


def tables():
    half = HEAD // 2
    freqs = (THETA ** (-np.arange(half, dtype=np.float64) / half)).astype(np.float32)
    angles = np.arange(STRETCH, dtype=np.float32)[:, None] * freqs
    cosine = np.cos(angles.astype(np.float64)).astype(np.float32)
    sine = np.sin(angles.astype(np.float64)).astype(np.float32)
    ct = np.concatenate([cosine, cosine], axis=1)
    st = np.concatenate([-sine, sine], axis=1)
    fr = np.broadcast_to(np.concatenate([freqs, freqs])[None, :], (8, HEAD))
    return ct, st, np.ascontiguousarray(fr)


def dot(a, b):
    return jnp.dot(a, b, preferred_element_type=f32)


def dot_t(a, b):
    return lax.dot_general(a, b, (((1,), (1,)), ((), ())), preferred_element_type=f32)


def kernel(
    plen_in, assign_in, slot_in, clen_in, gain_in, freq_in,
    prompt_ref, dec_ref, ck_ref, cv_ref, wqkv_ref, wout_ref, ct_ref, st_ref,
    out_ref, dout_ref,
    plen_ref, assign_ref, slot_ref, clen_ref, gain_ref, freq_ref,
    xs, wq, wo, ck, cv, acc, ssq, qs, kv, so, sm, at, pb, fr, nr, ct, st, bias,
    xn, dmv, x16, xd, jd, qd, kd, vd, qr, ms, ls, os_, plt, pls, qnew, qn, pks, pk, od, dsb, drb, dfb, o32,
    ring, opened, ssem, lsem, agS, agR, wS, wR, plS, plR, qnS, qnR, pkS, pkR, kvS, kvR, fS, fR, nS, nR, dS, dR, eS, eR,
):
    me = lax.axis_index("blk")
    pool = lax.axis_index("pool")
    batch = lax.axis_index("batch")
    x = me // 2
    c = lax.rem(me, 2)

    def near(dx, dc):
        return {"blk": lax.rem(x + dx + 4, 4) * 2 + lax.rem(c + dc, 2)}

    def other(j):
        return {"pool": 1 - pool, "batch": j}

    def peer(j):
        return {"blk": lax.rem(me + j, 8)}

    def remote(src, dst, ss, rs, dev):
        return pltpu.make_async_remote_copy(
            src_ref=src, dst_ref=dst, send_sem=ss, recv_sem=rs, device_id=dev, device_id_type=MESH
        )

    local = [pltpu.make_async_copy(dec_ref, dmv, lsem.at[1])]
    for q in range(4):
        rows = pl.ds(q * PIECE, PIECE)
        local.append(pltpu.make_async_copy(wqkv_ref.at[rows], wq.at[0, rows], lsem.at[2 + q]))
    local.append(pltpu.make_async_copy(ct_ref, ct, lsem.at[6]))
    local.append(pltpu.make_async_copy(st_ref, st, lsem.at[7]))
    local.append(pltpu.make_async_copy(ck_ref, ck, lsem.at[8]))
    local.append(pltpu.make_async_copy(cv_ref, cv, lsem.at[9]))
    local.append(pltpu.make_async_copy(wout_ref, wo.at[0], lsem.at[10]))
    for q in range(4):
        local.insert(2 + 2 * q, pltpu.make_async_copy(prompt_ref.at[0, :, pl.ds(q * PIECE, PIECE)], xs.at[0, q], lsem.at[(0, 11, 12, 13)[q]]))
    ldec, w0, t0, w1, t1, w2, t2, w3, t3, lct, lst, lck, lcv, lwo = local
    lweights = (w0, w1, w2, w3)
    ltokens = (t0, t1, t2, t3)
    small = [
        pltpu.make_async_copy(a, b, ssem.at[i])
        for i, (a, b) in enumerate((
            (plen_in, plen_ref), (assign_in, assign_ref), (slot_in, slot_ref),
            (clen_in, clen_ref), (gain_in, gain_ref), (freq_in, freq_ref),
        ))
    ]
    for cp in small:
        cp.start()
    for cp in local:
        cp.start()

    barrier = pltpu.get_barrier_semaphore()
    gate = me == 0
    for j in range(1, 8):
        @pl.when(lax.rem(me + j, 8) != 0)
        def _(j=j):
            pl.semaphore_signal(barrier, inc=1, device_id=peer(j), device_id_type=MESH)

    kv[:, :, 2 * HEAD:] = jnp.ones((2, STRETCH, HEAD), bf16)

    @pl.when(me != 0)
    def _():
        pl.semaphore_wait(barrier, 7)

    @pl.when(me == 1)
    def _():
        pl.semaphore_signal(ring, inc=1, device_id=peer(7), device_id_type=MESH)

    @pl.when(gate)
    def _():
        pl.semaphore_wait(ring, 1)

    def gather(direction, k):
        if direction == 0:
            if k < 4:
                return remote(prompt_ref.at[0, :, pl.ds(k * PIECE, PIECE)], xs.at[1, k], agS.at[0, k], agR.at[0, k], near(1, 0))
            return remote(xs.at[1, k - 4], xs.at[3, k - 4], agS.at[0, k], agR.at[2, k - 4], near(1, 0))
        if k < 4:
            q = (k + 2) % 4
            return remote(prompt_ref.at[0, :, pl.ds(q * PIECE, PIECE)], xs.at[2, q], agS.at[1, k], agR.at[1, q], near(-1, 0))
        return remote(xs.at[2, k - 2], xs.at[3, k - 2], agS.at[1, k], agR.at[2, k - 2], near(-1, 0))

    for k in range(4):
        gather(0, k).start()
        gather(1, k).start()

    def weight(k):
        if k < 4:
            rows = pl.ds(k * PIECE, PIECE)
            return remote(wqkv_ref.at[rows], wq.at[1, rows], wS.at[k], wR.at[k], near(0, 1))
        return remote(wout_ref, wo.at[1], wS.at[4], wR.at[4], near(0, 1))

    for k in range(5):
        weight(k).start()

    @pl.when(gate)
    def _():
        for j in range(8):
            pl.semaphore_signal(barrier, inc=1, device_id=other(j), device_id_type=MESH)

    for cp in small:
        cp.wait()
    plt[...] = jnp.full((8, 128), plen_ref[0, 0], jnp.int32)
    col = lax.broadcasted_iota(jnp.int32, (8, STRETCH), 1)
    bias[...] = jnp.where(col < jnp.full((8, STRETCH), plen_ref[0, 0], jnp.int32), 0.0, NEG)

    ldec.wait()
    for s in range(STEPS):
        x16[pl.ds(s * ROWS, ROWS), :] = dmv[s].astype(f32)
    wide = x16[...]
    factor = lax.rsqrt(jnp.mean(wide * wide, axis=-1, keepdims=True) + EPSILON)
    xd[...] = (wide * factor * gain_ref[...]).astype(bf16)
    joined = jnp.zeros((16, QKV), f32)
    for q in range(4):
        lweights[q].wait()
        joined = joined + dot(xd[:, q * PIECE:(q + 1) * PIECE], wq[0, pl.ds(q * PIECE, PIECE), :])
    jd[...] = joined

    def scaled(slot, q, a):
        wide = xs[slot, q].astype(f32)
        square = wide * wide
        part = square[:, :HEAD]
        for i in range(1, PIECE // HEAD):
            part = part + square[:, i * HEAD:(i + 1) * HEAD]
        ssq[a] += part
        return (wide * gain_ref[:, pl.ds(pl.multiple_of(q * PIECE, PIECE), PIECE)]).astype(bf16)

    def project(slot, q, a):
        tokens = scaled(slot, q, a)
        rows = pl.ds(pl.multiple_of(q * PIECE, PIECE), PIECE)
        for h in range(2):
            acc[a, h] += dot(tokens, wq[h, rows, :])

    def clear(a):
        acc[a] = jnp.zeros((2, TOK, QKV), f32)
        ssq[a] = jnp.zeros((TOK, HEAD), f32)

    clear(0)
    for q in range(4):
        ltokens[q].wait()

    def own_first(q, _):
        tokens = scaled(0, q, 0)
        xn[q] = tokens
        acc[0, 0] += dot(tokens, wq[0, pl.ds(pl.multiple_of(q * PIECE, PIECE), PIECE), :])
        return 0

    lax.fori_loop(0, 4, own_first, 0)

    def turn(u, cosine, sine):
        return u * cosine + pltpu.roll(u, HEAD // 2, 1) * sine

    def decode_queries():
        wanted = jnp.full((8, 128), assign_ref[0, 0], jnp.int32)
        newlen = jnp.zeros((8, 128), jnp.int32)
        for j in range(8):
            remote(plt, pls.at[j], plS.at[j], plR.at[j], other(j)).wait_recv()
        for j in range(8):
            newlen = newlen + jnp.where(wanted == j, pls[j], 0)
        row = lax.broadcasted_iota(jnp.int32, (16, 128), 0)
        row_r = lax.rem(row, ROWS)
        place = jnp.zeros((16, 128), jnp.int32)
        for r in range(ROWS):
            place = jnp.where(row_r == r, jnp.full((16, 128), clen_ref[r], jnp.int32), place)
        fresh = row_r == jnp.full((16, 128), slot_ref[0, 0], jnp.int32)
        place = jnp.where(fresh, jnp.broadcast_to(newlen[0:1, :], (16, 128)), place) + row // ROWS
        angle = place.astype(f32) * freq_ref[0:1, :]
        lane = lax.broadcasted_iota(jnp.int32, (16, 128), 1)
        dcos = jnp.cos(angle)
        dsin = jnp.sin(angle)
        dsin = jnp.where(lane < HEAD // 2, -dsin, dsin)

        for h in range(GROUP):
            qd[pl.ds(h * 16, 16), :] = turn(jd[:, h * HEAD:(h + 1) * HEAD], dcos, dsin)
        kd[...] = turn(jd[:, GROUP * HEAD:(GROUP + 1) * HEAD], dcos, dsin).astype(bf16)
        vd[...] = jd[:, (GROUP + 1) * HEAD:].astype(bf16)
        slots = jnp.full((16, 128), slot_ref[0, 0], jnp.int32)
        picked = jnp.zeros((16, 128), f32)
        for r in range(ROWS):
            part = qd[pl.ds(r, 16, stride=ROWS), :]
            qr[r] = part.astype(bf16)
            picked = picked + jnp.where(slots == r, part, 0.0)
        qnew[...] = picked.astype(bf16)

    def origin(slot):
        if isinstance(slot, int):
            return lax.rem(x + (0, 3, 1, 2)[slot], 4)
        return lax.rem(x + jnp.where(slot == 1, 3, jnp.where(slot == 2, 1, jnp.where(slot == 3, 2, 0))), 4)

    def exchange(slot, h):
        rows = pl.ds(pl.multiple_of((origin(slot) * 2 + c) * TOK, TOK), TOK)
        return remote(kv.at[h, rows, pl.ds(0, 2 * HEAD)], kv.at[1 - h, rows, pl.ds(0, 2 * HEAD)], kvS.at[slot, h], kvR.at[slot, 1 - h], near(0, 1))

    def exchanged(slot, h):
        rows = pl.ds(pl.multiple_of((origin(slot) * 2 + 1 - c) * TOK, TOK), TOK)
        return remote(kv.at[h, rows, pl.ds(0, 2 * HEAD)], kv.at[h, rows, pl.ds(0, 2 * HEAD)], kvS.at[slot, h], kvR.at[slot, h], near(0, 1))

    def finish(slot, a):
        rows = pl.ds(pl.multiple_of((origin(slot) * 2 + c) * TOK, TOK), TOK)
        factor = lax.rsqrt(jnp.sum(ssq[a], axis=-1, keepdims=True) * (1.0 / D) + EPSILON)
        cosine = ct[rows, :] * factor
        sine = st[rows, :] * factor
        for h in range(2):
            kv[h, rows, :HEAD] = turn(acc[a, h, :, GROUP * HEAD:(GROUP + 1) * HEAD], cosine, sine).astype(bf16)
            kv[h, rows, HEAD:2 * HEAD] = (acc[a, h, :, (GROUP + 1) * HEAD:] * factor).astype(bf16)
        for h in range(2):
            for g in range(GROUP):
                qs[slot, h * GROUP + g] = turn(acc[a, h, :, g * HEAD:(g + 1) * HEAD], cosine, sine).astype(bf16)
        for h in range(2):
            exchange(slot, h).start()

    def old_row(r):
        q16 = qr[r]
        edge = jnp.full((16, CACHE), clen_ref[r], jnp.int32)
        edge = jnp.where(jnp.full((16, CACHE), slot_ref[0, 0], jnp.int32) == r, 0, edge)
        span = lax.broadcasted_iota(jnp.int32, (16, CACHE), 1)
        old = jnp.where(span < edge, dot_t(q16, ck[r]) * SCALE2, NEG)
        own = dot_t(q16, kd[...]) * SCALE2
        i16 = lax.broadcasted_iota(jnp.int32, (16, 16), 0)
        j16 = lax.broadcasted_iota(jnp.int32, (16, 16), 1)
        keep = (lax.rem(j16, ROWS) == r) & (j16 // ROWS <= lax.rem(i16, STEPS))
        own = jnp.where(keep, own, NEG)
        top = jnp.maximum(jnp.max(old, axis=-1, keepdims=True), jnp.max(own, axis=-1, keepdims=True))
        pold = jnp.exp2(old - top)
        pown = jnp.exp2(own - top)
        total = jnp.sum(pold, axis=-1, keepdims=True) + jnp.sum(pown, axis=-1, keepdims=True)
        mixed = dot(pold.astype(bf16), cv[r]) + dot(pown.astype(bf16), vd[...])
        ms[r] = jnp.broadcast_to(top, (16, 128))
        ls[r] = jnp.broadcast_to(total, (16, 128))
        os_[r] = mixed

    def query(j):
        return remote(qnew, qn.at[batch], qnS.at[j], qnR.at[batch], other(j))

    @pl.when(gate)
    def _():
        pl.semaphore_wait(barrier, 8)
        for j in range(1, 8):
            pl.semaphore_signal(opened, inc=1, device_id=peer(j), device_id_type=MESH)

    @pl.when(me != 0)
    def _():
        pl.semaphore_wait(opened, 1)

    def length(j):
        return remote(plt, pls.at[batch], plS.at[j], plR.at[batch], other(j))

    for j in range(8):
        length(j).start()

    for k in range(4):
        weight(k).wait_recv()
    lct.wait()
    lst.wait()

    def own_second(q, _):
        acc[0, 1] += dot(xn[q], wq[1, pl.ds(pl.multiple_of(q * PIECE, PIECE), PIECE), :])
        return 0

    lax.fori_loop(0, 4, own_second, 0)
    finish(0, 0)

    clear(0)
    clear(1)
    lck.wait()
    lcv.wait()

    def near_step(t, _):
        q1 = t
        q2 = lax.rem(t + 2, 4)
        remote(xs.at[1, q1], xs.at[1, q1], agS.at[0, q1], agR.at[0, q1], near(1, 0)).wait_recv()
        remote(xs.at[2, q2], xs.at[2, q2], agS.at[1, q2], agR.at[1, q2], near(1, 0)).wait_recv()

        @pl.when(t < 2)
        def _():
            remote(xs.at[1, q1], xs.at[3, q1], agS.at[0, 4 + t], agR.at[2, q1], near(1, 0)).start()
            remote(xs.at[2, q2], xs.at[3, q2], agS.at[1, 4 + t], agR.at[2, q2], near(-1, 0)).start()

        project(1, q1, 0)
        project(2, q2, 1)

        @pl.when(t == 1)
        def _():
            decode_queries()
            for j in range(2):
                old_row(j)
            for j in range(8):
                query(j).start()
            for j in range(2, 4):
                old_row(j)

        return 0

    lax.fori_loop(0, 4, near_step, 0)
    finish(1, 0)
    finish(2, 1)

    def attend_own(d):
        krows = pl.ds(pl.multiple_of(origin(d) * 256, 256), 256)
        qi = lax.rem(lax.broadcasted_iota(jnp.int32, (2 * TOK, 256), 0), TOK) + c * TOK
        ki = lax.broadcasted_iota(jnp.int32, (2 * TOK, 256), 1)
        mask = jnp.where(ki <= qi, jnp.broadcast_to(bias[0:1, krows], (2 * TOK, 256)), NEG)
        for hp in range(4):
            q2 = qs[d, 2 * hp:2 * hp + 2].reshape(2 * TOK, HEAD)
            h = hp // 2
            s = dot_t(q2, kv[h, krows, :HEAD]) * SCALE2 + mask
            top = jnp.max(s, axis=-1, keepdims=True)
            p = jnp.exp2(s - top)
            sm[d, hp] = jnp.broadcast_to(top, (2 * TOK, HEAD))
            so[d, hp] = dot(p.astype(bf16), kv[h, krows, HEAD:])

    def attend_more(d, k):
        krows = pl.ds(pl.multiple_of(origin(k) * 256, 256), 256)

        @pl.when(origin(k) < origin(d))
        def _():
            for hp in range(4):
                q2 = qs[d, 2 * hp:2 * hp + 2].reshape(2 * TOK, HEAD)
                h = hp // 2
                s = dot_t(q2, kv[h, krows, :HEAD]) * SCALE2 + bias[0:1, krows]
                before = sm[d, hp]
                top = jnp.maximum(before, jnp.broadcast_to(jnp.max(s, axis=-1, keepdims=True), (2 * TOK, HEAD)))
                p = jnp.exp2(s - jnp.concatenate([top, top], axis=1))
                fade = jnp.exp2(before - top)
                sm[d, hp] = top
                so[d, hp] = so[d, hp] * jnp.concatenate([fade, fade], axis=1) + dot(p.astype(bf16), kv[h, krows, HEAD:])

    def attend_near(d):
        attend_own(d)

        def others(i, _):
            attend_more(d, lax.rem(d + i, 3))
            return 0

        lax.fori_loop(1, 3, others, 0)

    def settle(d):
        for hp in range(4):
            o = (so[d, hp, :, :HEAD] / so[d, hp, :, HEAD:]).astype(bf16)
            at[d, :, hp * 256:hp * 256 + HEAD] = o[:TOK]
            at[d, :, hp * 256 + HEAD:(hp + 1) * 256] = o[TOK:]

    for slot in range(3):
        for h in range(2):
            exchanged(slot, h).wait_recv()

    def before_far(i, _):
        attend_near(lax.rem(i + 1, 3))
        return 0

    lax.fori_loop(0, 3, before_far, 0)

    clear(0)

    def far_step(t, _):
        for q in (t, t + 2):
            remote(xs.at[3, q], xs.at[3, q], agS.at[0, q], agR.at[2, q], near(1, 0)).wait_recv()
            project(3, q, 0)
        return 0

    lax.fori_loop(0, 2, far_step, 0)
    finish(3, 0)
    lwo.wait()
    weight(4).wait_recv()
    for h in range(2):
        exchanged(3, h).wait_recv()

    def out_piece(d, q):
        cols = pl.ds(pl.multiple_of(q * PIECE, PIECE), PIECE)
        part = dot(at[d, :, :512], wo[0, :, cols]) + dot(at[d, :, 512:], wo[1, :, cols])
        pb[d, q] = part.astype(bf16)

    def far_send(q):
        if q < 2:
            return remote(pb.at[3, q], fr.at[0, q], fS.at[0, q], fR.at[0, q], near(1, 0))
        return remote(pb.at[3, q], fr.at[1, q - 2], fS.at[1, q - 2], fR.at[1, q - 2], near(-1, 0))

    def near_send(direction, q):
        return remote(
            pb.at[2 - direction, q], nr.at[direction, q], nS.at[direction, q], nR.at[direction, q],
            near(1 - 2 * direction, 0),
        )

    def answer():
        for j in range(8):
            remote(qnew, qn.at[j], qnS.at[j], qnR.at[j], other(j)).wait_recv()
        q = qn[...].reshape(8 * 16, HEAD)
        s = dot_t(q, kv[0, :, :HEAD]) * SCALE2 + bias[0:1, :]
        top = jnp.max(s, axis=-1, keepdims=True)
        p = jnp.exp2(s - top)
        o = dot(p.astype(bf16), kv[0, :, HEAD:])
        pks[:, 0] = o[:, :HEAD].reshape(8, 16, HEAD)
        pks[:, 1] = jnp.broadcast_to(top, (128, HEAD)).reshape(8, 16, HEAD)
        pks[:, 2] = o[:, HEAD:].reshape(8, 16, HEAD)

    def reply(j):
        return remote(pks.at[j], pk.at[batch], pkS.at[j], pkR.at[batch], other(j))

    def pieces(d, first, second):
        def piece(k, _):
            out_piece(d, jnp.where(k == 0, first, second))
            return 0

        lax.fori_loop(0, 2, piece, 0)

    attend_more(2, 3)
    settle(2)
    out_piece(2, 2)
    near_send(0, 2).start()
    attend_more(1, 3)
    settle(1)
    out_piece(1, 0)
    near_send(1, 0).start()
    out_piece(2, 3)
    near_send(0, 3).start()
    out_piece(1, 1)
    near_send(1, 1).start()
    answer()

    attend_own(3)
    for j in range(8):
        reply(j).start()

    def far_keys(k, _):
        attend_more(3, k)
        return 0

    lax.fori_loop(0, 3, far_keys, 0)
    settle(3)
    pieces(3, 0, 2)
    far_send(0).start()
    far_send(2).start()
    pieces(3, 1, 3)
    pieces(2, 0, 1)
    pieces(1, 2, 3)
    for j in range(8):
        remote(pks.at[j], pk.at[j], pkS.at[j], pkR.at[j], other(j)).wait_recv()
    want = jnp.full((16, 128), assign_ref[0, 0], jnp.int32)
    no = jnp.zeros((16, 128), f32)
    nm = jnp.zeros((16, 128), f32)
    nl = jnp.zeros((16, 128), f32)
    for j in range(8):
        hit = want == j
        no = no + jnp.where(hit, pk[j, 0], 0.0)
        nm = nm + jnp.where(hit, pk[j, 1], 0.0)
        nl = nl + jnp.where(hit, pk[j, 2], 0.0)
    slots = jnp.full((16, 128), slot_ref[0, 0], jnp.int32)
    for r in range(ROWS):
        mine = slots == r
        m2 = jnp.where(mine, nm, NEG)
        top = jnp.maximum(ms[r], m2)
        a = jnp.exp2(ms[r] - top)
        b = jnp.exp2(m2 - top)
        o = (os_[r] * a + no * b) / (ls[r] * a + nl * b)
        od[pl.ds(r, 16, stride=ROWS), :] = o
    part = jnp.zeros((16, D), f32)
    for h in range(GROUP):
        part = part + dot(od[pl.ds(h * 16, 16), :].astype(bf16), wo[0, pl.ds(h * HEAD, HEAD), :])
    for k in range(8):
        dsb[k] = part[:, k * 512:(k + 1) * 512].astype(bf16)

    def scatter(j):
        return remote(dsb.at[lax.rem(me + j, 8)], drb.at[j - 1], dS.at[j - 1], dR.at[j - 1], peer(j))

    for j in range(1, 8):
        scatter(j).start()

    far_send(1).start()
    far_send(3).start()

    attend_more(0, 3)
    settle(0)
    pieces(0, 0, 2)
    pieces(0, 1, 3)

    def relay(q):
        far_send(q).wait_recv()
        pb[2, q] = (pb[2, q].astype(f32) + fr[0, q].astype(f32)).astype(bf16)
        far_send(q + 2).wait_recv()
        pb[1, q + 2] = (pb[1, q + 2].astype(f32) + fr[1, q].astype(f32)).astype(bf16)
        near_send(0, q).start()
        near_send(1, q + 2).start()

    relay(0)
    for j in range(1, 8):
        scatter(j).wait_recv()
    mycols = pl.ds(pl.multiple_of(me * 512, 512), 512)
    total = dsb[me].astype(f32)
    for j in range(7):
        total = total + drb[j].astype(f32)
    done = (x16[:, mycols] + total).astype(bf16)
    dfb[0] = done
    o32[:, mycols] = done.astype(f32)

    def spread(j):
        return remote(dfb.at[0], dfb.at[j], eS.at[j - 1], eR.at[j - 1], peer(j))

    for j in range(1, 8):
        spread(j).start()

    relay(1)
    for j in range(1, 8):
        spread(j).wait_recv()
    for j in range(1, 8):
        cols = pl.ds(pl.multiple_of(lax.rem(me - j + 8, 8) * 512, 512), 512)
        o32[:, cols] = dfb[j].astype(f32)
    dout_ref[...] = o32[...].astype(bf16)

    for i, q in enumerate((0, 2, 1, 3)):
        near_send(0, q).wait_recv()
        near_send(1, q).wait_recv()
        cols = slice(q * PIECE, (q + 1) * PIECE)
        total = pb[0, q].astype(f32) + nr[0, q].astype(f32) + nr[1, q].astype(f32)
        out_ref[:, cols] = (xs[0, q].astype(f32) + total).astype(bf16)

    for k in range(6):
        gather(0, k).wait_send()
        gather(1, k).wait_send()
    for k in range(5):
        weight(k).wait_send()
    for j in range(8):
        length(j).wait_send()
        query(j).wait_send()
        reply(j).wait_send()
    for slot in range(4):
        for h in range(2):
            exchange(slot, h).wait_send()
    for q in range(4):
        far_send(q).wait_send()
        near_send(0, q).wait_send()
        near_send(1, q).wait_send()
    for j in range(1, 8):
        scatter(j).wait_send()
        spread(j).wait_send()


def body(
    prompt, prompt_len, dec_tokens, cache_k, cache_v, cache_len, assign, slot, gain, w_qkv, w_out
):
    ct, st, fr = tables()
    any_ = pl.BlockSpec(memory_space=pl.ANY)
    vmem = pl.BlockSpec(memory_space=pltpu.VMEM)
    V = pltpu.VMEM
    dma = pltpu.SemaphoreType.DMA
    OUT = pltpu.VMEM
    out, dout = pl.pallas_call(
        kernel,
        out_shape=(
            OUT((TOK, D), bf16),
            OUT((16, D), bf16),
        ),
        in_specs=[any_] * 14,
        out_specs=(vmem, vmem),
        scratch_shapes=[
            pltpu.SMEM((1, 1), jnp.int32),
            pltpu.SMEM((1, 1), jnp.int32),
            pltpu.SMEM((1, 1), jnp.int32),
            pltpu.SMEM((ROWS,), jnp.int32),
            V((1, D), f32),
            V((8, HEAD), f32),
            V((4, 4, TOK, PIECE), bf16),
            V((2, D, QKV), bf16),
            V((2, 512, D), bf16),
            V((ROWS, CACHE, HEAD), bf16),
            V((ROWS, CACHE, HEAD), bf16),
            V((2, 2, TOK, QKV), f32),
            V((2, TOK, HEAD), f32),
            V((4, 8, TOK, HEAD), bf16),
            V((2, STRETCH, 3 * HEAD), bf16),
            V((4, 4, 2 * TOK, 2 * HEAD), f32),
            V((4, 4, 2 * TOK, HEAD), f32),
            V((4, TOK, 1024), bf16),
            V((4, 4, TOK, PIECE), bf16),
            V((2, 2, TOK, PIECE), bf16),
            V((2, 4, TOK, PIECE), bf16),
            V((STRETCH, HEAD), f32),
            V((STRETCH, HEAD), f32),
            V((8, STRETCH), f32),
            V((4, TOK, PIECE), bf16),
            V((STEPS, ROWS, D), bf16),
            V((16, D), f32),
            V((16, D), bf16),
            V((16, QKV), f32),
            V((64, HEAD), f32),
            V((16, HEAD), bf16),
            V((16, HEAD), bf16),
            V((ROWS, 16, HEAD), bf16),
            V((ROWS, 16, HEAD), f32),
            V((ROWS, 16, HEAD), f32),
            V((ROWS, 16, HEAD), f32),
            V((8, 128), jnp.int32),
            V((8, 8, 128), jnp.int32),
            V((16, HEAD), bf16),
            V((8, 16, HEAD), bf16),
            V((8, 3, 16, HEAD), f32),
            V((8, 3, 16, HEAD), f32),
            V((64, HEAD), f32),
            V((8, 16, 512), bf16),
            V((7, 16, 512), bf16),
            V((8, 16, 512), bf16),
            V((16, D), f32),
            pltpu.SemaphoreType.REGULAR,
            pltpu.SemaphoreType.REGULAR,
            dma((6,)),
            dma((14,)),
            dma((2, 6)), dma((3, 4)),
            dma((5,)), dma((5,)),
            dma((8,)), dma((8,)),
            dma((8,)), dma((8,)),
            dma((8,)), dma((8,)),
            dma((4, 2)), dma((4, 2)),
            dma((2, 2)), dma((2, 2)),
            dma((2, 4)), dma((2, 4)),
            dma((7,)), dma((7,)),
            dma((7,)), dma((7,)),
        ],
        compiler_params=pltpu.CompilerParams(
            collective_id=0, has_side_effects=True, vmem_limit_bytes=59 * 2**20
        ),
        name="layer",
    )(
        prompt_len, assign, slot, cache_len, gain.reshape(1, D), jnp.asarray(fr),
        prompt, dec_tokens, cache_k, cache_v, w_qkv, w_out, jnp.asarray(ct), jnp.asarray(st),
    )
    return pl.pallas_call(
        writer,
        out_shape=(
            jax.ShapeDtypeStruct((1, TOK, D), bf16),
            jax.ShapeDtypeStruct((STEPS, ROWS, D), bf16),
        ),
        in_specs=[vmem, vmem],
        out_specs=(any_, any_),
        scratch_shapes=[V((STEPS, ROWS, D), bf16), dma((2,))],
        compiler_params=pltpu.CompilerParams(vmem_limit_bytes=8 * 2**20),
        name="write",
    )(out, dout)


def writer(out_ref, dout_ref, full_ref, dec_ref, stage, sem):
    copies = [pltpu.make_async_copy(out_ref, full_ref.at[0], sem.at[0])]
    copies[0].start()
    for s in range(STEPS):
        stage[s] = dout_ref[pl.ds(s * ROWS, ROWS), :]
    copies.append(pltpu.make_async_copy(stage, dec_ref, sem.at[1]))
    copies[1].start()
    for cp in copies:
        cp.wait()


def solution(mesh):
    return jax.shard_map(
        body,
        mesh=mesh,
        in_specs=(
            P(("pool", "batch"), "blk", None),
            P("pool", "batch"),
            P(None, ("pool", "batch"), None),
            P(("pool", "batch"), None, "blk"),
            P(("pool", "batch"), None, "blk"),
            P(("pool", "batch")),
            P("pool", "batch"),
            P("pool", "batch"),
            P(),
            P(None, "blk"),
            P("blk", None),
        ),
        out_specs=(P(("pool", "batch"), "blk", None), P(None, ("pool", "batch"), None)),
        check_vma=False,
    )
```

```python
import functools

import jax
import jax.numpy as jnp
import numpy as np
from jax import lax
from jax.experimental import pallas as pl
from jax.experimental.pallas import tpu as pltpu
from jax.sharding import PartitionSpec as P

MESH = pl.DeviceIdType.MESH
HEAD = 128
GROUP = 4
D = 4096
TOK = 128
STRETCH = 1024
CACHE = 4096
STEPS = 4
ROWS = 4
QKV = (GROUP + 2) * HEAD
PIECE = 1024
EPSILON = 1e-05
THETA = 500000.0
NEG = -1e30
SCALE2 = float(HEAD ** (-0.5) * np.log2(np.e))

f32 = jnp.float32
bf16 = jnp.bfloat16


def tables():
    half = HEAD // 2
    freqs = (THETA ** (-np.arange(half, dtype=np.float64) / half)).astype(np.float32)
    angles = np.arange(STRETCH, dtype=np.float32)[:, None] * freqs
    cosine = np.cos(angles.astype(np.float64)).astype(np.float32)
    sine = np.sin(angles.astype(np.float64)).astype(np.float32)
    ct = np.concatenate([cosine, cosine], axis=1)
    st = np.concatenate([-sine, sine], axis=1)
    fr = np.broadcast_to(np.concatenate([freqs, freqs])[None, :], (8, HEAD))
    return ct, st, np.ascontiguousarray(fr)


def dot(a, b):
    return jnp.dot(a, b, preferred_element_type=f32)


def dot_t(a, b):
    return lax.dot_general(a, b, (((1,), (1,)), ((), ())), preferred_element_type=f32)


def kernel(
    plen_in, assign_in, slot_in, clen_in, gain_in, freq_in,
    prompt_ref, dec_ref, ck_ref, cv_ref, wqkv_ref, wout_ref, ct_ref, st_ref,
    out_ref, dout_ref,
    plen_ref, assign_ref, slot_ref, clen_ref, gain_ref, freq_ref,
    xs, wq, wo, ck, cv, acc, ssq, qs, kv, so, sm, at, pb, fr, nr, ct, st, bias,
    xn, dmv, x16, xd, jd, qd, kd, vd, qr, ms, ls, os_, plt, pls, qnew, qn, pks, pk, od, hs, hr, dsb, drb, dfb, o32,
    ring, opened, ssem, lsem, agS, agR, farR, wS, wR, plS, plR, qnS, qnR, pkS, pkR, kvS, kvR, fS, fR, nS, nR, dS, dR,
):
    me = lax.axis_index("blk")
    pool = lax.axis_index("pool")
    batch = lax.axis_index("batch")
    x = me // 2
    c = lax.rem(me, 2)

    def near(dx, dc):
        return {"blk": lax.rem(x + dx + 4, 4) * 2 + lax.rem(c + dc, 2)}

    def other(j):
        return {"pool": 1 - pool, "batch": j}

    def peer(j):
        return {"blk": lax.rem(me + j, 8)}

    def remote(src, dst, ss, rs, dev):
        return pltpu.make_async_remote_copy(
            src_ref=src, dst_ref=dst, send_sem=ss, recv_sem=rs, device_id=dev, device_id_type=MESH
        )

    def arrived(ref, sem):
        remote(ref, ref, sem, sem, near(0, 1)).wait_recv()

    def gone(ref, sem):
        remote(ref, ref, sem, sem, near(0, 1)).wait_send()

    ldec = pltpu.make_async_copy(dec_ref, dmv, lsem.at[0])
    lweights = pltpu.make_async_copy(wqkv_ref, wq.at[0], lsem.at[1])
    ltokens = [
        pltpu.make_async_copy(prompt_ref.at[0, :, pl.ds(q * PIECE, PIECE)], xs.at[0, q], lsem.at[2])
        for q in range(4)
    ]
    lct = pltpu.make_async_copy(ct_ref, ct, lsem.at[3])
    lst = pltpu.make_async_copy(st_ref, st, lsem.at[4])
    lck = pltpu.make_async_copy(ck_ref, ck, lsem.at[5])
    lcv = pltpu.make_async_copy(cv_ref, cv, lsem.at[6])
    lwo = pltpu.make_async_copy(wout_ref, wo.at[0], lsem.at[7])
    local = [ldec, lweights, *ltokens, lct, lst, lck, lcv, lwo]
    small = [
        pltpu.make_async_copy(a, b, ssem.at[i])
        for i, (a, b) in enumerate((
            (plen_in, plen_ref), (assign_in, assign_ref), (slot_in, slot_ref),
            (clen_in, clen_ref), (gain_in, gain_ref), (freq_in, freq_ref),
        ))
    ]
    for cp in small:
        cp.start()
    for cp in local:
        cp.start()

    barrier = pltpu.get_barrier_semaphore()
    gate = me == 0
    for j in range(1, 8):
        @pl.when(lax.rem(me + j, 8) != 0)
        def _(j=j):
            pl.semaphore_signal(barrier, inc=1, device_id=peer(j), device_id_type=MESH)

    kv[:, :, 2 * HEAD:] = jnp.ones((2, STRETCH, HEAD), bf16)

    @pl.when(me != 0)
    def _():
        pl.semaphore_wait(barrier, 7)

    @pl.when(me == 1)
    def _():
        pl.semaphore_signal(ring, inc=1, device_id=peer(7), device_id_type=MESH)

    @pl.when(gate)
    def _():
        pl.semaphore_wait(ring, 1)

    def gather(direction, k):
        q = (k + 2 * direction) % 4
        cols = pl.ds(q * PIECE, PIECE)
        return remote(
            prompt_ref.at[0, :, cols], xs.at[1 + direction, q], agS, agR.at[direction, q], near(1 - 2 * direction, 0)
        )

    def onward(direction, k):
        q = 2 * direction + (k > 0)
        cols = pl.ds(0, PIECE) if k == 0 else pl.ds((k - 1) * (PIECE // 2), PIECE // 2)
        return remote(
            xs.at[1 + direction, q, :, cols], xs.at[3, q, :, cols], agS, farR.at[direction, k],
            near(1 - 2 * direction, 0),
        )

    for k in range(4):
        gather(0, k).start()
        gather(1, k).start()

    remote(wqkv_ref, wq.at[1], wS.at[0], wR.at[0], near(0, 1)).start()
    remote(wout_ref, wo.at[1], wS.at[1], wR.at[1], near(0, 1)).start()

    @pl.when(gate)
    def _():
        for j in range(8):
            pl.semaphore_signal(barrier, inc=1, device_id=other(j), device_id_type=MESH)

    for cp in small:
        cp.wait()
    plt[...] = jnp.full((8, 128), plen_ref[0, 0], jnp.int32)
    col = lax.broadcasted_iota(jnp.int32, (8, STRETCH), 1)
    bias[...] = jnp.where(col < jnp.full((8, STRETCH), plen_ref[0, 0], jnp.int32), 0.0, NEG)

    ldec.wait()
    for s in range(STEPS):
        x16[pl.ds(s * ROWS, ROWS), :] = dmv[s].astype(f32)
    wide = x16[...]
    factor = lax.rsqrt(jnp.mean(wide * wide, axis=-1, keepdims=True) + EPSILON)
    xd[...] = (wide * factor * gain_ref[...]).astype(bf16)
    joined = jnp.zeros((16, QKV), f32)
    lweights.wait()
    for q in range(4):
        joined = joined + dot(xd[:, q * PIECE:(q + 1) * PIECE], wq[0, pl.ds(q * PIECE, PIECE), :])
    jd[...] = joined

    def scaled(slot, q, a, at=0, size=PIECE):
        wide = xs[slot, q, :, pl.ds(at, size)].astype(f32)
        square = wide * wide
        part = square[:, :HEAD]
        for i in range(1, size // HEAD):
            part = part + square[:, i * HEAD:(i + 1) * HEAD]
        ssq[a] += part
        return (wide * gain_ref[:, pl.ds(pl.multiple_of(q * PIECE + at, size), size)]).astype(bf16)

    def project(slot, q, a, at=0, size=PIECE):
        tokens = scaled(slot, q, a, at, size)
        rows = pl.ds(pl.multiple_of(q * PIECE + at, size), size)
        for h in range(2):
            acc[a, h] += dot(tokens, wq[h, rows, :])

    def clear(a):
        acc[a] = jnp.zeros((2, TOK, QKV), f32)
        ssq[a] = jnp.zeros((TOK, HEAD), f32)

    clear(0)
    pltpu.make_async_copy(xs.at[0], xs.at[0], lsem.at[2]).wait()

    def own_first(q, _):
        tokens = scaled(0, q, 0)
        xn[q] = tokens
        acc[0, 0] += dot(tokens, wq[0, pl.ds(pl.multiple_of(q * PIECE, PIECE), PIECE), :])
        return 0

    lax.fori_loop(0, 4, own_first, 0)

    def turn(u, cosine, sine):
        return u * cosine + pltpu.roll(u, HEAD // 2, 1) * sine

    def decode_queries():
        wanted = jnp.full((8, 128), assign_ref[0, 0], jnp.int32)
        newlen = jnp.zeros((8, 128), jnp.int32)
        arrived(pls, plR)
        for j in range(8):
            newlen = newlen + jnp.where(wanted == j, pls[j], 0)
        row = lax.broadcasted_iota(jnp.int32, (16, 128), 0)
        row_r = lax.rem(row, ROWS)
        place = jnp.zeros((16, 128), jnp.int32)
        for r in range(ROWS):
            place = jnp.where(row_r == r, jnp.full((16, 128), clen_ref[r], jnp.int32), place)
        fresh = row_r == jnp.full((16, 128), slot_ref[0, 0], jnp.int32)
        place = jnp.where(fresh, jnp.broadcast_to(newlen[0:1, :], (16, 128)), place) + row // ROWS
        angle = place.astype(f32) * freq_ref[0:1, :]
        lane = lax.broadcasted_iota(jnp.int32, (16, 128), 1)
        dcos = jnp.cos(angle)
        dsin = jnp.sin(angle)
        dsin = jnp.where(lane < HEAD // 2, -dsin, dsin)

        for h in range(GROUP):
            qd[pl.ds(h * 16, 16), :] = turn(jd[:, h * HEAD:(h + 1) * HEAD], dcos, dsin)
        kd[...] = turn(jd[:, GROUP * HEAD:(GROUP + 1) * HEAD], dcos, dsin).astype(bf16)
        vd[...] = jd[:, (GROUP + 1) * HEAD:].astype(bf16)
        slots = jnp.full((16, 128), slot_ref[0, 0], jnp.int32)
        picked = jnp.zeros((16, 128), f32)
        for r in range(ROWS):
            part = qd[pl.ds(r, 16, stride=ROWS), :]
            qr[r] = part.astype(bf16)
            picked = picked + jnp.where(slots == r, part, 0.0)
        qnew[...] = picked.astype(bf16)

    def origin(slot):
        if isinstance(slot, int):
            return lax.rem(x + (0, 3, 1, 2)[slot], 4)
        return lax.rem(x + jnp.where(slot == 1, 3, jnp.where(slot == 2, 1, jnp.where(slot == 3, 2, 0))), 4)

    def exchange(slot, h):
        rows = pl.ds(pl.multiple_of((origin(slot) * 2 + c) * TOK, TOK), TOK)
        cols = pl.ds(0, 2 * HEAD)
        return remote(kv.at[h, rows, cols], kv.at[1 - h, rows, cols], kvS, kvR.at[slot // 3], near(0, 1))

    def finish(slot, a):
        rows = pl.ds(pl.multiple_of((origin(slot) * 2 + c) * TOK, TOK), TOK)
        factor = lax.rsqrt(jnp.sum(ssq[a], axis=-1, keepdims=True) * (1.0 / D) + EPSILON)
        cosine = ct[rows, :] * factor
        sine = st[rows, :] * factor
        for h in range(2):
            kv[h, rows, :HEAD] = turn(acc[a, h, :, GROUP * HEAD:(GROUP + 1) * HEAD], cosine, sine).astype(bf16)
            kv[h, rows, HEAD:2 * HEAD] = (acc[a, h, :, (GROUP + 1) * HEAD:] * factor).astype(bf16)
        for h in range(2):
            for g in range(GROUP):
                qs[slot, h * GROUP + g] = turn(acc[a, h, :, g * HEAD:(g + 1) * HEAD], cosine, sine).astype(bf16)
            exchange(slot, h).start()

    def old_row(r):
        q16 = qr[r]
        edge = jnp.full((16, CACHE), clen_ref[r], jnp.int32)
        edge = jnp.where(jnp.full((16, CACHE), slot_ref[0, 0], jnp.int32) == r, 0, edge)
        span = lax.broadcasted_iota(jnp.int32, (16, CACHE), 1)
        old = jnp.where(span < edge, dot_t(q16, ck[r]) * SCALE2, NEG)
        own = dot_t(q16, kd[...]) * SCALE2
        i16 = lax.broadcasted_iota(jnp.int32, (16, 16), 0)
        j16 = lax.broadcasted_iota(jnp.int32, (16, 16), 1)
        keep = (lax.rem(j16, ROWS) == r) & (j16 // ROWS <= lax.rem(i16, STEPS))
        own = jnp.where(keep, own, NEG)
        top = jnp.maximum(jnp.max(old, axis=-1, keepdims=True), jnp.max(own, axis=-1, keepdims=True))
        pold = jnp.exp2(old - top)
        pown = jnp.exp2(own - top)
        total = jnp.sum(pold, axis=-1, keepdims=True) + jnp.sum(pown, axis=-1, keepdims=True)
        mixed = dot(pold.astype(bf16), cv[r]) + dot(pown.astype(bf16), vd[...])
        ms[r] = jnp.broadcast_to(top, (16, 128))
        ls[r] = jnp.broadcast_to(total, (16, 128))
        os_[r] = mixed

    def query(j):
        return remote(qnew, qn.at[batch], qnS, qnR, other(j))

    @pl.when(gate)
    def _():
        pl.semaphore_wait(barrier, 8)
        for j in range(1, 8):
            pl.semaphore_signal(opened, inc=1, device_id=peer(j), device_id_type=MESH)

    @pl.when(me != 0)
    def _():
        pl.semaphore_wait(opened, 1)

    def length(j):
        return remote(plt, pls.at[batch], plS, plR, other(j))

    for j in range(8):
        length(j).start()

    arrived(wq.at[1], wR.at[0])
    lct.wait()
    lst.wait()

    def own_second(q, _):
        acc[0, 1] += dot(xn[q], wq[1, pl.ds(pl.multiple_of(q * PIECE, PIECE), PIECE), :])
        return 0

    lax.fori_loop(0, 4, own_second, 0)
    finish(0, 0)

    clear(0)
    clear(1)
    lck.wait()
    lcv.wait()

    def near_step(t, _):
        q1 = t
        q2 = lax.rem(t + 2, 4)
        arrived(xs.at[1, q1], agR.at[0, q1])
        arrived(xs.at[2, q2], agR.at[1, q2])

        @pl.when(t == 0)
        def _():
            onward(0, 0).start()
            onward(1, 0).start()

        @pl.when(t == 1)
        def _():
            for k in (1, 2):
                onward(0, k).start()
                onward(1, k).start()

        project(1, q1, 0)
        project(2, q2, 1)

        @pl.when(t == 1)
        def _():
            decode_queries()
            for j in range(2):
                old_row(j)
            for j in range(8):
                query(j).start()
            for j in range(2, 4):
                old_row(j)

        return 0

    lax.fori_loop(0, 4, near_step, 0)
    finish(1, 0)
    finish(2, 1)

    def attend_own(d):
        krows = pl.ds(pl.multiple_of(origin(d) * 256, 256), 256)
        qi = lax.rem(lax.broadcasted_iota(jnp.int32, (2 * TOK, 256), 0), TOK) + c * TOK
        ki = lax.broadcasted_iota(jnp.int32, (2 * TOK, 256), 1)
        mask = jnp.where(ki <= qi, jnp.broadcast_to(bias[0:1, krows], (2 * TOK, 256)), NEG)
        for hp in range(4):
            q2 = qs[d, 2 * hp:2 * hp + 2].reshape(2 * TOK, HEAD)
            h = hp // 2
            s = dot_t(q2, kv[h, krows, :HEAD]) * SCALE2 + mask
            top = jnp.max(s, axis=-1, keepdims=True)
            p = jnp.exp2(s - top)
            sm[d, hp] = jnp.broadcast_to(top, (2 * TOK, HEAD))
            so[d, hp] = dot(p.astype(bf16), kv[h, krows, HEAD:])

    def attend_more(d, k):
        krows = pl.ds(pl.multiple_of(origin(k) * 256, 256), 256)

        @pl.when(origin(k) < origin(d))
        def _():
            for hp in range(4):
                q2 = qs[d, 2 * hp:2 * hp + 2].reshape(2 * TOK, HEAD)
                h = hp // 2
                s = dot_t(q2, kv[h, krows, :HEAD]) * SCALE2 + bias[0:1, krows]
                before = sm[d, hp]
                top = jnp.maximum(before, jnp.broadcast_to(jnp.max(s, axis=-1, keepdims=True), (2 * TOK, HEAD)))
                p = jnp.exp2(s - jnp.concatenate([top, top], axis=1))
                fade = jnp.exp2(before - top)
                sm[d, hp] = top
                so[d, hp] = so[d, hp] * jnp.concatenate([fade, fade], axis=1) + dot(p.astype(bf16), kv[h, krows, HEAD:])

    def attend_near(d):
        attend_own(d)

        def others(i, _):
            attend_more(d, lax.rem(d + i, 3))
            return 0

        lax.fori_loop(1, 3, others, 0)

    def settle(d):
        for hp in range(4):
            o = (so[d, hp, :, :HEAD] / so[d, hp, :, HEAD:]).astype(bf16)
            at[d, :, hp * 256:hp * 256 + HEAD] = o[:TOK]
            at[d, :, hp * 256 + HEAD:(hp + 1) * 256] = o[TOK:]

    arrived(kv.at[0, pl.ds(0, 6 * TOK), pl.ds(0, 2 * HEAD)], kvR.at[0])

    def before_far(i, _):
        attend_near(lax.rem(i + 1, 3))
        return 0

    lax.fori_loop(0, 3, before_far, 0)

    clear(0)

    for direction in range(2):
        arrived(xs.at[3, 2 * direction], farR.at[direction, 0])
        project(3, 2 * direction, 0)
    for k in range(2):
        for direction in range(2):
            q = 2 * direction + 1
            half = PIECE // 2
            arrived(xs.at[3, q, :, pl.ds(k * half, half)], farR.at[direction, 1 + k])
            project(3, q, 0, k * half, half)
    finish(3, 0)
    lwo.wait()
    arrived(wo.at[1], wR.at[1])
    arrived(kv.at[0, pl.ds(0, 2 * TOK), pl.ds(0, 2 * HEAD)], kvR.at[1])

    def out_piece(d, q):
        cols = pl.ds(pl.multiple_of(q * PIECE, PIECE), PIECE)
        part = dot(at[d, :, :512], wo[0, :, cols]) + dot(at[d, :, 512:], wo[1, :, cols])
        pb[d, q] = part.astype(bf16)

    def far_send(q):
        if q < 2:
            return remote(pb.at[3, q], fr.at[0, q], fS, fR.at[0, q], near(1, 0))
        return remote(pb.at[3, q], fr.at[1, q - 2], fS, fR.at[1, q - 2], near(-1, 0))

    def near_send(direction, q):
        return remote(
            pb.at[2 - direction, q], nr.at[direction, q], nS, nR.at[direction, q],
            near(1 - 2 * direction, 0),
        )

    def answer():
        arrived(qn, qnR)
        q = qn[...].reshape(8 * 16, HEAD)
        s = dot_t(q, kv[0, :, :HEAD]) * SCALE2 + bias[0:1, :]
        top = jnp.max(s, axis=-1, keepdims=True)
        p = jnp.exp2(s - top)
        o = dot(p.astype(bf16), kv[0, :, HEAD:])
        pks[:, 0] = o[:, :HEAD].reshape(8, 16, HEAD)
        pks[:, 1] = jnp.broadcast_to(top, (128, HEAD)).reshape(8, 16, HEAD)
        pks[:, 2] = o[:, HEAD:].reshape(8, 16, HEAD)

    def reply(j):
        return remote(pks.at[j], pk.at[batch], pkS, pkR, other(j))

    def pieces(d, first, second):
        def piece(k, _):
            out_piece(d, jnp.where(k == 0, first, second))
            return 0

        lax.fori_loop(0, 2, piece, 0)

    attend_more(2, 3)
    settle(2)
    out_piece(2, 2)
    near_send(0, 2).start()
    attend_more(1, 3)
    settle(1)
    out_piece(1, 0)
    near_send(1, 0).start()
    out_piece(2, 3)
    near_send(0, 3).start()
    out_piece(1, 1)
    near_send(1, 1).start()
    answer()

    attend_own(3)
    for j in range(8):
        reply(j).start()

    def far_keys(k, _):
        attend_more(3, k)
        return 0

    lax.fori_loop(0, 3, far_keys, 0)
    settle(3)
    pieces(3, 0, 2)
    far_send(0).start()
    far_send(2).start()
    pieces(3, 1, 3)
    pieces(2, 0, 1)
    pieces(1, 2, 3)
    arrived(pk, pkR)
    want = jnp.full((16, 128), assign_ref[0, 0], jnp.int32)
    no = jnp.zeros((16, 128), f32)
    nm = jnp.zeros((16, 128), f32)
    nl = jnp.zeros((16, 128), f32)
    for j in range(8):
        hit = want == j
        no = no + jnp.where(hit, pk[j, 0], 0.0)
        nm = nm + jnp.where(hit, pk[j, 1], 0.0)
        nl = nl + jnp.where(hit, pk[j, 2], 0.0)
    slots = jnp.full((16, 128), slot_ref[0, 0], jnp.int32)
    for r in range(ROWS):
        mine = slots == r
        m2 = jnp.where(mine, nm, NEG)
        top = jnp.maximum(ms[r], m2)
        a = jnp.exp2(ms[r] - top)
        b = jnp.exp2(m2 - top)
        o = (os_[r] * a + no * b) / (ls[r] * a + nl * b)
        od[pl.ds(r, 16, stride=ROWS), :] = o
    part = jnp.zeros((16, D), f32)
    for h in range(GROUP):
        part = part + dot(od[pl.ds(h * 16, 16), :].astype(bf16), wo[0, pl.ds(h * HEAD, HEAD), :])
    o32[...] = part

    def half_cols(core):
        return pl.ds(pl.multiple_of(core * (D // 2), D // 2), D // 2)

    def chip_cols(core, chip):
        return pl.ds(pl.multiple_of(core * (D // 2) + chip * 512, 512), 512)

    hs[...] = o32[:, half_cols(1 - c)].astype(bf16)
    attend_more(0, 3)
    settle(0)
    remote(hs, hr, dS.at[0], dR.at[0], near(0, 1)).start()
    pieces(0, 0, 2)
    arrived(hr, dR.at[0])
    o32[:, half_cols(c)] = o32[:, half_cols(c)] + hr[...].astype(f32)
    for k in range(4):
        dsb[k] = o32[:, chip_cols(c, lax.rem(x + k, 4))].astype(bf16)
    for k in range(1, 4):
        remote(dsb.at[k], drb.at[k - 1], dS.at[1], dR.at[1], near(k, 0)).start()
    far_send(1).start()
    far_send(3).start()

    pieces(0, 1, 3)

    def relay(q):
        arrived(fr.at[0, q], fR.at[0, q])
        pb[2, q] = (pb[2, q].astype(f32) + fr[0, q].astype(f32)).astype(bf16)
        arrived(fr.at[1, q], fR.at[1, q])
        pb[1, q + 2] = (pb[1, q + 2].astype(f32) + fr[1, q].astype(f32)).astype(bf16)
        near_send(0, q).start()
        near_send(1, q + 2).start()

    relay(0)
    arrived(drb, dR.at[1])
    total = o32[:, chip_cols(c, x)]
    for k in range(3):
        total = total + drb[k].astype(f32)
    dfb[0, 0] = (x16[:, chip_cols(c, x)] + total).astype(bf16)
    for k in range(1, 4):
        remote(dfb.at[0, 0], dfb.at[0, k], dS.at[2], dR.at[2], near(k, 0)).start()
    relay(1)
    arrived(dfb.at[0, pl.ds(1, 3)], dR.at[2])
    remote(dfb.at[0], dfb.at[1], dS.at[3], dR.at[3], near(0, 1)).start()
    arrived(dfb.at[1], dR.at[3])
    for core in range(2):
        for k in range(4):
            o32[:, chip_cols(lax.rem(c + core, 2), lax.rem(x - k + 4, 4))] = dfb[core, k].astype(f32)
    dout_ref[...] = o32[...].astype(bf16)

    for i, q in enumerate((0, 2, 1, 3)):
        arrived(nr.at[0, q], nR.at[0, q])
        arrived(nr.at[1, q], nR.at[1, q])
        cols = slice(q * PIECE, (q + 1) * PIECE)
        total = pb[0, q].astype(f32) + nr[0, q].astype(f32) + nr[1, q].astype(f32)
        out_ref[:, cols] = (xs[0, q].astype(f32) + total).astype(bf16)

    gone(xs.at[pl.ds(0, 3)], agS)
    gone(wq.at[0], wS.at[0])
    gone(wo.at[0], wS.at[1])
    gone(pls, plS)
    gone(qn, qnS)
    gone(pk, pkS)
    gone(kv.at[0, :, pl.ds(0, 2 * HEAD)], kvS)
    gone(pb.at[3], fS)
    gone(pb.at[pl.ds(1, 2)], nS)
    gone(hr, dS.at[0])
    gone(drb, dS.at[1])
    gone(drb, dS.at[2])
    gone(dfb.at[0], dS.at[3])


def body(
    prompt, prompt_len, dec_tokens, cache_k, cache_v, cache_len, assign, slot, gain, w_qkv, w_out
):
    ct, st, fr = tables()
    any_ = pl.BlockSpec(memory_space=pl.ANY)
    vmem = pl.BlockSpec(memory_space=pltpu.VMEM)
    V = pltpu.VMEM
    dma = pltpu.SemaphoreType.DMA
    OUT = pltpu.VMEM
    out, dout = pl.pallas_call(
        kernel,
        out_shape=(
            OUT((TOK, D), bf16),
            OUT((16, D), bf16),
        ),
        in_specs=[any_] * 14,
        out_specs=(vmem, vmem),
        scratch_shapes=[
            pltpu.SMEM((1, 1), jnp.int32),
            pltpu.SMEM((1, 1), jnp.int32),
            pltpu.SMEM((1, 1), jnp.int32),
            pltpu.SMEM((ROWS,), jnp.int32),
            V((1, D), f32),
            V((8, HEAD), f32),
            V((4, 4, TOK, PIECE), bf16),
            V((2, D, QKV), bf16),
            V((2, 512, D), bf16),
            V((ROWS, CACHE, HEAD), bf16),
            V((ROWS, CACHE, HEAD), bf16),
            V((2, 2, TOK, QKV), f32),
            V((2, TOK, HEAD), f32),
            V((4, 8, TOK, HEAD), bf16),
            V((2, STRETCH, 3 * HEAD), bf16),
            V((4, 4, 2 * TOK, 2 * HEAD), f32),
            V((4, 4, 2 * TOK, HEAD), f32),
            V((4, TOK, 1024), bf16),
            V((4, 4, TOK, PIECE), bf16),
            V((2, 2, TOK, PIECE), bf16),
            V((2, 4, TOK, PIECE), bf16),
            V((STRETCH, HEAD), f32),
            V((STRETCH, HEAD), f32),
            V((8, STRETCH), f32),
            V((4, TOK, PIECE), bf16),
            V((STEPS, ROWS, D), bf16),
            V((16, D), f32),
            V((16, D), bf16),
            V((16, QKV), f32),
            V((64, HEAD), f32),
            V((16, HEAD), bf16),
            V((16, HEAD), bf16),
            V((ROWS, 16, HEAD), bf16),
            V((ROWS, 16, HEAD), f32),
            V((ROWS, 16, HEAD), f32),
            V((ROWS, 16, HEAD), f32),
            V((8, 128), jnp.int32),
            V((8, 8, 128), jnp.int32),
            V((16, HEAD), bf16),
            V((8, 16, HEAD), bf16),
            V((8, 3, 16, HEAD), f32),
            V((8, 3, 16, HEAD), f32),
            V((64, HEAD), f32),
            V((16, D // 2), bf16),
            V((16, D // 2), bf16),
            V((4, 16, 512), bf16),
            V((3, 16, 512), bf16),
            V((2, 4, 16, 512), bf16),
            V((16, D), f32),
            pltpu.SemaphoreType.REGULAR,
            pltpu.SemaphoreType.REGULAR,
            dma((6,)), dma((8,)),
            dma, dma((2, 4)), dma((2, 3)),
            dma((2,)), dma((2,)),
            dma, dma, dma, dma, dma, dma,
            dma, dma((2,)),
            dma, dma((2, 2)),
            dma, dma((2, 4)),
            dma((4,)), dma((4,)),
        ],
        compiler_params=pltpu.CompilerParams(
            collective_id=0, has_side_effects=True, vmem_limit_bytes=59 * 2**20
        ),
        name="layer",
    )(
        prompt_len, assign, slot, cache_len, gain.reshape(1, D), jnp.asarray(fr),
        prompt, dec_tokens, cache_k, cache_v, w_qkv, w_out, jnp.asarray(ct), jnp.asarray(st),
    )
    return pl.pallas_call(
        writer,
        out_shape=(
            jax.ShapeDtypeStruct((1, TOK, D), bf16),
            jax.ShapeDtypeStruct((STEPS, ROWS, D), bf16),
        ),
        in_specs=[vmem, vmem],
        out_specs=(any_, any_),
        scratch_shapes=[V((STEPS, ROWS, D), bf16), dma((5,))],
        compiler_params=pltpu.CompilerParams(vmem_limit_bytes=8 * 2**20),
        name="write",
    )(out, dout)


def writer(out_ref, dout_ref, full_ref, dec_ref, stage, sem):
    copies = []
    for q in range(4):
        rows = pl.ds(q * 32, 32)
        copies.append(pltpu.make_async_copy(out_ref.at[rows], full_ref.at[0, rows], sem.at[q]))
        copies[q].start()
    for s in range(STEPS):
        stage[s] = dout_ref[pl.ds(s * ROWS, ROWS), :]
    copies.append(pltpu.make_async_copy(stage, dec_ref, sem.at[4]))
    copies[4].start()
    for cp in copies:
        cp.wait()


def solution(mesh):
    return jax.shard_map(
        body,
        mesh=mesh,
        in_specs=(
            P(("pool", "batch"), "blk", None),
            P("pool", "batch"),
            P(None, ("pool", "batch"), None),
            P(("pool", "batch"), None, "blk"),
            P(("pool", "batch"), None, "blk"),
            P(("pool", "batch")),
            P("pool", "batch"),
            P("pool", "batch"),
            P(),
            P(None, "blk"),
            P("blk", None),
        ),
        out_specs=(P(("pool", "batch"), "blk", None), P(None, ("pool", "batch"), None)),
        check_vma=False,
    )
```

```python
import functools

import jax
import jax.numpy as jnp
import numpy as np
from jax import lax
from jax.experimental import pallas as pl
from jax.experimental.pallas import tpu as pltpu
from jax.sharding import PartitionSpec as P

MESH = pl.DeviceIdType.MESH
HEAD = 128
GROUP = 4
D = 4096
TOK = 128
STRETCH = 1024
CACHE = 4096
STEPS = 4
ROWS = 4
QKV = (GROUP + 2) * HEAD
PIECE = 1024
PARTS = ((0, 1024), (0, 512), (512, 256), (768, 256))
EPSILON = 1e-05
THETA = 500000.0
NEG = -1e30
SCALE2 = float(HEAD ** (-0.5) * np.log2(np.e))

f32 = jnp.float32
bf16 = jnp.bfloat16


def tables():
    half = HEAD // 2
    freqs = (THETA ** (-np.arange(half, dtype=np.float64) / half)).astype(np.float32)
    angles = np.arange(STRETCH, dtype=np.float32)[:, None] * freqs
    cosine = np.cos(angles.astype(np.float64)).astype(np.float32)
    sine = np.sin(angles.astype(np.float64)).astype(np.float32)
    ct = np.concatenate([cosine, cosine], axis=1)
    st = np.concatenate([-sine, sine], axis=1)
    fr = np.broadcast_to(np.concatenate([freqs, freqs])[None, :], (8, HEAD))
    return ct, st, np.ascontiguousarray(fr)


def dot(a, b):
    return jnp.dot(a, b, preferred_element_type=f32)


def dot_t(a, b):
    return lax.dot_general(a, b, (((1,), (1,)), ((), ())), preferred_element_type=f32)


def kernel(
    plen_in, assign_in, slot_in, clen_in, gain_in, freq_in,
    prompt_ref, dec_ref, ck_ref, cv_ref, wqkv_ref, wout_ref, ct_ref, st_ref,
    out_ref, dout_ref,
    plen_ref, assign_ref, slot_ref, clen_ref, gain_ref, freq_ref,
    xs, wq, wo, ck, cv, acc, ssq, qs, kv, so, sm, at, pb, fr, nr, ct, st, bias,
    xn, dmv, x16, xd, jd, qd, kd, vd, qr, ms, ls, os_, plt, pls, qnew, qn, pks, pk, od, hs, hr, dsb, drb, dfb, o32,
    ring, opened, ssem, lsem, agS, agR, farR, wS, wR, plS, plR, qnS, qnR, pkS, pkR, kvS, kvR, fS, fR, nS, nR, dS, dR,
):
    me = lax.axis_index("blk")
    pool = lax.axis_index("pool")
    batch = lax.axis_index("batch")
    x = me // 2
    c = lax.rem(me, 2)

    def near(dx, dc):
        return {"blk": lax.rem(x + dx + 4, 4) * 2 + lax.rem(c + dc, 2)}

    def other(j):
        return {"pool": 1 - pool, "batch": j}

    def peer(j):
        return {"blk": lax.rem(me + j, 8)}

    def remote(src, dst, ss, rs, dev):
        return pltpu.make_async_remote_copy(
            src_ref=src, dst_ref=dst, send_sem=ss, recv_sem=rs, device_id=dev, device_id_type=MESH
        )

    def arrived(ref, sem):
        remote(ref, ref, sem, sem, near(0, 1)).wait_recv()

    def gone(ref, sem):
        remote(ref, ref, sem, sem, near(0, 1)).wait_send()

    ldec = pltpu.make_async_copy(dec_ref, dmv, lsem.at[0])
    lweights = pltpu.make_async_copy(wqkv_ref, wq.at[0], lsem.at[1])
    ltokens = [
        pltpu.make_async_copy(prompt_ref.at[0, :, pl.ds(q * PIECE, PIECE)], xs.at[0, q], lsem.at[2])
        for q in range(4)
    ]
    lct = pltpu.make_async_copy(ct_ref, ct, lsem.at[3])
    lst = pltpu.make_async_copy(st_ref, st, lsem.at[4])
    lck = pltpu.make_async_copy(ck_ref, ck, lsem.at[5])
    lcv = pltpu.make_async_copy(cv_ref, cv, lsem.at[6])
    lwo = pltpu.make_async_copy(wout_ref, wo.at[0], lsem.at[7])
    local = [*ltokens, ldec, lweights, lct, lst, lck, lcv, lwo]
    small = [
        pltpu.make_async_copy(a, b, ssem.at[i])
        for i, (a, b) in enumerate((
            (plen_in, plen_ref), (assign_in, assign_ref), (slot_in, slot_ref),
            (clen_in, clen_ref), (gain_in, gain_ref), (freq_in, freq_ref),
        ))
    ]
    for cp in local[:4]:
        cp.start()
    for cp in small:
        cp.start()
    for cp in local[4:]:
        cp.start()

    barrier = pltpu.get_barrier_semaphore()
    gate = me == 0
    for j in range(1, 8):
        @pl.when(lax.rem(me + j, 8) != 0)
        def _(j=j):
            pl.semaphore_signal(barrier, inc=1, device_id=peer(j), device_id_type=MESH)

    kv[:, :, 2 * HEAD:] = jnp.ones((2, STRETCH, HEAD), bf16)

    @pl.when(me != 0)
    def _():
        pl.semaphore_wait(barrier, 7)

    @pl.when(me == 1)
    def _():
        pl.semaphore_signal(ring, inc=1, device_id=peer(7), device_id_type=MESH)

    @pl.when(gate)
    def _():
        pl.semaphore_wait(ring, 1)

    def gather(direction, k):
        q = (k + 2 * direction) % 4
        cols = pl.ds(q * PIECE, PIECE)
        src = prompt_ref.at[0, :, cols] if k == 0 else xs.at[0, q]
        return remote(src, xs.at[1 + direction, q], agS, agR.at[direction, q], near(1 - 2 * direction, 0))

    def onward(direction, k):
        q = 2 * direction + (k > 0)
        cols = pl.ds(*PARTS[k])
        return remote(
            xs.at[1 + direction, q, :, cols], xs.at[3, q, :, cols], agS, farR.at[direction, k],
            near(1 - 2 * direction, 0),
        )

    for k in range(4):
        if k == 1:
            pltpu.make_async_copy(xs.at[0], xs.at[0], lsem.at[2]).wait()
        gather(0, k).start()
        gather(1, k).start()

    remote(wqkv_ref, wq.at[1], wS.at[0], wR.at[0], near(0, 1)).start()
    remote(wout_ref, wo.at[1], wS.at[1], wR.at[1], near(0, 1)).start()

    @pl.when(gate)
    def _():
        for j in range(8):
            pl.semaphore_signal(barrier, inc=1, device_id=other(j), device_id_type=MESH)

    for cp in small:
        cp.wait()
    plt[...] = jnp.full((8, 128), plen_ref[0, 0], jnp.int32)
    col = lax.broadcasted_iota(jnp.int32, (8, STRETCH), 1)
    bias[...] = jnp.where(col < jnp.full((8, STRETCH), plen_ref[0, 0], jnp.int32), 0.0, NEG)

    ldec.wait()
    for s in range(STEPS):
        x16[pl.ds(s * ROWS, ROWS), :] = dmv[s].astype(f32)
    wide = x16[...]
    factor = lax.rsqrt(jnp.mean(wide * wide, axis=-1, keepdims=True) + EPSILON)
    xd[...] = (wide * factor * gain_ref[...]).astype(bf16)
    joined = jnp.zeros((16, QKV), f32)
    lweights.wait()
    for q in range(4):
        joined = joined + dot(xd[:, q * PIECE:(q + 1) * PIECE], wq[0, pl.ds(q * PIECE, PIECE), :])
    jd[...] = joined

    def scaled(slot, q, a, at=0, size=PIECE):
        wide = xs[slot, q, :, pl.ds(at, size)].astype(f32)
        square = wide * wide
        part = square[:, :HEAD]
        for i in range(1, size // HEAD):
            part = part + square[:, i * HEAD:(i + 1) * HEAD]
        ssq[a] += part
        return (wide * gain_ref[:, pl.ds(pl.multiple_of(q * PIECE + at, size), size)]).astype(bf16)

    def project(slot, q, a, at=0, size=PIECE):
        tokens = scaled(slot, q, a, at, size)
        rows = pl.ds(pl.multiple_of(q * PIECE + at, size), size)
        for h in range(2):
            acc[a, h] += dot(tokens, wq[h, rows, :])

    def clear(a):
        acc[a] = jnp.zeros((2, TOK, QKV), f32)
        ssq[a] = jnp.zeros((TOK, HEAD), f32)

    clear(0)

    def own_first(q, _):
        tokens = scaled(0, q, 0)
        xn[q] = tokens
        acc[0, 0] += dot(tokens, wq[0, pl.ds(pl.multiple_of(q * PIECE, PIECE), PIECE), :])
        return 0

    lax.fori_loop(0, 4, own_first, 0)

    def turn(u, cosine, sine):
        return u * cosine + pltpu.roll(u, HEAD // 2, 1) * sine

    def decode_queries():
        wanted = jnp.full((8, 128), assign_ref[0, 0], jnp.int32)
        newlen = jnp.zeros((8, 128), jnp.int32)
        arrived(pls, plR)
        for j in range(8):
            newlen = newlen + jnp.where(wanted == j, pls[j], 0)
        row = lax.broadcasted_iota(jnp.int32, (16, 128), 0)
        row_r = lax.rem(row, ROWS)
        place = jnp.zeros((16, 128), jnp.int32)
        for r in range(ROWS):
            place = jnp.where(row_r == r, jnp.full((16, 128), clen_ref[r], jnp.int32), place)
        fresh = row_r == jnp.full((16, 128), slot_ref[0, 0], jnp.int32)
        place = jnp.where(fresh, jnp.broadcast_to(newlen[0:1, :], (16, 128)), place) + row // ROWS
        angle = place.astype(f32) * freq_ref[0:1, :]
        lane = lax.broadcasted_iota(jnp.int32, (16, 128), 1)
        dcos = jnp.cos(angle)
        dsin = jnp.sin(angle)
        dsin = jnp.where(lane < HEAD // 2, -dsin, dsin)

        for h in range(GROUP):
            qd[pl.ds(h * 16, 16), :] = turn(jd[:, h * HEAD:(h + 1) * HEAD], dcos, dsin)
        kd[...] = turn(jd[:, GROUP * HEAD:(GROUP + 1) * HEAD], dcos, dsin).astype(bf16)
        vd[...] = jd[:, (GROUP + 1) * HEAD:].astype(bf16)
        slots = jnp.full((16, 128), slot_ref[0, 0], jnp.int32)
        picked = jnp.zeros((16, 128), f32)
        for r in range(ROWS):
            part = qd[pl.ds(r, 16, stride=ROWS), :]
            qr[r] = part.astype(bf16)
            picked = picked + jnp.where(slots == r, part, 0.0)
        qnew[...] = picked.astype(bf16)

    def origin(slot):
        if isinstance(slot, int):
            return lax.rem(x + (0, 3, 1, 2)[slot], 4)
        return lax.rem(x + jnp.where(slot == 1, 3, jnp.where(slot == 2, 1, jnp.where(slot == 3, 2, 0))), 4)

    def exchange(slot, h):
        rows = pl.ds(pl.multiple_of((origin(slot) * 2 + c) * TOK, TOK), TOK)
        cols = pl.ds(0, 2 * HEAD)
        return remote(kv.at[h, rows, cols], kv.at[1 - h, rows, cols], kvS, kvR.at[slot // 3], near(0, 1))

    def factors(slot, a):
        rows = pl.ds(pl.multiple_of((origin(slot) * 2 + c) * TOK, TOK), TOK)
        factor = lax.rsqrt(jnp.sum(ssq[a], axis=-1, keepdims=True) * (1.0 / D) + EPSILON)
        return rows, factor, ct[rows, :] * factor, st[rows, :] * factor

    def finish_query(slot, a, h, cosine, sine):
        for g in range(GROUP):
            qs[slot, h * GROUP + g] = turn(acc[a, h, :, g * HEAD:(g + 1) * HEAD], cosine, sine).astype(bf16)

    def finish_keys(slot, a):
        rows, factor, cosine, sine = factors(slot, a)
        for h in range(2):
            kv[h, rows, :HEAD] = turn(acc[a, h, :, GROUP * HEAD:(GROUP + 1) * HEAD], cosine, sine).astype(bf16)
            kv[h, rows, HEAD:2 * HEAD] = (acc[a, h, :, (GROUP + 1) * HEAD:] * factor).astype(bf16)
        exchange(slot, 0).start()
        qs[slot, 0] = turn(acc[a, 0, :, :HEAD], cosine, sine).astype(bf16)
        exchange(slot, 1).start()

    def finish(slot, a):
        finish_keys(slot, a)
        rows, factor, cosine, sine = factors(slot, a)
        for h in range(2):
            finish_query(slot, a, h, cosine, sine)

    def old_row(r):
        q16 = qr[r]
        edge = jnp.full((16, CACHE), clen_ref[r], jnp.int32)
        edge = jnp.where(jnp.full((16, CACHE), slot_ref[0, 0], jnp.int32) == r, 0, edge)
        span = lax.broadcasted_iota(jnp.int32, (16, CACHE), 1)
        old = jnp.where(span < edge, dot_t(q16, ck[r]) * SCALE2, NEG)
        own = dot_t(q16, kd[...]) * SCALE2
        i16 = lax.broadcasted_iota(jnp.int32, (16, 16), 0)
        j16 = lax.broadcasted_iota(jnp.int32, (16, 16), 1)
        keep = (lax.rem(j16, ROWS) == r) & (j16 // ROWS <= lax.rem(i16, STEPS))
        own = jnp.where(keep, own, NEG)
        top = jnp.maximum(jnp.max(old, axis=-1, keepdims=True), jnp.max(own, axis=-1, keepdims=True))
        pold = jnp.exp2(old - top)
        pown = jnp.exp2(own - top)
        total = jnp.sum(pold, axis=-1, keepdims=True) + jnp.sum(pown, axis=-1, keepdims=True)
        mixed = dot(pold.astype(bf16), cv[r]) + dot(pown.astype(bf16), vd[...])
        ms[r] = jnp.broadcast_to(top, (16, 128))
        ls[r] = jnp.broadcast_to(total, (16, 128))
        os_[r] = mixed

    def query(j):
        return remote(qnew, qn.at[batch], qnS, qnR, other(j))

    @pl.when(gate)
    def _():
        pl.semaphore_wait(barrier, 8)
        for j in range(1, 8):
            pl.semaphore_signal(opened, inc=1, device_id=peer(j), device_id_type=MESH)

    @pl.when(me != 0)
    def _():
        pl.semaphore_wait(opened, 1)

    def length(j):
        return remote(plt, pls.at[batch], plS, plR, other(j))

    for j in range(8):
        length(j).start()

    arrived(wq.at[1], wR.at[0])
    lct.wait()
    lst.wait()

    def own_second(q, _):
        acc[0, 1] += dot(xn[q], wq[1, pl.ds(pl.multiple_of(q * PIECE, PIECE), PIECE), :])
        return 0

    lax.fori_loop(0, 4, own_second, 0)
    finish(0, 0)

    clear(0)
    clear(1)
    lck.wait()
    lcv.wait()

    def near_step(t, _):
        q1 = t
        q2 = lax.rem(t + 2, 4)
        arrived(xs.at[1, q1], agR.at[0, q1])
        arrived(xs.at[2, q2], agR.at[1, q2])

        @pl.when(t == 0)
        def _():
            onward(0, 0).start()
            onward(1, 0).start()

        @pl.when(t == 1)
        def _():
            for k in (1, 2, 3):
                onward(0, k).start()
                onward(1, k).start()

        project(1, q1, 0)
        project(2, q2, 1)

        @pl.when(t == 1)
        def _():
            decode_queries()
            for j in range(2):
                old_row(j)
            for j in range(8):
                query(j).start()
            for j in range(2, 4):
                old_row(j)

        return 0

    lax.fori_loop(0, 4, near_step, 0)
    finish(1, 0)
    finish(2, 1)

    def attend_own(d):
        krows = pl.ds(pl.multiple_of(origin(d) * 256, 256), 256)
        qi = lax.rem(lax.broadcasted_iota(jnp.int32, (2 * TOK, 256), 0), TOK) + c * TOK
        ki = lax.broadcasted_iota(jnp.int32, (2 * TOK, 256), 1)
        mask = jnp.where(ki <= qi, jnp.broadcast_to(bias[0:1, krows], (2 * TOK, 256)), NEG)
        for hp in range(4):
            q2 = qs[d, 2 * hp:2 * hp + 2].reshape(2 * TOK, HEAD)
            h = hp // 2
            s = dot_t(q2, kv[h, krows, :HEAD]) * SCALE2 + mask
            top = jnp.max(s, axis=-1, keepdims=True)
            p = jnp.exp2(s - top)
            sm[d, hp] = jnp.broadcast_to(top, (2 * TOK, HEAD))
            so[d, hp] = dot(p.astype(bf16), kv[h, krows, HEAD:])

    def attend_more(d, k):
        krows = pl.ds(pl.multiple_of(origin(k) * 256, 256), 256)

        @pl.when(origin(k) < origin(d))
        def _():
            more_keys(d, krows)

    def more_keys(d, krows):
        for hp in range(4):
            q2 = qs[d, 2 * hp:2 * hp + 2].reshape(2 * TOK, HEAD)
            h = hp // 2
            s = dot_t(q2, kv[h, krows, :HEAD]) * SCALE2 + bias[0:1, krows]
            before = sm[d, hp]
            top = jnp.maximum(before, jnp.broadcast_to(jnp.max(s, axis=-1, keepdims=True), (2 * TOK, HEAD)))
            p = jnp.exp2(s - jnp.concatenate([top, top], axis=1))
            fade = jnp.exp2(before - top)
            sm[d, hp] = top
            so[d, hp] = so[d, hp] * jnp.concatenate([fade, fade], axis=1) + dot(p.astype(bf16), kv[h, krows, HEAD:])

    def attend_near(d):
        attend_own(d)

        def others(i, _):
            attend_more(d, lax.rem(d + i, 3))
            return 0

        lax.fori_loop(1, 3, others, 0)

    def settle(d):
        for hp in range(4):
            o = (so[d, hp, :, :HEAD] / so[d, hp, :, HEAD:]).astype(bf16)
            at[d, :, hp * 256:hp * 256 + HEAD] = o[:TOK]
            at[d, :, hp * 256 + HEAD:(hp + 1) * 256] = o[TOK:]

    arrived(kv.at[0, pl.ds(0, 6 * TOK), pl.ds(0, 2 * HEAD)], kvR.at[0])

    def before_far(i, _):
        attend_near(lax.rem(i + 1, 3))
        return 0

    lax.fori_loop(0, 3, before_far, 0)

    def out_piece(d, q):
        cols = pl.ds(pl.multiple_of(q * PIECE, PIECE), PIECE)
        part = dot(at[d, :, :512], wo[0, :, cols]) + dot(at[d, :, 512:], wo[1, :, cols])
        pb[d, q] = part.astype(bf16)

    def half_piece(d, q, half):
        cols = pl.ds(pl.multiple_of(q * PIECE + half * 512, 512), 512)
        part = dot(at[d, :, :512], wo[0, :, cols]) + dot(at[d, :, 512:], wo[1, :, cols])
        pb[d, q, :, half * 512:(half + 1) * 512] = part.astype(bf16)

    def half_send(direction, q, half):
        cols = pl.ds(half * 512, 512)
        return remote(
            pb.at[2 - direction, q, :, cols], nr.at[direction, q, :, cols], nS, nR.at[direction, q],
            near(1 - 2 * direction, 0),
        )

    def far_send(q):
        if q < 2:
            return remote(pb.at[3, q], fr.at[0, q], fS, fR.at[0, q], near(1, 0))
        return remote(pb.at[3, q], fr.at[1, q - 2], fS, fR.at[1, q - 2], near(-1, 0))

    def near_send(direction, q):
        return remote(
            pb.at[2 - direction, q], nr.at[direction, q], nS, nR.at[direction, q],
            near(1 - 2 * direction, 0),
        )

    clear(0)

    for direction in range(2):
        arrived(xs.at[3, 2 * direction], farR.at[direction, 0])
        project(3, 2 * direction, 0)
    lwo.wait()
    arrived(wo.at[1], wR.at[1])
    right_needs = origin(3) < origin(2)
    left_needs = origin(3) < origin(1)

    @pl.when(jnp.logical_not(right_needs))
    def _():
        settle(2)
        out_piece(2, 2)

    @pl.when(jnp.logical_not(left_needs))
    def _():
        settle(1)
        out_piece(1, 0)

    for k in range(1, 4):
        for direction in range(2):
            q = 2 * direction + 1
            arrived(xs.at[3, q, :, pl.ds(*PARTS[k])], farR.at[direction, k])
            project(3, q, 0, *PARTS[k])

    @pl.when(jnp.logical_not(right_needs))
    def _():
        near_send(0, 2).start()

    @pl.when(jnp.logical_not(left_needs))
    def _():
        near_send(1, 0).start()

    finish_keys(3, 0)
    arrived(kv.at[0, pl.ds(0, 2 * TOK), pl.ds(0, 2 * HEAD)], kvR.at[1])

    def answer():
        arrived(qn, qnR)
        q = qn[...].reshape(8 * 16, HEAD)
        s = dot_t(q, kv[0, :, :HEAD]) * SCALE2 + bias[0:1, :]
        top = jnp.max(s, axis=-1, keepdims=True)
        p = jnp.exp2(s - top)
        o = dot(p.astype(bf16), kv[0, :, HEAD:])
        pks[:, 0] = o[:, :HEAD].reshape(8, 16, HEAD)
        pks[:, 1] = jnp.broadcast_to(top, (128, HEAD)).reshape(8, 16, HEAD)
        pks[:, 2] = o[:, HEAD:].reshape(8, 16, HEAD)

    def reply(j):
        return remote(pks.at[j], pk.at[batch], pkS, pkR, other(j))

    def pieces(d, first, second):
        def piece(k, _):
            out_piece(d, jnp.where(k == 0, first, second))
            return 0

        lax.fori_loop(0, 2, piece, 0)

    far_rows = pl.ds(pl.multiple_of(origin(3) * 256, 256), 256)

    def near_block(i, _):
        d = jnp.where(c == 0, 2 - i, 1 + i)

        @pl.when(jnp.where(d == 2, origin(2), origin(1)) > origin(3))
        def _():
            more_keys(d, far_rows)
            settle(d)
            for half in range(2):
                half_piece(d, jnp.where(d == 2, 2, 0), half)

                @pl.when(d == 2)
                def _(half=half):
                    half_send(0, 2, half).start()

                @pl.when(d == 1)
                def _(half=half):
                    half_send(1, 0, half).start()

        return 0

    lax.fori_loop(0, 2, near_block, 0)
    out_piece(2, 3)
    near_send(0, 3).start()
    out_piece(1, 1)
    near_send(1, 1).start()
    rows3, factor3, cosine3, sine3 = factors(3, 0)
    for h in range(2):
        finish_query(3, 0, h, cosine3, sine3)
    answer()

    attend_own(3)
    for j in range(8):
        reply(j).start()

    def far_keys(k, _):
        attend_more(3, k)
        return 0

    lax.fori_loop(0, 3, far_keys, 0)
    settle(3)
    pieces(3, 0, 2)
    far_send(0).start()
    far_send(2).start()
    pieces(3, 1, 3)
    pieces(2, 0, 1)
    pieces(1, 2, 3)
    arrived(pk, pkR)
    want = jnp.full((16, 128), assign_ref[0, 0], jnp.int32)
    no = jnp.zeros((16, 128), f32)
    nm = jnp.zeros((16, 128), f32)
    nl = jnp.zeros((16, 128), f32)
    for j in range(8):
        hit = want == j
        no = no + jnp.where(hit, pk[j, 0], 0.0)
        nm = nm + jnp.where(hit, pk[j, 1], 0.0)
        nl = nl + jnp.where(hit, pk[j, 2], 0.0)
    slots = jnp.full((16, 128), slot_ref[0, 0], jnp.int32)
    for r in range(ROWS):
        mine = slots == r
        m2 = jnp.where(mine, nm, NEG)
        top = jnp.maximum(ms[r], m2)
        a = jnp.exp2(ms[r] - top)
        b = jnp.exp2(m2 - top)
        o = (os_[r] * a + no * b) / (ls[r] * a + nl * b)
        od[pl.ds(r, 16, stride=ROWS), :] = o
    part = jnp.zeros((16, D), f32)
    for h in range(GROUP):
        part = part + dot(od[pl.ds(h * 16, 16), :].astype(bf16), wo[0, pl.ds(h * HEAD, HEAD), :])
    o32[...] = part

    def half_cols(core):
        return pl.ds(pl.multiple_of(core * (D // 2), D // 2), D // 2)

    def chip_cols(core, chip):
        return pl.ds(pl.multiple_of(core * (D // 2) + chip * 512, 512), 512)

    hs[...] = o32[:, half_cols(1 - c)].astype(bf16)
    attend_more(0, 3)
    settle(0)
    remote(hs, hr, dS.at[0], dR.at[0], near(0, 1)).start()
    pieces(0, 0, 2)
    arrived(hr, dR.at[0])
    o32[:, half_cols(c)] = o32[:, half_cols(c)] + hr[...].astype(f32)
    for k in range(4):
        dsb[k] = o32[:, chip_cols(c, lax.rem(x + k, 4))].astype(bf16)
    for k in range(1, 4):
        remote(dsb.at[k], drb.at[k - 1], dS.at[1], dR.at[1], near(k, 0)).start()
    far_send(1).start()
    far_send(3).start()

    pieces(0, 1, 3)

    def relay(q):
        arrived(fr.at[0, q], fR.at[0, q])
        pb[2, q] = (pb[2, q].astype(f32) + fr[0, q].astype(f32)).astype(bf16)
        arrived(fr.at[1, q], fR.at[1, q])
        pb[1, q + 2] = (pb[1, q + 2].astype(f32) + fr[1, q].astype(f32)).astype(bf16)
        near_send(0, q).start()
        near_send(1, q + 2).start()

    relay(0)
    arrived(drb, dR.at[1])
    total = o32[:, chip_cols(c, x)]
    for k in range(3):
        total = total + drb[k].astype(f32)
    dfb[0, 0] = (x16[:, chip_cols(c, x)] + total).astype(bf16)
    for k in range(1, 4):
        remote(dfb.at[0, 0], dfb.at[0, k], dS.at[2], dR.at[2], near(k, 0)).start()
    relay(1)
    arrived(dfb.at[0, pl.ds(1, 3)], dR.at[2])
    remote(dfb.at[0], dfb.at[1], dS.at[3], dR.at[3], near(0, 1)).start()
    arrived(dfb.at[1], dR.at[3])
    for core in range(2):
        for k in range(4):
            o32[:, chip_cols(lax.rem(c + core, 2), lax.rem(x - k + 4, 4))] = dfb[core, k].astype(f32)
    dout_ref[...] = o32[...].astype(bf16)

    for i, q in enumerate((0, 2, 1, 3)):
        arrived(nr.at[0, q], nR.at[0, q])
        arrived(nr.at[1, q], nR.at[1, q])
        cols = slice(q * PIECE, (q + 1) * PIECE)
        total = pb[0, q].astype(f32) + nr[0, q].astype(f32) + nr[1, q].astype(f32)
        out_ref[:, cols] = (xs[0, q].astype(f32) + total).astype(bf16)

    gone(xs.at[pl.ds(0, 3)], agS)
    gone(wq.at[0], wS.at[0])
    gone(wo.at[0], wS.at[1])
    gone(pls, plS)
    gone(qn, qnS)
    gone(pk, pkS)
    gone(kv.at[0, :, pl.ds(0, 2 * HEAD)], kvS)
    gone(pb.at[3], fS)
    gone(pb.at[pl.ds(1, 2)], nS)
    gone(hr, dS.at[0])
    gone(drb, dS.at[1])
    gone(drb, dS.at[2])
    gone(dfb.at[0], dS.at[3])


def body(
    prompt, prompt_len, dec_tokens, cache_k, cache_v, cache_len, assign, slot, gain, w_qkv, w_out
):
    ct, st, fr = tables()
    any_ = pl.BlockSpec(memory_space=pl.ANY)
    vmem = pl.BlockSpec(memory_space=pltpu.VMEM)
    V = pltpu.VMEM
    dma = pltpu.SemaphoreType.DMA
    OUT = pltpu.VMEM
    out, dout = pl.pallas_call(
        kernel,
        out_shape=(
            OUT((TOK, D), bf16),
            OUT((16, D), bf16),
        ),
        in_specs=[any_] * 14,
        out_specs=(vmem, vmem),
        scratch_shapes=[
            pltpu.SMEM((1, 1), jnp.int32),
            pltpu.SMEM((1, 1), jnp.int32),
            pltpu.SMEM((1, 1), jnp.int32),
            pltpu.SMEM((ROWS,), jnp.int32),
            V((1, D), f32),
            V((8, HEAD), f32),
            V((4, 4, TOK, PIECE), bf16),
            V((2, D, QKV), bf16),
            V((2, 512, D), bf16),
            V((ROWS, CACHE, HEAD), bf16),
            V((ROWS, CACHE, HEAD), bf16),
            V((2, 2, TOK, QKV), f32),
            V((2, TOK, HEAD), f32),
            V((4, 8, TOK, HEAD), bf16),
            V((2, STRETCH, 3 * HEAD), bf16),
            V((4, 4, 2 * TOK, 2 * HEAD), f32),
            V((4, 4, 2 * TOK, HEAD), f32),
            V((4, TOK, 1024), bf16),
            V((4, 4, TOK, PIECE), bf16),
            V((2, 2, TOK, PIECE), bf16),
            V((2, 4, TOK, PIECE), bf16),
            V((STRETCH, HEAD), f32),
            V((STRETCH, HEAD), f32),
            V((8, STRETCH), f32),
            V((4, TOK, PIECE), bf16),
            V((STEPS, ROWS, D), bf16),
            V((16, D), f32),
            V((16, D), bf16),
            V((16, QKV), f32),
            V((64, HEAD), f32),
            V((16, HEAD), bf16),
            V((16, HEAD), bf16),
            V((ROWS, 16, HEAD), bf16),
            V((ROWS, 16, HEAD), f32),
            V((ROWS, 16, HEAD), f32),
            V((ROWS, 16, HEAD), f32),
            V((8, 128), jnp.int32),
            V((8, 8, 128), jnp.int32),
            V((16, HEAD), bf16),
            V((8, 16, HEAD), bf16),
            V((8, 3, 16, HEAD), f32),
            V((8, 3, 16, HEAD), f32),
            V((64, HEAD), f32),
            V((16, D // 2), bf16),
            V((16, D // 2), bf16),
            V((4, 16, 512), bf16),
            V((3, 16, 512), bf16),
            V((2, 4, 16, 512), bf16),
            V((16, D), f32),
            pltpu.SemaphoreType.REGULAR,
            pltpu.SemaphoreType.REGULAR,
            dma((6,)), dma((8,)),
            dma, dma((2, 4)), dma((2, 4)),
            dma((2,)), dma((2,)),
            dma, dma, dma, dma, dma, dma,
            dma, dma((2,)),
            dma, dma((2, 2)),
            dma, dma((2, 4)),
            dma((4,)), dma((4,)),
        ],
        compiler_params=pltpu.CompilerParams(
            collective_id=0, has_side_effects=True, vmem_limit_bytes=59 * 2**20
        ),
        name="layer",
    )(
        prompt_len, assign, slot, cache_len, gain.reshape(1, D), jnp.asarray(fr),
        prompt, dec_tokens, cache_k, cache_v, w_qkv, w_out, jnp.asarray(ct), jnp.asarray(st),
    )
    return pl.pallas_call(
        writer,
        out_shape=(
            jax.ShapeDtypeStruct((1, TOK, D), bf16),
            jax.ShapeDtypeStruct((STEPS, ROWS, D), bf16),
        ),
        in_specs=[vmem, vmem],
        out_specs=(any_, any_),
        scratch_shapes=[V((STEPS, ROWS, D), bf16), dma((5,))],
        compiler_params=pltpu.CompilerParams(vmem_limit_bytes=8 * 2**20),
        name="write",
    )(out, dout)


def writer(out_ref, dout_ref, full_ref, dec_ref, stage, sem):
    copies = []
    for q in range(4):
        rows = pl.ds(q * 32, 32)
        copies.append(pltpu.make_async_copy(out_ref.at[rows], full_ref.at[0, rows], sem.at[q]))
        copies[q].start()
    for s in range(STEPS):
        stage[s] = dout_ref[pl.ds(s * ROWS, ROWS), :]
    copies.append(pltpu.make_async_copy(stage, dec_ref, sem.at[4]))
    copies[4].start()
    for cp in copies:
        cp.wait()


def solution(mesh):
    return jax.shard_map(
        body,
        mesh=mesh,
        in_specs=(
            P(("pool", "batch"), "blk", None),
            P("pool", "batch"),
            P(None, ("pool", "batch"), None),
            P(("pool", "batch"), None, "blk"),
            P(("pool", "batch"), None, "blk"),
            P(("pool", "batch")),
            P("pool", "batch"),
            P("pool", "batch"),
            P(),
            P(None, "blk"),
            P("blk", None),
        ),
        out_specs=(P(("pool", "batch"), "blk", None), P(None, ("pool", "batch"), None)),
        check_vma=False,
    )
```

```python
import functools

import jax
import jax.numpy as jnp
import numpy as np
from jax import lax
from jax.experimental import pallas as pl
from jax.experimental.pallas import tpu as pltpu
from jax.sharding import PartitionSpec as P

MESH = pl.DeviceIdType.MESH
HEAD = 128
GROUP = 4
D = 4096
TOK = 128
STRETCH = 1024
CACHE = 4096
STEPS = 4
ROWS = 4
QKV = (GROUP + 2) * HEAD
PIECE = 1024
PARTS = ((0, 1024), (0, 512), (512, 256), (768, 256))
EPSILON = 1e-05
THETA = 500000.0
NEG = -1e30
SCALE2 = float(HEAD ** (-0.5) * np.log2(np.e))

f32 = jnp.float32
bf16 = jnp.bfloat16


def tables():
    half = HEAD // 2
    freqs = (THETA ** (-np.arange(half, dtype=np.float64) / half)).astype(np.float32)
    angles = np.arange(STRETCH, dtype=np.float32)[:, None] * freqs
    cosine = np.cos(angles.astype(np.float64)).astype(np.float32)
    sine = np.sin(angles.astype(np.float64)).astype(np.float32)
    ct = np.concatenate([cosine, cosine], axis=1)
    st = np.concatenate([-sine, sine], axis=1)
    fr = np.broadcast_to(np.concatenate([freqs, freqs])[None, :], (8, HEAD))
    return ct, st, np.ascontiguousarray(fr)


def dot(a, b):
    return jnp.dot(a, b, preferred_element_type=f32)


def dot_t(a, b):
    return lax.dot_general(a, b, (((1,), (1,)), ((), ())), preferred_element_type=f32)


def kernel(
    plen_in, assign_in, slot_in, clen_in, gain_in, freq_in,
    prompt_ref, dec_ref, ck_ref, cv_ref, wqkv_ref, wout_ref, ct_ref, st_ref,
    out_ref, dout_ref,
    plen_ref, assign_ref, slot_ref, clen_ref, gain_ref, freq_ref,
    xs, wq, wo, ck, cv, acc, ssq, qs, kv, so, sm, at, pb, fr, nr, ct, st, bias,
    xn, dmv, x16, xd, jd, qd, kd, vd, qr, ms, ls, os_, plt, pls, qnew, qn, pks, pk, od, hs, hr, dsb, drb, dfb, lr, lhs, lhr, lsb, lrb, lfb, o32,
    ring, opened, ssem, lsem, agS, agR, farR, wS, wR, plS, plR, qnS, qnR, pkS, pkR, kvS, kvR, fS, fR, nS, nR, dS, dR, eS, eR,
):
    me = lax.axis_index("blk")
    pool = lax.axis_index("pool")
    batch = lax.axis_index("batch")
    x = me // 2
    c = lax.rem(me, 2)

    def near(dx, dc):
        return {"blk": lax.rem(x + dx + 4, 4) * 2 + lax.rem(c + dc, 2)}

    def other(j):
        return {"pool": 1 - pool, "batch": j}

    def peer(j):
        return {"blk": lax.rem(me + j, 8)}

    def remote(src, dst, ss, rs, dev):
        return pltpu.make_async_remote_copy(
            src_ref=src, dst_ref=dst, send_sem=ss, recv_sem=rs, device_id=dev, device_id_type=MESH
        )

    def arrived(ref, sem):
        remote(ref, ref, sem, sem, near(0, 1)).wait_recv()

    def gone(ref, sem):
        remote(ref, ref, sem, sem, near(0, 1)).wait_send()

    ldec = pltpu.make_async_copy(dec_ref, dmv, lsem.at[0])
    lweights = pltpu.make_async_copy(wqkv_ref, wq.at[0], lsem.at[1])
    ltokens = [
        pltpu.make_async_copy(prompt_ref.at[0, :, pl.ds(q * PIECE, PIECE)], xs.at[0, q], lsem.at[2])
        for q in range(4)
    ]
    lct = pltpu.make_async_copy(ct_ref, ct, lsem.at[3])
    lst = pltpu.make_async_copy(st_ref, st, lsem.at[4])
    lck = pltpu.make_async_copy(ck_ref, ck, lsem.at[5])
    lcv = pltpu.make_async_copy(cv_ref, cv, lsem.at[6])
    lwo = pltpu.make_async_copy(wout_ref, wo.at[0], lsem.at[7])
    local = [*ltokens, ldec, lweights, lct, lst, lck, lcv, lwo]
    small = [
        pltpu.make_async_copy(a, b, ssem.at[i])
        for i, (a, b) in enumerate((
            (plen_in, plen_ref), (assign_in, assign_ref), (slot_in, slot_ref),
            (clen_in, clen_ref), (gain_in, gain_ref), (freq_in, freq_ref),
        ))
    ]
    for cp in local[:4]:
        cp.start()
    for cp in small:
        cp.start()
    for cp in local[4:]:
        cp.start()

    barrier = pltpu.get_barrier_semaphore()
    gate = me == 0
    for j in range(1, 8):
        @pl.when(lax.rem(me + j, 8) != 0)
        def _(j=j):
            pl.semaphore_signal(barrier, inc=1, device_id=peer(j), device_id_type=MESH)

    kv[:, :, 2 * HEAD:] = jnp.ones((2, STRETCH, HEAD), bf16)

    @pl.when(me != 0)
    def _():
        pl.semaphore_wait(barrier, 7)

    @pl.when(me == 1)
    def _():
        pl.semaphore_signal(ring, inc=1, device_id=peer(7), device_id_type=MESH)

    @pl.when(gate)
    def _():
        pl.semaphore_wait(ring, 1)

    def gather(direction, k):
        q = (k + 2 * direction) % 4
        cols = pl.ds(q * PIECE, PIECE)
        src = prompt_ref.at[0, :, cols] if k == 0 else xs.at[0, q]
        return remote(src, xs.at[1 + direction, q], agS, agR.at[direction, q], near(1 - 2 * direction, 0))

    def onward(direction, k):
        q = 2 * direction + (k > 0)
        cols = pl.ds(*PARTS[k])
        return remote(
            xs.at[1 + direction, q, :, cols], xs.at[3, q, :, cols], agS, farR.at[direction, k],
            near(1 - 2 * direction, 0),
        )

    for k in range(4):
        if k == 1:
            pltpu.make_async_copy(xs.at[0], xs.at[0], lsem.at[2]).wait()
        gather(0, k).start()
        gather(1, k).start()

    remote(wqkv_ref, wq.at[1], wS.at[0], wR.at[0], near(0, 1)).start()
    remote(wout_ref, wo.at[1], wS.at[1], wR.at[1], near(0, 1)).start()

    @pl.when(gate)
    def _():
        for j in range(8):
            pl.semaphore_signal(barrier, inc=1, device_id=other(j), device_id_type=MESH)

    for cp in small:
        cp.wait()
    plt[...] = jnp.full((8, 128), plen_ref[0, 0], jnp.int32)
    col = lax.broadcasted_iota(jnp.int32, (8, STRETCH), 1)
    bias[...] = jnp.where(col < jnp.full((8, STRETCH), plen_ref[0, 0], jnp.int32), 0.0, NEG)

    ldec.wait()
    for s in range(STEPS):
        x16[pl.ds(s * ROWS, ROWS), :] = dmv[s].astype(f32)
    wide = x16[...]
    factor = lax.rsqrt(jnp.mean(wide * wide, axis=-1, keepdims=True) + EPSILON)
    xd[...] = (wide * factor * gain_ref[...]).astype(bf16)
    joined = jnp.zeros((16, QKV), f32)
    lweights.wait()
    for q in range(4):
        joined = joined + dot(xd[:, q * PIECE:(q + 1) * PIECE], wq[0, pl.ds(q * PIECE, PIECE), :])
    jd[...] = joined

    def scaled(slot, q, a, at=0, size=PIECE):
        wide = xs[slot, q, :, pl.ds(at, size)].astype(f32)
        square = wide * wide
        part = square[:, :HEAD]
        for i in range(1, size // HEAD):
            part = part + square[:, i * HEAD:(i + 1) * HEAD]
        ssq[a] += part
        return (wide * gain_ref[:, pl.ds(pl.multiple_of(q * PIECE + at, size), size)]).astype(bf16)

    def project(slot, q, a, at=0, size=PIECE):
        tokens = scaled(slot, q, a, at, size)
        rows = pl.ds(pl.multiple_of(q * PIECE + at, size), size)
        for h in range(2):
            acc[a, h] += dot(tokens, wq[h, rows, :])

    def clear(a):
        acc[a] = jnp.zeros((2, TOK, QKV), f32)
        ssq[a] = jnp.zeros((TOK, HEAD), f32)

    clear(0)

    def own_first(q, _):
        tokens = scaled(0, q, 0)
        xn[q] = tokens
        acc[0, 0] += dot(tokens, wq[0, pl.ds(pl.multiple_of(q * PIECE, PIECE), PIECE), :])
        return 0

    lax.fori_loop(0, 4, own_first, 0)

    def turn(u, cosine, sine):
        return u * cosine + pltpu.roll(u, HEAD // 2, 1) * sine

    def decode_queries():
        wanted = jnp.full((8, 128), assign_ref[0, 0], jnp.int32)
        newlen = jnp.zeros((8, 128), jnp.int32)
        arrived(pls, plR)
        for j in range(8):
            newlen = newlen + jnp.where(wanted == j, pls[j], 0)
        row = lax.broadcasted_iota(jnp.int32, (16, 128), 0)
        row_r = lax.rem(row, ROWS)
        place = jnp.zeros((16, 128), jnp.int32)
        for r in range(ROWS):
            place = jnp.where(row_r == r, jnp.full((16, 128), clen_ref[r], jnp.int32), place)
        fresh = row_r == jnp.full((16, 128), slot_ref[0, 0], jnp.int32)
        place = jnp.where(fresh, jnp.broadcast_to(newlen[0:1, :], (16, 128)), place) + row // ROWS
        angle = place.astype(f32) * freq_ref[0:1, :]
        lane = lax.broadcasted_iota(jnp.int32, (16, 128), 1)
        dcos = jnp.cos(angle)
        dsin = jnp.sin(angle)
        dsin = jnp.where(lane < HEAD // 2, -dsin, dsin)

        for h in range(GROUP):
            qd[pl.ds(h * 16, 16), :] = turn(jd[:, h * HEAD:(h + 1) * HEAD], dcos, dsin)
        kd[...] = turn(jd[:, GROUP * HEAD:(GROUP + 1) * HEAD], dcos, dsin).astype(bf16)
        vd[...] = jd[:, (GROUP + 1) * HEAD:].astype(bf16)
        slots = jnp.full((16, 128), slot_ref[0, 0], jnp.int32)
        picked = jnp.zeros((16, 128), f32)
        for r in range(ROWS):
            part = qd[pl.ds(r, 16, stride=ROWS), :]
            qr[r] = part.astype(bf16)
            picked = picked + jnp.where(slots == r, part, 0.0)
        qnew[...] = picked.astype(bf16)

    def origin(slot):
        if isinstance(slot, int):
            return lax.rem(x + (0, 3, 1, 2)[slot], 4)
        return lax.rem(x + jnp.where(slot == 1, 3, jnp.where(slot == 2, 1, jnp.where(slot == 3, 2, 0))), 4)

    def exchange(slot, h):
        rows = pl.ds(pl.multiple_of((origin(slot) * 2 + c) * TOK, TOK), TOK)
        cols = pl.ds(0, 2 * HEAD)
        return remote(kv.at[h, rows, cols], kv.at[1 - h, rows, cols], kvS, kvR.at[slot // 3], near(0, 1))

    def factors(slot, a):
        rows = pl.ds(pl.multiple_of((origin(slot) * 2 + c) * TOK, TOK), TOK)
        factor = lax.rsqrt(jnp.sum(ssq[a], axis=-1, keepdims=True) * (1.0 / D) + EPSILON)
        return rows, factor, ct[rows, :] * factor, st[rows, :] * factor

    def finish_query(slot, a, h, cosine, sine):
        for g in range(GROUP):
            qs[slot, h * GROUP + g] = turn(acc[a, h, :, g * HEAD:(g + 1) * HEAD], cosine, sine).astype(bf16)

    def finish_keys(slot, a):
        rows, factor, cosine, sine = factors(slot, a)
        for h in range(2):
            kv[h, rows, :HEAD] = turn(acc[a, h, :, GROUP * HEAD:(GROUP + 1) * HEAD], cosine, sine).astype(bf16)
            kv[h, rows, HEAD:2 * HEAD] = (acc[a, h, :, (GROUP + 1) * HEAD:] * factor).astype(bf16)
        exchange(slot, 0).start()
        qs[slot, 0] = turn(acc[a, 0, :, :HEAD], cosine, sine).astype(bf16)
        exchange(slot, 1).start()

    def finish(slot, a):
        finish_keys(slot, a)
        rows, factor, cosine, sine = factors(slot, a)
        for h in range(2):
            finish_query(slot, a, h, cosine, sine)

    def old_row(r):
        q16 = qr[r]
        edge = jnp.full((16, CACHE), clen_ref[r], jnp.int32)
        edge = jnp.where(jnp.full((16, CACHE), slot_ref[0, 0], jnp.int32) == r, 0, edge)
        span = lax.broadcasted_iota(jnp.int32, (16, CACHE), 1)
        old = jnp.where(span < edge, dot_t(q16, ck[r]) * SCALE2, NEG)
        own = dot_t(q16, kd[...]) * SCALE2
        i16 = lax.broadcasted_iota(jnp.int32, (16, 16), 0)
        j16 = lax.broadcasted_iota(jnp.int32, (16, 16), 1)
        keep = (lax.rem(j16, ROWS) == r) & (j16 // ROWS <= lax.rem(i16, STEPS))
        own = jnp.where(keep, own, NEG)
        top = jnp.maximum(jnp.max(old, axis=-1, keepdims=True), jnp.max(own, axis=-1, keepdims=True))
        pold = jnp.exp2(old - top)
        pown = jnp.exp2(own - top)
        total = jnp.sum(pold, axis=-1, keepdims=True) + jnp.sum(pown, axis=-1, keepdims=True)
        mixed = dot(pold.astype(bf16), cv[r]) + dot(pown.astype(bf16), vd[...])
        ms[r] = jnp.broadcast_to(top, (16, 128))
        ls[r] = jnp.broadcast_to(total, (16, 128))
        os_[r] = mixed

    def query(j):
        return remote(qnew, qn.at[batch], qnS, qnR, other(j))

    @pl.when(gate)
    def _():
        pl.semaphore_wait(barrier, 8)
        for j in range(1, 8):
            pl.semaphore_signal(opened, inc=1, device_id=peer(j), device_id_type=MESH)

    @pl.when(me != 0)
    def _():
        pl.semaphore_wait(opened, 1)

    def length(j):
        return remote(plt, pls.at[batch], plS, plR, other(j))

    for j in range(8):
        length(j).start()

    arrived(wq.at[1], wR.at[0])
    lct.wait()
    lst.wait()

    def own_second(q, _):
        acc[0, 1] += dot(xn[q], wq[1, pl.ds(pl.multiple_of(q * PIECE, PIECE), PIECE), :])
        return 0

    lax.fori_loop(0, 4, own_second, 0)
    finish(0, 0)

    def half_cols(core):
        return pl.ds(pl.multiple_of(core * (D // 2), D // 2), D // 2)

    def chip_cols(core, chip):
        return pl.ds(pl.multiple_of(core * (D // 2) + chip * 512, 512), 512)

    def early_rows():
        for r in range(ROWS):
            od[pl.ds(r, 16, stride=ROWS), :] = os_[r] / ls[r]
        lwo.wait()
        part = jnp.zeros((16, D), f32)
        for h in range(GROUP):
            part = part + dot(od[pl.ds(h * 16, 16), :].astype(bf16), wo[0, pl.ds(h * HEAD, HEAD), :])
        o32[...] = part
        hs[...] = o32[:, half_cols(1 - c)].astype(bf16)

    def early_halves():
        arrived(hr, dR.at[0])
        o32[:, half_cols(c)] = o32[:, half_cols(c)] + hr[...].astype(f32)
        for k in range(4):
            dsb[k] = o32[:, chip_cols(c, lax.rem(x + k, 4))].astype(bf16)

    clear(0)
    clear(1)
    lck.wait()
    lcv.wait()

    def near_step(t, _):
        q1 = t
        q2 = lax.rem(t + 2, 4)
        arrived(xs.at[1, q1], agR.at[0, q1])
        arrived(xs.at[2, q2], agR.at[1, q2])

        @pl.when(t == 0)
        def _():
            onward(0, 0).start()
            onward(1, 0).start()

        @pl.when(t == 1)
        def _():
            for k in (1, 2, 3):
                onward(0, k).start()
                onward(1, k).start()

        project(1, q1, 0)
        project(2, q2, 1)

        @pl.when(t == 1)
        def _():
            decode_queries()
            for j in range(2):
                old_row(j)
            for j in range(8):
                query(j).start()
            for j in range(2, 4):
                old_row(j)

        @pl.when(t == 2)
        def _():
            early_rows()

        @pl.when(t == 3)
        def _():
            remote(hs, hr, dS.at[0], dR.at[0], near(0, 1)).start()

        return 0

    lax.fori_loop(0, 4, near_step, 0)
    finish(1, 0)
    finish(2, 1)

    def attend_own(d):
        krows = pl.ds(pl.multiple_of(origin(d) * 256, 256), 256)
        qi = lax.rem(lax.broadcasted_iota(jnp.int32, (2 * TOK, 256), 0), TOK) + c * TOK
        ki = lax.broadcasted_iota(jnp.int32, (2 * TOK, 256), 1)
        mask = jnp.where(ki <= qi, jnp.broadcast_to(bias[0:1, krows], (2 * TOK, 256)), NEG)
        for hp in range(4):
            q2 = qs[d, 2 * hp:2 * hp + 2].reshape(2 * TOK, HEAD)
            h = hp // 2
            s = dot_t(q2, kv[h, krows, :HEAD]) * SCALE2 + mask
            top = jnp.max(s, axis=-1, keepdims=True)
            p = jnp.exp2(s - top)
            sm[d, hp] = jnp.broadcast_to(top, (2 * TOK, HEAD))
            so[d, hp] = dot(p.astype(bf16), kv[h, krows, HEAD:])

    def attend_more(d, k):
        krows = pl.ds(pl.multiple_of(origin(k) * 256, 256), 256)

        @pl.when(origin(k) < origin(d))
        def _():
            more_keys(d, krows)

    def more_keys(d, krows):
        for hp in range(4):
            q2 = qs[d, 2 * hp:2 * hp + 2].reshape(2 * TOK, HEAD)
            h = hp // 2
            s = dot_t(q2, kv[h, krows, :HEAD]) * SCALE2 + bias[0:1, krows]
            before = sm[d, hp]
            top = jnp.maximum(before, jnp.broadcast_to(jnp.max(s, axis=-1, keepdims=True), (2 * TOK, HEAD)))
            p = jnp.exp2(s - jnp.concatenate([top, top], axis=1))
            fade = jnp.exp2(before - top)
            sm[d, hp] = top
            so[d, hp] = so[d, hp] * jnp.concatenate([fade, fade], axis=1) + dot(p.astype(bf16), kv[h, krows, HEAD:])

    def attend_near(d):
        attend_own(d)

        def others(i, _):
            attend_more(d, lax.rem(d + i, 3))
            return 0

        lax.fori_loop(1, 3, others, 0)

    def settle(d):
        for hp in range(4):
            o = (so[d, hp, :, :HEAD] / so[d, hp, :, HEAD:]).astype(bf16)
            at[d, :, hp * 256:hp * 256 + HEAD] = o[:TOK]
            at[d, :, hp * 256 + HEAD:(hp + 1) * 256] = o[TOK:]

    arrived(kv.at[0, pl.ds(0, 6 * TOK), pl.ds(0, 2 * HEAD)], kvR.at[0])

    def before_far(i, _):
        attend_near(lax.rem(i + 1, 3))
        return 0

    lax.fori_loop(0, 3, before_far, 0)

    def out_piece(d, q):
        cols = pl.ds(pl.multiple_of(q * PIECE, PIECE), PIECE)
        part = dot(at[d, :, :512], wo[0, :, cols]) + dot(at[d, :, 512:], wo[1, :, cols])
        pb[d, q] = part.astype(bf16)

    def half_piece(d, q, half):
        cols = pl.ds(pl.multiple_of(q * PIECE + half * 512, 512), 512)
        part = dot(at[d, :, :512], wo[0, :, cols]) + dot(at[d, :, 512:], wo[1, :, cols])
        pb[d, q, :, half * 512:(half + 1) * 512] = part.astype(bf16)

    def half_send(direction, q, half):
        cols = pl.ds(half * 512, 512)
        return remote(
            pb.at[2 - direction, q, :, cols], nr.at[direction, q, :, cols], nS, nR.at[direction, q],
            near(1 - 2 * direction, 0),
        )

    def far_send(q):
        if q < 2:
            return remote(pb.at[3, q], fr.at[0, q], fS, fR.at[0, q], near(1, 0))
        return remote(pb.at[3, q], fr.at[1, q - 2], fS, fR.at[1, q - 2], near(-1, 0))

    def near_send(direction, q):
        return remote(
            pb.at[2 - direction, q], nr.at[direction, q], nS, nR.at[direction, q],
            near(1 - 2 * direction, 0),
        )

    clear(0)

    for direction in range(2):
        arrived(xs.at[3, 2 * direction], farR.at[direction, 0])
        project(3, 2 * direction, 0)
    early_halves()
    arrived(wo.at[1], wR.at[1])
    right_needs = origin(3) < origin(2)
    left_needs = origin(3) < origin(1)

    @pl.when(jnp.logical_not(right_needs))
    def _():
        settle(2)
        out_piece(2, 2)

    @pl.when(jnp.logical_not(left_needs))
    def _():
        settle(1)
        out_piece(1, 0)

    for k in range(1, 4):
        remote(dsb.at[k], drb.at[k - 1], dS.at[1], dR.at[1], near(k, 0)).start()

    for k in range(1, 4):
        for direction in range(2):
            q = 2 * direction + 1
            arrived(xs.at[3, q, :, pl.ds(*PARTS[k])], farR.at[direction, k])
            project(3, q, 0, *PARTS[k])

    @pl.when(jnp.logical_not(right_needs))
    def _():
        near_send(0, 2).start()

    @pl.when(jnp.logical_not(left_needs))
    def _():
        near_send(1, 0).start()

    finish_keys(3, 0)
    arrived(drb, dR.at[1])
    total = o32[:, chip_cols(c, x)]
    for k in range(3):
        total = total + drb[k].astype(f32)
    dfb[0, 0] = (x16[:, chip_cols(c, x)] + total).astype(bf16)
    for k in range(1, 4):
        remote(dfb.at[0, 0], dfb.at[0, k], dS.at[2], dR.at[2], near(k, 0)).start()
    arrived(kv.at[0, pl.ds(0, 2 * TOK), pl.ds(0, 2 * HEAD)], kvR.at[1])

    def answer():
        arrived(qn, qnR)
        q = qn[...].reshape(8 * 16, HEAD)
        s = dot_t(q, kv[0, :, :HEAD]) * SCALE2 + bias[0:1, :]
        top = jnp.max(s, axis=-1, keepdims=True)
        p = jnp.exp2(s - top)
        o = dot(p.astype(bf16), kv[0, :, HEAD:])
        pks[:, 0] = o[:, :HEAD].reshape(8, 16, HEAD)
        pks[:, 1] = jnp.broadcast_to(top, (128, HEAD)).reshape(8, 16, HEAD)
        pks[:, 2] = o[:, HEAD:].reshape(8, 16, HEAD)

    def reply(j):
        return remote(pks.at[j], pk.at[batch], pkS, pkR, other(j))

    def pieces(d, first, second):
        def piece(k, _):
            out_piece(d, jnp.where(k == 0, first, second))
            return 0

        lax.fori_loop(0, 2, piece, 0)

    far_rows = pl.ds(pl.multiple_of(origin(3) * 256, 256), 256)

    def near_block(i, _):
        d = jnp.where(c == 0, 2 - i, 1 + i)

        @pl.when(jnp.where(d == 2, origin(2), origin(1)) > origin(3))
        def _():
            more_keys(d, far_rows)
            settle(d)
            for half in range(2):
                half_piece(d, jnp.where(d == 2, 2, 0), half)

                @pl.when(d == 2)
                def _(half=half):
                    half_send(0, 2, half).start()

                @pl.when(d == 1)
                def _(half=half):
                    half_send(1, 0, half).start()

        return 0

    lax.fori_loop(0, 2, near_block, 0)
    out_piece(2, 3)
    near_send(0, 3).start()
    out_piece(1, 1)
    near_send(1, 1).start()
    rows3, factor3, cosine3, sine3 = factors(3, 0)
    for h in range(2):
        finish_query(3, 0, h, cosine3, sine3)
    answer()

    attend_own(3)
    for j in range(8):
        reply(j).start()

    def far_keys(k, _):
        attend_more(3, k)
        return 0

    lax.fori_loop(0, 3, far_keys, 0)
    settle(3)
    pieces(3, 0, 2)
    far_send(0).start()
    far_send(2).start()
    pieces(3, 1, 3)
    pieces(2, 0, 1)
    pieces(1, 2, 3)
    arrived(pk, pkR)
    want = jnp.full((16, 128), assign_ref[0, 0], jnp.int32)
    no = jnp.zeros((16, 128), f32)
    nm = jnp.zeros((16, 128), f32)
    nl = jnp.zeros((16, 128), f32)
    for j in range(8):
        hit = want == j
        no = no + jnp.where(hit, pk[j, 0], 0.0)
        nm = nm + jnp.where(hit, pk[j, 1], 0.0)
        nl = nl + jnp.where(hit, pk[j, 2], 0.0)
    slots = jnp.full((16, 128), slot_ref[0, 0], jnp.int32)
    mo = jnp.zeros((16, 128), f32)
    mm = jnp.zeros((16, 128), f32)
    ml = jnp.zeros((16, 128), f32)
    for r in range(ROWS):
        mine = slots == r
        mo = mo + jnp.where(mine, os_[r], 0.0)
        mm = mm + jnp.where(mine, ms[r], 0.0)
        ml = ml + jnp.where(mine, ls[r], 0.0)
    top = jnp.maximum(mm, nm)
    a = jnp.exp2(mm - top)
    b = jnp.exp2(nm - top)
    o = (mo * a + no * b) / (ml * a + nl * b)
    head = lax.broadcasted_iota(jnp.int32, (16, 128), 0) // STEPS
    part = jnp.zeros((16, D), f32)
    for h in range(GROUP):
        part = part + dot(jnp.where(head == h, o, 0.0).astype(bf16), wo[0, pl.ds(h * HEAD, HEAD), :])
    part = part[:8] + part[8:]
    part = part + pltpu.roll(part, 4, 0)
    first = lax.broadcasted_iota(jnp.int32, (8, 256), 0) < STEPS
    for k in range(8):
        lr[:, k * 256:(k + 1) * 256] = jnp.where(
            first, part[:, k * 512:k * 512 + 256], part[:, k * 512 + 256:(k + 1) * 512]
        )

    def packed_half(core):
        return pl.ds(pl.multiple_of(core * 1024, 1024), 1024)

    def packed_chip(core, chip):
        return pl.ds(pl.multiple_of(core * 1024 + chip * 256, 256), 256)

    lhs[...] = lr[:, packed_half(1 - c)].astype(bf16)
    attend_more(0, 3)
    settle(0)
    remote(lhs, lhr, eS.at[0], eR.at[0], near(0, 1)).start()
    pieces(0, 0, 2)
    arrived(lhr, eR.at[0])
    lr[:, packed_half(c)] = lr[:, packed_half(c)] + lhr[...].astype(f32)
    for k in range(4):
        lsb[k] = lr[:, packed_chip(c, lax.rem(x + k, 4))].astype(bf16)
    for k in range(1, 4):
        remote(lsb.at[k], lrb.at[k - 1], eS.at[1], eR.at[1], near(k, 0)).start()
    far_send(1).start()
    far_send(3).start()

    pieces(0, 1, 3)
    arrived(dfb.at[0, pl.ds(1, 3)], dR.at[2])
    remote(dfb.at[0], dfb.at[1], dS.at[3], dR.at[3], near(0, 1)).start()

    def relay(q):
        arrived(fr.at[0, q], fR.at[0, q])
        pb[2, q] = (pb[2, q].astype(f32) + fr[0, q].astype(f32)).astype(bf16)
        near_send(0, q).start()
        arrived(fr.at[1, q], fR.at[1, q])
        pb[1, q + 2] = (pb[1, q + 2].astype(f32) + fr[1, q].astype(f32)).astype(bf16)
        near_send(1, q + 2).start()

    relay(0)
    arrived(lrb, eR.at[1])
    total = lr[:, packed_chip(c, x)]
    for k in range(3):
        total = total + lrb[k].astype(f32)
    pick_i = lax.broadcasted_iota(jnp.int32, (16, 16), 0)
    pick_j = lax.broadcasted_iota(jnp.int32, (16, 16), 1)
    pick = pick_j == lax.rem(pick_i, STEPS) * ROWS + jnp.full((16, 16), slot_ref[0, 0], jnp.int32)
    tokens = dot(jnp.where(pick, 1.0, 0.0).astype(bf16), x16[:, chip_cols(c, x)].astype(bf16))[:8]
    lfb[0, 0] = (jnp.where(first, tokens[:, :256], tokens[:, 256:]) + total).astype(bf16)
    for k in range(1, 4):
        remote(lfb.at[0, 0], lfb.at[0, k], eS.at[2], eR.at[2], near(k, 0)).start()
    relay(1)
    arrived(lfb.at[0, pl.ds(1, 3)], eR.at[2])
    remote(lfb.at[0], lfb.at[1], eS.at[3], eR.at[3], near(0, 1)).start()
    arrived(dfb.at[1], dR.at[3])
    arrived(lfb.at[1], eR.at[3])
    for core in range(2):
        for k in range(4):
            o32[:, chip_cols(lax.rem(c + core, 2), lax.rem(x - k + 4, 4))] = dfb[core, k].astype(f32)
            lr[:, packed_chip(lax.rem(c + core, 2), lax.rem(x - k + 4, 4))] = lfb[core, k].astype(f32)
    here = lax.broadcasted_iota(jnp.int32, (ROWS, 256), 0) == jnp.full((ROWS, 256), slot_ref[0, 0], jnp.int32)
    for s in range(STEPS):
        for k in range(8):
            for half in range(2):
                cols = slice(k * 512 + half * 256, k * 512 + (half + 1) * 256)
                late = lr[4 * half + s:4 * half + s + 1, k * 256:(k + 1) * 256]
                dout_ref[s, :, cols] = jnp.where(
                    here, jnp.broadcast_to(late, (ROWS, 256)), o32[s * ROWS:(s + 1) * ROWS, cols]
                ).astype(bf16)

    for i, q in enumerate((0, 2, 1, 3)):
        arrived(nr.at[0, q], nR.at[0, q])
        arrived(nr.at[1, q], nR.at[1, q])
        cols = slice(q * PIECE, (q + 1) * PIECE)
        total = pb[0, q].astype(f32) + nr[0, q].astype(f32) + nr[1, q].astype(f32)
        out_ref[:, cols] = (xs[0, q].astype(f32) + total).astype(bf16)

    gone(xs.at[pl.ds(0, 3)], agS)
    gone(wq.at[0], wS.at[0])
    gone(wo.at[0], wS.at[1])
    gone(pls, plS)
    gone(qn, qnS)
    gone(pk, pkS)
    gone(kv.at[0, :, pl.ds(0, 2 * HEAD)], kvS)
    gone(pb.at[3], fS)
    gone(pb.at[pl.ds(1, 2)], nS)
    gone(hr, dS.at[0])
    gone(drb, dS.at[1])
    gone(drb, dS.at[2])
    gone(dfb.at[0], dS.at[3])
    gone(lhr, eS.at[0])
    gone(lrb, eS.at[1])
    gone(lrb, eS.at[2])
    gone(lfb.at[0], eS.at[3])


def body(
    prompt, prompt_len, dec_tokens, cache_k, cache_v, cache_len, assign, slot, gain, w_qkv, w_out
):
    ct, st, fr = tables()
    any_ = pl.BlockSpec(memory_space=pl.ANY)
    vmem = pl.BlockSpec(memory_space=pltpu.VMEM)
    V = pltpu.VMEM
    dma = pltpu.SemaphoreType.DMA
    OUT = pltpu.VMEM
    out, dout = pl.pallas_call(
        kernel,
        out_shape=(
            OUT((TOK, D), bf16),
            OUT((STEPS, ROWS, D), bf16),
        ),
        in_specs=[any_] * 14,
        out_specs=(vmem, vmem),
        scratch_shapes=[
            pltpu.SMEM((1, 1), jnp.int32),
            pltpu.SMEM((1, 1), jnp.int32),
            pltpu.SMEM((1, 1), jnp.int32),
            pltpu.SMEM((ROWS,), jnp.int32),
            V((1, D), f32),
            V((8, HEAD), f32),
            V((4, 4, TOK, PIECE), bf16),
            V((2, D, QKV), bf16),
            V((2, 512, D), bf16),
            V((ROWS, CACHE, HEAD), bf16),
            V((ROWS, CACHE, HEAD), bf16),
            V((2, 2, TOK, QKV), f32),
            V((2, TOK, HEAD), f32),
            V((4, 8, TOK, HEAD), bf16),
            V((2, STRETCH, 3 * HEAD), bf16),
            V((4, 4, 2 * TOK, 2 * HEAD), f32),
            V((4, 4, 2 * TOK, HEAD), f32),
            V((4, TOK, 1024), bf16),
            V((4, 4, TOK, PIECE), bf16),
            V((2, 2, TOK, PIECE), bf16),
            V((2, 4, TOK, PIECE), bf16),
            V((STRETCH, HEAD), f32),
            V((STRETCH, HEAD), f32),
            V((8, STRETCH), f32),
            V((4, TOK, PIECE), bf16),
            V((STEPS, ROWS, D), bf16),
            V((16, D), f32),
            V((16, D), bf16),
            V((16, QKV), f32),
            V((72, HEAD), f32),
            V((16, HEAD), bf16),
            V((16, HEAD), bf16),
            V((ROWS, 16, HEAD), bf16),
            V((ROWS, 16, HEAD), f32),
            V((ROWS, 16, HEAD), f32),
            V((ROWS, 16, HEAD), f32),
            V((8, 128), jnp.int32),
            V((8, 8, 128), jnp.int32),
            V((16, HEAD), bf16),
            V((8, 16, HEAD), bf16),
            V((8, 3, 16, HEAD), f32),
            V((8, 3, 16, HEAD), f32),
            V((72, HEAD), f32),
            V((16, D // 2), bf16),
            V((16, D // 2), bf16),
            V((4, 16, 512), bf16),
            V((3, 16, 512), bf16),
            V((2, 4, 16, 512), bf16),
            V((8, D // 2), f32),
            V((8, D // 4), bf16),
            V((8, D // 4), bf16),
            V((4, 8, 256), bf16),
            V((3, 8, 256), bf16),
            V((2, 4, 8, 256), bf16),
            V((16, D), f32),
            pltpu.SemaphoreType.REGULAR,
            pltpu.SemaphoreType.REGULAR,
            dma((6,)), dma((8,)),
            dma, dma((2, 4)), dma((2, 4)),
            dma((2,)), dma((2,)),
            dma, dma, dma, dma, dma, dma,
            dma, dma((2,)),
            dma, dma((2, 2)),
            dma, dma((2, 4)),
            dma((4,)), dma((4,)),
            dma((4,)), dma((4,)),
        ],
        compiler_params=pltpu.CompilerParams(
            collective_id=0, has_side_effects=True, vmem_limit_bytes=59 * 2**20
        ),
        name="layer",
    )(
        prompt_len, assign, slot, cache_len, gain.reshape(1, D), jnp.asarray(fr),
        prompt, dec_tokens, cache_k, cache_v, w_qkv, w_out, jnp.asarray(ct), jnp.asarray(st),
    )
    return pl.pallas_call(
        writer,
        out_shape=(
            jax.ShapeDtypeStruct((1, TOK, D), bf16),
            jax.ShapeDtypeStruct((STEPS, ROWS, D), bf16),
        ),
        in_specs=[vmem, vmem],
        out_specs=(any_, any_),
        scratch_shapes=[dma((2,))],
        compiler_params=pltpu.CompilerParams(vmem_limit_bytes=8 * 2**20),
        name="write",
    )(out, dout)


def writer(out_ref, dout_ref, full_ref, dec_ref, sem):
    copies = [
        pltpu.make_async_copy(out_ref, full_ref.at[0], sem.at[0]),
        pltpu.make_async_copy(dout_ref, dec_ref, sem.at[1]),
    ]
    for cp in copies:
        cp.start()
    for cp in copies:
        cp.wait()


def solution(mesh):
    return jax.shard_map(
        body,
        mesh=mesh,
        in_specs=(
            P(("pool", "batch"), "blk", None),
            P("pool", "batch"),
            P(None, ("pool", "batch"), None),
            P(("pool", "batch"), None, "blk"),
            P(("pool", "batch"), None, "blk"),
            P(("pool", "batch")),
            P("pool", "batch"),
            P("pool", "batch"),
            P(),
            P(None, "blk"),
            P("blk", None),
        ),
        out_specs=(P(("pool", "batch"), "blk", None), P(None, ("pool", "batch"), None)),
        check_vma=False,
    )
```

```python
import functools

import jax
import jax.numpy as jnp
import numpy as np
from jax import lax
from jax.experimental import pallas as pl
from jax.experimental.pallas import tpu as pltpu
from jax.sharding import PartitionSpec as P

MESH = pl.DeviceIdType.MESH
HEAD = 128
GROUP = 4
D = 4096
TOK = 128
STRETCH = 1024
CACHE = 4096
STEPS = 4
ROWS = 4
QKV = (GROUP + 2) * HEAD
PIECE = 1024
FIRST = ((0, 256), (256, 768))
PARTS = ((0, 1024), (0, 512), (512, 256), (768, 256))
EPSILON = 1e-05
THETA = 500000.0
NEG = -1e30
SCALE2 = float(HEAD ** (-0.5) * np.log2(np.e))

f32 = jnp.float32
bf16 = jnp.bfloat16


def tables():
    half = HEAD // 2
    freqs = (THETA ** (-np.arange(half, dtype=np.float64) / half)).astype(np.float32)
    angles = np.arange(STRETCH, dtype=np.float32)[:, None] * freqs
    cosine = np.cos(angles.astype(np.float64)).astype(np.float32)
    sine = np.sin(angles.astype(np.float64)).astype(np.float32)
    ct = np.concatenate([cosine, cosine], axis=1)
    st = np.concatenate([-sine, sine], axis=1)
    fr = np.broadcast_to(np.concatenate([freqs, freqs])[None, :], (8, HEAD))
    return ct, st, np.ascontiguousarray(fr)


def dot(a, b):
    return jnp.dot(a, b, preferred_element_type=f32)


def dot_t(a, b):
    return lax.dot_general(a, b, (((1,), (1,)), ((), ())), preferred_element_type=f32)


def kernel(
    plen_in, assign_in, slot_in, clen_in, gain_in, freq_in,
    prompt_ref, dec_ref, ck_ref, cv_ref, wqkv_ref, wout_ref, ct_ref, st_ref,
    out_ref, dout_ref,
    plen_ref, assign_ref, slot_ref, clen_ref, gain_ref, freq_ref,
    xs, wq, wo, ck, cv, acc, ssq, qs, kv, so, sm, at, pb, fr, nr, ct, st, bias,
    xn, dmv, x16, xd, jd, qd, kd, vd, qr, ms, ls, os_, plt, pls, qnew, qn, pks, pk, od, hs, hr, dsb, drb, dfb, lr, lhs, lhr, lsb, lrb, lfb, o32,
    ring, opened, ssem, lsem, agS, agR, farR, wS, wR, plS, plR, qnS, qnR, pkS, pkR, kvS, kvR, fS, fR, nS, nR, dS, dR, eS, eR,
):
    me = lax.axis_index("blk")
    pool = lax.axis_index("pool")
    batch = lax.axis_index("batch")
    x = me // 2
    c = lax.rem(me, 2)

    def near(dx, dc):
        return {"blk": lax.rem(x + dx + 4, 4) * 2 + lax.rem(c + dc, 2)}

    def other(j):
        return {"pool": 1 - pool, "batch": j}

    def peer(j):
        return {"blk": lax.rem(me + j, 8)}

    def remote(src, dst, ss, rs, dev):
        return pltpu.make_async_remote_copy(
            src_ref=src, dst_ref=dst, send_sem=ss, recv_sem=rs, device_id=dev, device_id_type=MESH
        )

    def arrived(ref, sem):
        remote(ref, ref, sem, sem, near(0, 1)).wait_recv()

    def gone(ref, sem):
        remote(ref, ref, sem, sem, near(0, 1)).wait_send()

    ldec = pltpu.make_async_copy(dec_ref, dmv, lsem.at[0])
    lweights = pltpu.make_async_copy(wqkv_ref, wq.at[0], lsem.at[1])
    ltokens = [
        pltpu.make_async_copy(prompt_ref.at[0, :, pl.ds(q * PIECE, PIECE)], xs.at[0, q], lsem.at[2])
        for q in range(4)
    ]
    lct = pltpu.make_async_copy(ct_ref, ct, lsem.at[3])
    lst = pltpu.make_async_copy(st_ref, st, lsem.at[4])
    lck = pltpu.make_async_copy(ck_ref, ck, lsem.at[5])
    lcv = pltpu.make_async_copy(cv_ref, cv, lsem.at[6])
    lwo = pltpu.make_async_copy(wout_ref, wo.at[0], lsem.at[7])
    local = [*ltokens, ldec, lweights, lct, lst, lck, lcv, lwo]
    small = [
        pltpu.make_async_copy(a, b, ssem.at[i])
        for i, (a, b) in enumerate((
            (plen_in, plen_ref), (assign_in, assign_ref), (slot_in, slot_ref),
            (clen_in, clen_ref), (gain_in, gain_ref), (freq_in, freq_ref),
        ))
    ]
    for cp in local[:4]:
        cp.start()
    for cp in small:
        cp.start()
    for cp in local[4:]:
        cp.start()

    barrier = pltpu.get_barrier_semaphore()
    gate = me == 0
    for j in range(1, 8):
        @pl.when(lax.rem(me + j, 8) != 0)
        def _(j=j):
            pl.semaphore_signal(barrier, inc=1, device_id=peer(j), device_id_type=MESH)

    kv[:, :, 2 * HEAD:] = jnp.ones((2, STRETCH, HEAD), bf16)

    @pl.when(me != 0)
    def _():
        pl.semaphore_wait(barrier, 7)

    @pl.when(me == 1)
    def _():
        pl.semaphore_signal(ring, inc=1, device_id=peer(7), device_id_type=MESH)

    @pl.when(gate)
    def _():
        pl.semaphore_wait(ring, 1)

    def gather(direction, k):
        q = (k + 2 * direction) % 4
        cols = pl.ds(q * PIECE, PIECE)
        src = prompt_ref.at[0, :, cols] if k == 0 else xs.at[0, q]
        return remote(src, xs.at[1 + direction, q], agS, agR.at[direction, q], near(1 - 2 * direction, 0))

    def onward(direction, k):
        q = 2 * direction + (k > 0)
        cols = pl.ds(*PARTS[k])
        return remote(
            xs.at[1 + direction, q, :, cols], xs.at[3, q, :, cols], agS, farR.at[direction, k],
            near(1 - 2 * direction, 0),
        )

    for k in range(4):
        if k == 1:
            pltpu.make_async_copy(xs.at[0], xs.at[0], lsem.at[2]).wait()
        gather(0, k).start()
        gather(1, k).start()

    remote(wqkv_ref, wq.at[1], wS.at[0], wR.at[0], near(0, 1)).start()
    remote(wout_ref, wo.at[1], wS.at[1], wR.at[1], near(0, 1)).start()

    @pl.when(gate)
    def _():
        for j in range(8):
            pl.semaphore_signal(barrier, inc=1, device_id=other(j), device_id_type=MESH)

    for cp in small:
        cp.wait()
    plt[...] = jnp.full((8, 128), plen_ref[0, 0], jnp.int32)
    col = lax.broadcasted_iota(jnp.int32, (8, STRETCH), 1)
    bias[...] = jnp.where(col < jnp.full((8, STRETCH), plen_ref[0, 0], jnp.int32), 0.0, NEG)

    ldec.wait()
    for s in range(STEPS):
        x16[pl.ds(s * ROWS, ROWS), :] = dmv[s].astype(f32)
    wide = x16[...]
    factor = lax.rsqrt(jnp.mean(wide * wide, axis=-1, keepdims=True) + EPSILON)
    xd[...] = (wide * factor * gain_ref[...]).astype(bf16)
    joined = jnp.zeros((16, QKV), f32)
    lweights.wait()
    for q in range(4):
        joined = joined + dot(xd[:, q * PIECE:(q + 1) * PIECE], wq[0, pl.ds(q * PIECE, PIECE), :])
    jd[...] = joined

    def scaled(slot, q, a, at=0, size=PIECE):
        wide = xs[slot, q, :, pl.ds(at, size)].astype(f32)
        square = wide * wide
        part = square[:, :HEAD]
        for i in range(1, size // HEAD):
            part = part + square[:, i * HEAD:(i + 1) * HEAD]
        ssq[a] += part
        return (wide * gain_ref[:, pl.ds(pl.multiple_of(q * PIECE + at, size), size)]).astype(bf16)

    def project(slot, q, a, at=0, size=PIECE):
        tokens = scaled(slot, q, a, at, size)
        rows = pl.ds(pl.multiple_of(q * PIECE + at, size), size)
        for h in range(2):
            acc[a, h] += dot(tokens, wq[h, rows, :])

    def clear(a):
        acc[a] = jnp.zeros((2, TOK, QKV), f32)
        ssq[a] = jnp.zeros((TOK, HEAD), f32)

    clear(0)

    def own_first(q, _):
        tokens = scaled(0, q, 0)
        xn[q] = tokens
        acc[0, 0] += dot(tokens, wq[0, pl.ds(pl.multiple_of(q * PIECE, PIECE), PIECE), :])
        return 0

    lax.fori_loop(0, 4, own_first, 0)

    def turn(u, cosine, sine):
        return u * cosine + pltpu.roll(u, HEAD // 2, 1) * sine

    def decode_queries():
        wanted = jnp.full((8, 128), assign_ref[0, 0], jnp.int32)
        newlen = jnp.zeros((8, 128), jnp.int32)
        arrived(pls, plR)
        for j in range(8):
            newlen = newlen + jnp.where(wanted == j, pls[j], 0)
        row = lax.broadcasted_iota(jnp.int32, (16, 128), 0)
        row_r = lax.rem(row, ROWS)
        place = jnp.zeros((16, 128), jnp.int32)
        for r in range(ROWS):
            place = jnp.where(row_r == r, jnp.full((16, 128), clen_ref[r], jnp.int32), place)
        fresh = row_r == jnp.full((16, 128), slot_ref[0, 0], jnp.int32)
        place = jnp.where(fresh, jnp.broadcast_to(newlen[0:1, :], (16, 128)), place) + row // ROWS
        angle = place.astype(f32) * freq_ref[0:1, :]
        lane = lax.broadcasted_iota(jnp.int32, (16, 128), 1)
        dcos = jnp.cos(angle)
        dsin = jnp.sin(angle)
        dsin = jnp.where(lane < HEAD // 2, -dsin, dsin)

        for h in range(GROUP):
            qd[pl.ds(h * 16, 16), :] = turn(jd[:, h * HEAD:(h + 1) * HEAD], dcos, dsin)
        kd[...] = turn(jd[:, GROUP * HEAD:(GROUP + 1) * HEAD], dcos, dsin).astype(bf16)
        vd[...] = jd[:, (GROUP + 1) * HEAD:].astype(bf16)
        slots = jnp.full((16, 128), slot_ref[0, 0], jnp.int32)
        picked = jnp.zeros((16, 128), f32)
        for r in range(ROWS):
            part = qd[pl.ds(r, 16, stride=ROWS), :]
            qr[r] = part.astype(bf16)
            picked = picked + jnp.where(slots == r, part, 0.0)
        qnew[...] = picked.astype(bf16)

    def origin(slot):
        if isinstance(slot, int):
            return lax.rem(x + (0, 3, 1, 2)[slot], 4)
        return lax.rem(x + jnp.where(slot == 1, 3, jnp.where(slot == 2, 1, jnp.where(slot == 3, 2, 0))), 4)

    def exchange(slot, h):
        rows = pl.ds(pl.multiple_of((origin(slot) * 2 + c) * TOK, TOK), TOK)
        cols = pl.ds(0, 2 * HEAD)
        return remote(kv.at[h, rows, cols], kv.at[1 - h, rows, cols], kvS, kvR.at[slot // 3], near(0, 1))

    def factors(slot, a):
        rows = pl.ds(pl.multiple_of((origin(slot) * 2 + c) * TOK, TOK), TOK)
        factor = lax.rsqrt(jnp.sum(ssq[a], axis=-1, keepdims=True) * (1.0 / D) + EPSILON)
        return rows, factor, ct[rows, :] * factor, st[rows, :] * factor

    def finish_query(slot, a, h, cosine, sine):
        for g in range(GROUP):
            qs[slot, h * GROUP + g] = turn(acc[a, h, :, g * HEAD:(g + 1) * HEAD], cosine, sine).astype(bf16)

    def finish_keys(slot, a):
        rows, factor, cosine, sine = factors(slot, a)
        for h in range(2):
            kv[h, rows, :HEAD] = turn(acc[a, h, :, GROUP * HEAD:(GROUP + 1) * HEAD], cosine, sine).astype(bf16)
            kv[h, rows, HEAD:2 * HEAD] = (acc[a, h, :, (GROUP + 1) * HEAD:] * factor).astype(bf16)
        exchange(slot, 0).start()
        qs[slot, 0] = turn(acc[a, 0, :, :HEAD], cosine, sine).astype(bf16)
        exchange(slot, 1).start()

    def finish(slot, a):
        finish_keys(slot, a)
        rows, factor, cosine, sine = factors(slot, a)
        for h in range(2):
            finish_query(slot, a, h, cosine, sine)

    def old_row(r):
        q16 = qr[r]
        edge = jnp.full((16, CACHE), clen_ref[r], jnp.int32)
        edge = jnp.where(jnp.full((16, CACHE), slot_ref[0, 0], jnp.int32) == r, 0, edge)
        span = lax.broadcasted_iota(jnp.int32, (16, CACHE), 1)
        old = jnp.where(span < edge, dot_t(q16, ck[r]) * SCALE2, NEG)
        own = dot_t(q16, kd[...]) * SCALE2
        i16 = lax.broadcasted_iota(jnp.int32, (16, 16), 0)
        j16 = lax.broadcasted_iota(jnp.int32, (16, 16), 1)
        keep = (lax.rem(j16, ROWS) == r) & (j16 // ROWS <= lax.rem(i16, STEPS))
        own = jnp.where(keep, own, NEG)
        top = jnp.maximum(jnp.max(old, axis=-1, keepdims=True), jnp.max(own, axis=-1, keepdims=True))
        pold = jnp.exp2(old - top)
        pown = jnp.exp2(own - top)
        total = jnp.sum(pold, axis=-1, keepdims=True) + jnp.sum(pown, axis=-1, keepdims=True)
        mixed = dot(pold.astype(bf16), cv[r]) + dot(pown.astype(bf16), vd[...])
        ms[r] = jnp.broadcast_to(top, (16, 128))
        ls[r] = jnp.broadcast_to(total, (16, 128))
        os_[r] = mixed

    def query(j):
        return remote(qnew, qn.at[batch], qnS, qnR, other(j))

    @pl.when(gate)
    def _():
        pl.semaphore_wait(barrier, 8)
        for j in range(1, 8):
            pl.semaphore_signal(opened, inc=1, device_id=peer(j), device_id_type=MESH)

    @pl.when(me != 0)
    def _():
        pl.semaphore_wait(opened, 1)

    def length(j):
        return remote(plt, pls.at[batch], plS, plR, other(j))

    for j in range(8):
        length(j).start()

    arrived(wq.at[1], wR.at[0])
    lct.wait()
    lst.wait()

    def own_second(q, _):
        acc[0, 1] += dot(xn[q], wq[1, pl.ds(pl.multiple_of(q * PIECE, PIECE), PIECE), :])
        return 0

    lax.fori_loop(0, 4, own_second, 0)
    finish(0, 0)

    def half_cols(core):
        return pl.ds(pl.multiple_of(core * (D // 2), D // 2), D // 2)

    def chip_cols(core, chip):
        return pl.ds(pl.multiple_of(core * (D // 2) + chip * 512, 512), 512)

    def early_rows():
        for r in range(ROWS):
            od[pl.ds(r, 16, stride=ROWS), :] = os_[r] / ls[r]
        lwo.wait()
        part = jnp.zeros((16, D), f32)
        for h in range(GROUP):
            part = part + dot(od[pl.ds(h * 16, 16), :].astype(bf16), wo[0, pl.ds(h * HEAD, HEAD), :])
        o32[...] = part
        hs[...] = o32[:, half_cols(1 - c)].astype(bf16)

    def early_halves():
        arrived(hr, dR.at[0])
        o32[:, half_cols(c)] = o32[:, half_cols(c)] + hr[...].astype(f32)
        for k in range(4):
            dsb[k] = o32[:, chip_cols(c, lax.rem(x + k, 4))].astype(bf16)

    clear(0)
    clear(1)
    lck.wait()
    lcv.wait()

    def near_step(t, _):
        q1 = t
        q2 = lax.rem(t + 2, 4)
        arrived(xs.at[1, q1], agR.at[0, q1])
        arrived(xs.at[2, q2], agR.at[1, q2])

        @pl.when(t == 0)
        def _():
            onward(0, 0).start()
            onward(1, 0).start()

        @pl.when(t == 1)
        def _():
            for k in (1, 2, 3):
                onward(0, k).start()
                onward(1, k).start()

        project(1, q1, 0)
        project(2, q2, 1)

        @pl.when(t == 1)
        def _():
            decode_queries()
            for j in range(2):
                old_row(j)
            for j in range(8):
                query(j).start()
            for j in range(2, 4):
                old_row(j)

        @pl.when(t == 2)
        def _():
            early_rows()

        @pl.when(t == 3)
        def _():
            remote(hs, hr, dS.at[0], dR.at[0], near(0, 1)).start()

        return 0

    lax.fori_loop(0, 4, near_step, 0)
    finish(1, 0)
    finish(2, 1)

    def attend_own(d):
        krows = pl.ds(pl.multiple_of(origin(d) * 256, 256), 256)
        qi = lax.rem(lax.broadcasted_iota(jnp.int32, (2 * TOK, 256), 0), TOK) + c * TOK
        ki = lax.broadcasted_iota(jnp.int32, (2 * TOK, 256), 1)
        mask = jnp.where(ki <= qi, jnp.broadcast_to(bias[0:1, krows], (2 * TOK, 256)), NEG)
        for hp in range(4):
            q2 = qs[d, 2 * hp:2 * hp + 2].reshape(2 * TOK, HEAD)
            h = hp // 2
            s = dot_t(q2, kv[h, krows, :HEAD]) * SCALE2 + mask
            top = jnp.max(s, axis=-1, keepdims=True)
            p = jnp.exp2(s - top)
            sm[d, hp] = jnp.broadcast_to(top, (2 * TOK, HEAD))
            so[d, hp] = dot(p.astype(bf16), kv[h, krows, HEAD:])

    def attend_more(d, k):
        krows = pl.ds(pl.multiple_of(origin(k) * 256, 256), 256)

        @pl.when(origin(k) < origin(d))
        def _():
            more_keys(d, krows)

    def more_keys(d, krows):
        for hp in range(4):
            q2 = qs[d, 2 * hp:2 * hp + 2].reshape(2 * TOK, HEAD)
            h = hp // 2
            s = dot_t(q2, kv[h, krows, :HEAD]) * SCALE2 + bias[0:1, krows]
            before = sm[d, hp]
            top = jnp.maximum(before, jnp.broadcast_to(jnp.max(s, axis=-1, keepdims=True), (2 * TOK, HEAD)))
            p = jnp.exp2(s - jnp.concatenate([top, top], axis=1))
            fade = jnp.exp2(before - top)
            sm[d, hp] = top
            so[d, hp] = so[d, hp] * jnp.concatenate([fade, fade], axis=1) + dot(p.astype(bf16), kv[h, krows, HEAD:])

    def attend_near(d):
        attend_own(d)

        def others(i, _):
            attend_more(d, lax.rem(d + i, 3))
            return 0

        lax.fori_loop(1, 3, others, 0)

    def settle(d):
        for hp in range(4):
            o = (so[d, hp, :, :HEAD] / so[d, hp, :, HEAD:]).astype(bf16)
            at[d, :, hp * 256:hp * 256 + HEAD] = o[:TOK]
            at[d, :, hp * 256 + HEAD:(hp + 1) * 256] = o[TOK:]

    arrived(kv.at[0, pl.ds(0, 6 * TOK), pl.ds(0, 2 * HEAD)], kvR.at[0])

    def before_far(i, _):
        attend_near(lax.rem(i + 1, 3))
        return 0

    lax.fori_loop(0, 3, before_far, 0)

    def out_piece(d, q):
        cols = pl.ds(pl.multiple_of(q * PIECE, PIECE), PIECE)
        part = dot(at[d, :, :512], wo[0, :, cols]) + dot(at[d, :, 512:], wo[1, :, cols])
        pb[d, q] = part.astype(bf16)

    def half_piece(d, q, half):
        at0, size = FIRST[half]
        cols = pl.ds(pl.multiple_of(q * PIECE + at0, 256), size)
        part = dot(at[d, :, :512], wo[0, :, cols]) + dot(at[d, :, 512:], wo[1, :, cols])
        pb[d, q, :, at0:at0 + size] = part.astype(bf16)

    def half_send(direction, q, half):
        cols = pl.ds(*FIRST[half])
        return remote(
            pb.at[2 - direction, q, :, cols], nr.at[direction, q, :, cols], nS, nR.at[direction, q],
            near(1 - 2 * direction, 0),
        )

    def far_send(q):
        if q < 2:
            return remote(pb.at[3, q], fr.at[0, q], fS, fR.at[0, q], near(1, 0))
        return remote(pb.at[3, q], fr.at[1, q - 2], fS, fR.at[1, q - 2], near(-1, 0))

    def near_send(direction, q):
        return remote(
            pb.at[2 - direction, q], nr.at[direction, q], nS, nR.at[direction, q],
            near(1 - 2 * direction, 0),
        )

    clear(0)

    for direction in range(2):
        arrived(xs.at[3, 2 * direction], farR.at[direction, 0])
        project(3, 2 * direction, 0)
    early_halves()
    arrived(wo.at[1], wR.at[1])
    right_needs = origin(3) < origin(2)
    left_needs = origin(3) < origin(1)

    @pl.when(jnp.logical_not(right_needs))
    def _():
        settle(2)
        out_piece(2, 2)

    @pl.when(jnp.logical_not(left_needs))
    def _():
        settle(1)
        out_piece(1, 0)

    for k in range(1, 4):
        remote(dsb.at[k], drb.at[k - 1], dS.at[1], dR.at[1], near(k, 0)).start()

    for k in range(1, 4):
        for direction in range(2):
            q = 2 * direction + 1
            arrived(xs.at[3, q, :, pl.ds(*PARTS[k])], farR.at[direction, k])
            project(3, q, 0, *PARTS[k])

    @pl.when(jnp.logical_not(right_needs))
    def _():
        near_send(0, 2).start()

    @pl.when(jnp.logical_not(left_needs))
    def _():
        near_send(1, 0).start()

    finish_keys(3, 0)
    arrived(drb, dR.at[1])
    total = o32[:, chip_cols(c, x)]
    for k in range(3):
        total = total + drb[k].astype(f32)
    dfb[0, 0] = (x16[:, chip_cols(c, x)] + total).astype(bf16)
    for k in range(1, 4):
        remote(dfb.at[0, 0], dfb.at[0, k], dS.at[2], dR.at[2], near(k, 0)).start()
    arrived(kv.at[0, pl.ds(0, 2 * TOK), pl.ds(0, 2 * HEAD)], kvR.at[1])

    def answer():
        arrived(qn, qnR)
        q = qn[...].reshape(8 * 16, HEAD)
        s = dot_t(q, kv[0, :, :HEAD]) * SCALE2 + bias[0:1, :]
        top = jnp.max(s, axis=-1, keepdims=True)
        p = jnp.exp2(s - top)
        o = dot(p.astype(bf16), kv[0, :, HEAD:])
        pks[:, 0] = o[:, :HEAD].reshape(8, 16, HEAD)
        pks[:, 1] = jnp.broadcast_to(top, (128, HEAD)).reshape(8, 16, HEAD)
        pks[:, 2] = o[:, HEAD:].reshape(8, 16, HEAD)

    def reply(j):
        return remote(pks.at[j], pk.at[batch], pkS, pkR, other(j))

    def pieces(d, first, second):
        def piece(k, _):
            out_piece(d, jnp.where(k == 0, first, second))
            return 0

        lax.fori_loop(0, 2, piece, 0)

    far_rows = pl.ds(pl.multiple_of(origin(3) * 256, 256), 256)

    def near_block(i, _):
        d = jnp.where(c == 0, 2 - i, 1 + i)

        @pl.when(jnp.where(d == 2, origin(2), origin(1)) > origin(3))
        def _():
            more_keys(d, far_rows)
            settle(d)
            for half in range(2):
                half_piece(d, jnp.where(d == 2, 2, 0), half)

                @pl.when(d == 2)
                def _(half=half):
                    half_send(0, 2, half).start()

                @pl.when(d == 1)
                def _(half=half):
                    half_send(1, 0, half).start()

        return 0

    lax.fori_loop(0, 2, near_block, 0)
    out_piece(2, 3)
    near_send(0, 3).start()
    out_piece(1, 1)
    near_send(1, 1).start()
    rows3, factor3, cosine3, sine3 = factors(3, 0)
    for h in range(2):
        finish_query(3, 0, h, cosine3, sine3)
    answer()

    attend_own(3)
    for j in range(8):
        reply(j).start()

    def far_keys(k, _):
        attend_more(3, k)
        return 0

    lax.fori_loop(0, 3, far_keys, 0)
    settle(3)
    pieces(3, 0, 2)
    far_send(0).start()
    far_send(2).start()
    pieces(3, 1, 3)
    pieces(2, 0, 1)
    pieces(1, 2, 3)
    arrived(pk, pkR)
    want = jnp.full((16, 128), assign_ref[0, 0], jnp.int32)
    no = jnp.zeros((16, 128), f32)
    nm = jnp.zeros((16, 128), f32)
    nl = jnp.zeros((16, 128), f32)
    for j in range(8):
        hit = want == j
        no = no + jnp.where(hit, pk[j, 0], 0.0)
        nm = nm + jnp.where(hit, pk[j, 1], 0.0)
        nl = nl + jnp.where(hit, pk[j, 2], 0.0)
    slots = jnp.full((16, 128), slot_ref[0, 0], jnp.int32)
    mo = jnp.zeros((16, 128), f32)
    mm = jnp.zeros((16, 128), f32)
    ml = jnp.zeros((16, 128), f32)
    for r in range(ROWS):
        mine = slots == r
        mo = mo + jnp.where(mine, os_[r], 0.0)
        mm = mm + jnp.where(mine, ms[r], 0.0)
        ml = ml + jnp.where(mine, ls[r], 0.0)
    top = jnp.maximum(mm, nm)
    a = jnp.exp2(mm - top)
    b = jnp.exp2(nm - top)
    o = (mo * a + no * b) / (ml * a + nl * b)
    head = lax.broadcasted_iota(jnp.int32, (16, 128), 0) // STEPS
    part = jnp.zeros((16, D), f32)
    for h in range(GROUP):
        part = part + dot(jnp.where(head == h, o, 0.0).astype(bf16), wo[0, pl.ds(h * HEAD, HEAD), :])
    part = part[:8] + part[8:]
    part = part + pltpu.roll(part, 4, 0)
    first = lax.broadcasted_iota(jnp.int32, (8, 256), 0) < STEPS
    for k in range(8):
        lr[:, k * 256:(k + 1) * 256] = jnp.where(
            first, part[:, k * 512:k * 512 + 256], part[:, k * 512 + 256:(k + 1) * 512]
        )

    def packed_half(core):
        return pl.ds(pl.multiple_of(core * 1024, 1024), 1024)

    def packed_chip(core, chip):
        return pl.ds(pl.multiple_of(core * 1024 + chip * 256, 256), 256)

    lhs[...] = lr[:, packed_half(1 - c)].astype(bf16)
    attend_more(0, 3)
    settle(0)
    remote(lhs, lhr, eS.at[0], eR.at[0], near(0, 1)).start()
    pieces(0, 0, 2)
    arrived(lhr, eR.at[0])
    lr[:, packed_half(c)] = lr[:, packed_half(c)] + lhr[...].astype(f32)
    for k in range(4):
        lsb[k] = lr[:, packed_chip(c, lax.rem(x + k, 4))].astype(bf16)
    for k in range(1, 4):
        remote(lsb.at[k], lrb.at[k - 1], eS.at[1], eR.at[1], near(k, 0)).start()
    far_send(1).start()
    far_send(3).start()

    pieces(0, 1, 3)
    arrived(dfb.at[0, pl.ds(1, 3)], dR.at[2])
    remote(dfb.at[0], dfb.at[1], dS.at[3], dR.at[3], near(0, 1)).start()

    def relay(q):
        arrived(fr.at[0, q], fR.at[0, q])
        pb[2, q] = (pb[2, q].astype(f32) + fr[0, q].astype(f32)).astype(bf16)
        near_send(0, q).start()
        arrived(fr.at[1, q], fR.at[1, q])
        pb[1, q + 2] = (pb[1, q + 2].astype(f32) + fr[1, q].astype(f32)).astype(bf16)
        near_send(1, q + 2).start()

    relay(0)
    arrived(lrb, eR.at[1])
    total = lr[:, packed_chip(c, x)]
    for k in range(3):
        total = total + lrb[k].astype(f32)
    pick_i = lax.broadcasted_iota(jnp.int32, (16, 16), 0)
    pick_j = lax.broadcasted_iota(jnp.int32, (16, 16), 1)
    pick = pick_j == lax.rem(pick_i, STEPS) * ROWS + jnp.full((16, 16), slot_ref[0, 0], jnp.int32)
    tokens = dot(jnp.where(pick, 1.0, 0.0).astype(bf16), x16[:, chip_cols(c, x)].astype(bf16))[:8]
    lfb[0, 0] = (jnp.where(first, tokens[:, :256], tokens[:, 256:]) + total).astype(bf16)
    for k in range(1, 4):
        remote(lfb.at[0, 0], lfb.at[0, k], eS.at[2], eR.at[2], near(k, 0)).start()
    relay(1)
    arrived(lfb.at[0, pl.ds(1, 3)], eR.at[2])
    remote(lfb.at[0], lfb.at[1], eS.at[3], eR.at[3], near(0, 1)).start()
    arrived(dfb.at[1], dR.at[3])
    arrived(lfb.at[1], eR.at[3])
    for core in range(2):
        for k in range(4):
            o32[:, chip_cols(lax.rem(c + core, 2), lax.rem(x - k + 4, 4))] = dfb[core, k].astype(f32)
            lr[:, packed_chip(lax.rem(c + core, 2), lax.rem(x - k + 4, 4))] = lfb[core, k].astype(f32)
    here = lax.broadcasted_iota(jnp.int32, (ROWS, 256), 0) == jnp.full((ROWS, 256), slot_ref[0, 0], jnp.int32)
    for s in range(STEPS):
        for k in range(8):
            for half in range(2):
                cols = slice(k * 512 + half * 256, k * 512 + (half + 1) * 256)
                late = lr[4 * half + s:4 * half + s + 1, k * 256:(k + 1) * 256]
                dout_ref[s, :, cols] = jnp.where(
                    here, jnp.broadcast_to(late, (ROWS, 256)), o32[s * ROWS:(s + 1) * ROWS, cols]
                ).astype(bf16)

    for i, q in enumerate((0, 2, 1, 3)):
        arrived(nr.at[0, q], nR.at[0, q])
        arrived(nr.at[1, q], nR.at[1, q])
        cols = slice(q * PIECE, (q + 1) * PIECE)
        total = pb[0, q].astype(f32) + nr[0, q].astype(f32) + nr[1, q].astype(f32)
        out_ref[:, cols] = (xs[0, q].astype(f32) + total).astype(bf16)

    gone(xs.at[pl.ds(0, 3)], agS)
    gone(wq.at[0], wS.at[0])
    gone(wo.at[0], wS.at[1])
    gone(pls, plS)
    gone(qn, qnS)
    gone(pk, pkS)
    gone(kv.at[0, :, pl.ds(0, 2 * HEAD)], kvS)
    gone(pb.at[3], fS)
    gone(pb.at[pl.ds(1, 2)], nS)
    gone(hr, dS.at[0])
    gone(drb, dS.at[1])
    gone(drb, dS.at[2])
    gone(dfb.at[0], dS.at[3])
    gone(lhr, eS.at[0])
    gone(lrb, eS.at[1])
    gone(lrb, eS.at[2])
    gone(lfb.at[0], eS.at[3])


def body(
    prompt, prompt_len, dec_tokens, cache_k, cache_v, cache_len, assign, slot, gain, w_qkv, w_out
):
    ct, st, fr = tables()
    any_ = pl.BlockSpec(memory_space=pl.ANY)
    vmem = pl.BlockSpec(memory_space=pltpu.VMEM)
    V = pltpu.VMEM
    dma = pltpu.SemaphoreType.DMA
    OUT = pltpu.VMEM
    out, dout = pl.pallas_call(
        kernel,
        out_shape=(
            OUT((TOK, D), bf16),
            OUT((STEPS, ROWS, D), bf16),
        ),
        in_specs=[any_] * 14,
        out_specs=(vmem, vmem),
        scratch_shapes=[
            pltpu.SMEM((1, 1), jnp.int32),
            pltpu.SMEM((1, 1), jnp.int32),
            pltpu.SMEM((1, 1), jnp.int32),
            pltpu.SMEM((ROWS,), jnp.int32),
            V((1, D), f32),
            V((8, HEAD), f32),
            V((4, 4, TOK, PIECE), bf16),
            V((2, D, QKV), bf16),
            V((2, 512, D), bf16),
            V((ROWS, CACHE, HEAD), bf16),
            V((ROWS, CACHE, HEAD), bf16),
            V((2, 2, TOK, QKV), f32),
            V((2, TOK, HEAD), f32),
            V((4, 8, TOK, HEAD), bf16),
            V((2, STRETCH, 3 * HEAD), bf16),
            V((4, 4, 2 * TOK, 2 * HEAD), f32),
            V((4, 4, 2 * TOK, HEAD), f32),
            V((4, TOK, 1024), bf16),
            V((4, 4, TOK, PIECE), bf16),
            V((2, 2, TOK, PIECE), bf16),
            V((2, 4, TOK, PIECE), bf16),
            V((STRETCH, HEAD), f32),
            V((STRETCH, HEAD), f32),
            V((8, STRETCH), f32),
            V((4, TOK, PIECE), bf16),
            V((STEPS, ROWS, D), bf16),
            V((16, D), f32),
            V((16, D), bf16),
            V((16, QKV), f32),
            V((72, HEAD), f32),
            V((16, HEAD), bf16),
            V((16, HEAD), bf16),
            V((ROWS, 16, HEAD), bf16),
            V((ROWS, 16, HEAD), f32),
            V((ROWS, 16, HEAD), f32),
            V((ROWS, 16, HEAD), f32),
            V((8, 128), jnp.int32),
            V((8, 8, 128), jnp.int32),
            V((16, HEAD), bf16),
            V((8, 16, HEAD), bf16),
            V((8, 3, 16, HEAD), f32),
            V((8, 3, 16, HEAD), f32),
            V((72, HEAD), f32),
            V((16, D // 2), bf16),
            V((16, D // 2), bf16),
            V((4, 16, 512), bf16),
            V((3, 16, 512), bf16),
            V((2, 4, 16, 512), bf16),
            V((8, D // 2), f32),
            V((8, D // 4), bf16),
            V((8, D // 4), bf16),
            V((4, 8, 256), bf16),
            V((3, 8, 256), bf16),
            V((2, 4, 8, 256), bf16),
            V((16, D), f32),
            pltpu.SemaphoreType.REGULAR,
            pltpu.SemaphoreType.REGULAR,
            dma((6,)), dma((8,)),
            dma, dma((2, 4)), dma((2, 4)),
            dma((2,)), dma((2,)),
            dma, dma, dma, dma, dma, dma,
            dma, dma((2,)),
            dma, dma((2, 2)),
            dma, dma((2, 4)),
            dma((4,)), dma((4,)),
            dma((4,)), dma((4,)),
        ],
        compiler_params=pltpu.CompilerParams(
            collective_id=0, has_side_effects=True, vmem_limit_bytes=59 * 2**20
        ),
        name="layer",
    )(
        prompt_len, assign, slot, cache_len, gain.reshape(1, D), jnp.asarray(fr),
        prompt, dec_tokens, cache_k, cache_v, w_qkv, w_out, jnp.asarray(ct), jnp.asarray(st),
    )
    return pl.pallas_call(
        writer,
        out_shape=(
            jax.ShapeDtypeStruct((1, TOK, D), bf16),
            jax.ShapeDtypeStruct((STEPS, ROWS, D), bf16),
        ),
        in_specs=[vmem, vmem],
        out_specs=(any_, any_),
        scratch_shapes=[dma((2,))],
        compiler_params=pltpu.CompilerParams(vmem_limit_bytes=8 * 2**20),
        name="write",
    )(out, dout)


def writer(out_ref, dout_ref, full_ref, dec_ref, sem):
    copies = [
        pltpu.make_async_copy(out_ref, full_ref.at[0], sem.at[0]),
        pltpu.make_async_copy(dout_ref, dec_ref, sem.at[1]),
    ]
    for cp in copies:
        cp.start()
    for cp in copies:
        cp.wait()


def solution(mesh):
    return jax.shard_map(
        body,
        mesh=mesh,
        in_specs=(
            P(("pool", "batch"), "blk", None),
            P("pool", "batch"),
            P(None, ("pool", "batch"), None),
            P(("pool", "batch"), None, "blk"),
            P(("pool", "batch"), None, "blk"),
            P(("pool", "batch")),
            P("pool", "batch"),
            P("pool", "batch"),
            P(),
            P(None, "blk"),
            P("blk", None),
        ),
        out_specs=(P(("pool", "batch"), "blk", None), P(None, ("pool", "batch"), None)),
        check_vma=False,
    )
```
